32 devices in a mesh: dp: 8 (over y, x, core), seq: 4 (over z).
Axes of the slice: x: 2, y: 2, z: 4, core: 2. Of those that a mesh axis runs over, the one named last changes fastest.
Arguments:
- tokens: bfloat16 [8, 1024, 1536], P('dp', 'seq'), may hold values from -6 to 6
- cotangent: bfloat16 [8, 1024, 1536], P('dp', 'seq'), may hold values from -6 to 6
- w_query: bfloat16 [1, 1536, 1536], P(None, 'dp'), may hold values from -1 to 1
- w_key: bfloat16 [1, 1536, 768], P(None, 'dp'), may hold values from -1 to 1
- w_value: bfloat16 [1, 1536, 768], P(None, 'dp'), may hold values from -0.15625 to 0.15625
- w_out: bfloat16 [1, 1536, 1536], P(None, 'dp'), may hold values from -1.25 to 1.25
- w_gate: bfloat16 [1, 1536, 4096], P(None, 'dp'), may hold values from -0.15625 to 0.15625
- w_up: bfloat16 [1, 1536, 4096], P(None, 'dp'), may hold values from -0.15625 to 0.15625
- w_down: bfloat16 [1, 4096, 1536], P(None, 'dp'), may hold values from -0.09375 to 0.09375
- gain_attn: bfloat16 [1, 1536], P(None, 'dp'), may hold values from 0.5 to 1.5
- gain_mlp: bfloat16 [1, 1536], P(None, 'dp'), may hold values from 0.5 to 1.5
Outputs:
- activations: float32 [8, 1024, 1536], P('dp', 'seq')
- input_grad: float32 [8, 1024, 1536], P('dp', 'seq')
- grad_w_query: float32 [1, 1536, 1536], P(None, 'dp')
- grad_w_key: float32 [1, 1536, 768], P(None, 'dp')
- grad_w_value: float32 [1, 1536, 768], P(None, 'dp')
- grad_w_out: float32 [1, 1536, 1536], P(None, 'dp')
- grad_w_gate: float32 [1, 1536, 4096], P(None, 'dp')
- grad_w_up: float32 [1, 1536, 4096], P(None, 'dp')
- grad_w_down: float32 [1, 4096, 1536], P(None, 'dp')
- grad_gain_attn: float32 [1, 1536], P(None, 'dp')
- grad_gain_mlp: float32 [1, 1536], P(None, 'dp')
The draws below stay inside these ranges and needn't reach their ends.
All inputs are finite; a program needn't handle non-finite values.
Results may differ from the reference program's by a relative error of at most 0.02.
Values may be sent and summed in bfloat16 or wider, within the bound.
A program may use at most 256 MiB of HBM per device.

```python
import jax
import jax.numpy as jnp
from jax import lax

D = 1536
HEADS = 16
KV_HEADS = 8
HEAD_DIM = 96
FF = 4096
LAYERS = 1
LENGTH = 1024
SEQUENCES = 8
KVD = 768


def paired_normals(key):
    base = jax.random.normal(jax.random.fold_in(key, 101), (LAYERS, D, HEADS * HEAD_DIM), jnp.float32)
    noise = jax.random.normal(jax.random.fold_in(key, 202), (LAYERS, D, KV_HEADS * HEAD_DIM), jnp.float32)
    return (jnp.clip(base, -4.0, 4.0), jnp.clip(noise, -4.0, 4.0))


def draw_w_query(key, part):
    base, noise = paired_normals(key)
    values = base * D ** (-0.5)
    return jnp.clip(values, -1.0, 1.0).astype(jnp.bfloat16)


def draw_w_key(key, part):
    base, noise = paired_normals(key)
    values = noise * D ** (-0.5)
    return jnp.clip(values, -1.0, 1.0).astype(jnp.bfloat16)


def steps_of(key, dims, cuts, smallest, top_value):
    level, own = 1.0, jax.random.fold_in(key, 6)
    for axis_at, shards_of in cuts:
        draws = jnp.exp(jax.random.uniform(jax.random.fold_in(own, axis_at), (shards_of,), jnp.float32, smallest / len(cuts), top_value / len(cuts)))
        level = level * jnp.repeat(draws, dims[axis_at] // shards_of).reshape([-1 if axis == axis_at else 1 for axis in range(len(dims))])
    return level


def scatter_about(key, extent, deviation, limit, pieces=(), kind=jnp.bfloat16):
    level = steps_of(key, extent, pieces, -0.22, 0.18) if pieces else 1.0
    array = jax.random.normal(key, extent, jnp.float32) * deviation * level
    return jnp.minimum(jnp.maximum(array, -limit), limit).astype(kind)


def setup_inputs(seed: int = 0) -> dict:
    seeds = jax.random.split(jax.random.key(seed), 12)
    return {
        "tokens": scatter_about(seeds[0], (SEQUENCES, LENGTH, D), 1.0, 6.0, ((0, 8), (1, 4))),
        "cotangent": scatter_about(seeds[1], (SEQUENCES, LENGTH, D), 1.0, 6.0, ((0, 8), (1, 4))),
        "w_query": draw_w_query(jax.random.fold_in(seeds[11], 71), 0),
        "w_key": draw_w_key(jax.random.fold_in(seeds[11], 71), 0),
        "w_value": scatter_about(seeds[4], (LAYERS, D, KVD), D ** -0.5, 0.15625, ((1, 8),)),
        "w_out": scatter_about(seeds[5], (LAYERS, D, D), (D // 64) ** -0.5, 1.25, ((1, 8),)),
        "w_gate": scatter_about(seeds[6], (LAYERS, D, FF), D ** -0.5, 0.15625, ((1, 8),)),
        "w_up": scatter_about(seeds[7], (LAYERS, D, FF), D ** -0.5, 0.15625, ((1, 8),)),
        "w_down": scatter_about(seeds[8], (LAYERS, FF, D), FF ** -0.5, 0.09375, ((1, 8),)),
        "gain_attn": jnp.clip(1.0 + 0.1 * jax.random.normal(seeds[9], (LAYERS, D), jnp.float32), 0.5, 1.5).astype(jnp.bfloat16),
        "gain_mlp": jnp.clip(1.0 + 0.1 * jax.random.normal(seeds[10], (LAYERS, D), jnp.float32), 0.5, 1.5).astype(jnp.bfloat16),
    }


@jax.custom_vjp
def low(v):
    return lax.optimization_barrier(v.astype(jnp.bfloat16)).astype(jnp.float32)

@jax.custom_vjp
def low_back(v):
    return v

def low_keep(v):
    return (low(v), None)

def low_pass(kept, grad):
    return (grad,)

def back_keep(v):
    return (v, None)

def back_low(kept, grad):
    return (low(grad),)
low.defvjp(low_keep, low_pass)
low_back.defvjp(back_keep, back_low)
EPS = 1e-05
ROPE_BASE = 100000.0

def rope_tables(positions, half_dim):
    frequency = ROPE_BASE ** (-jnp.arange(half_dim).astype(jnp.float32) / half_dim)
    angles = positions[:, None] * frequency[None, :]
    return (jnp.cos(angles), jnp.sin(angles))

def rotate(field, cosine_table, sine_table):
    half_dim = field.shape[-1] // 2
    first_half = field[..., :half_dim]
    second = field[..., half_dim:]
    cosine_b = cosine_table[:, None, :]
    sine_b = sine_table[:, None, :]
    return jnp.concatenate([first_half * cosine_b - second * sine_b, second * cosine_b + first_half * sine_b], axis=-1)

def norm_apply(values, gain):
    return values * lax.rsqrt(lax.optimization_barrier(jnp.mean(values * values, axis=-1, keepdims=True)) + EPS) * gain

def product(left, right):
    return jnp.dot(left, right, preferred_element_type=jnp.float32, precision=lax.Precision.HIGHEST)

def attention(query, keys, values):
    full_span = query.shape[0]
    block_rows = min(512, full_span)
    group = HEADS // KV_HEADS
    grouped = query.reshape(full_span, KV_HEADS, group, HEAD_DIM)
    key_pos = jnp.arange(full_span, dtype=jnp.int32)

    def one_block(block_start):
        query_rows = lax.dynamic_slice_in_dim(grouped, block_start, block_rows, 0)
        scores = jnp.einsum('qgrd,kgd->grqk', query_rows, keys, precision=lax.Precision.HIGHEST) * HEAD_DIM ** (-0.5)
        query_pos = block_start + jnp.arange(block_rows, dtype=jnp.int32)
        allowed = key_pos[None, :] <= query_pos[:, None]
        scores = low_back(jnp.where(allowed, scores, -1e+30))
        row_max = lax.optimization_barrier(jnp.max(scores, axis=-1, keepdims=True))
        weights = jnp.exp(scores - row_max)
        probs_low = low(weights / lax.optimization_barrier(jnp.sum(weights, axis=-1, keepdims=True)))
        result = jnp.einsum('grqk,kgd->qgrd', probs_low, values, precision=lax.Precision.HIGHEST)
        return result.reshape(block_rows, HEADS * HEAD_DIM)
    starts = jnp.arange(full_span // block_rows, dtype=jnp.int32) * block_rows
    outputs = lax.map(jax.checkpoint(one_block), starts)
    return low_back(low(outputs.reshape(full_span, HEADS * HEAD_DIM)))

def layer(state, weights, cosine_table, sine_table):
    w_q, w_k, w_v, w_o, w_gate, w_up, w_down, gain_one, gain_two = weights
    full_span = state.shape[0]
    normed_one = low(norm_apply(state, gain_one))
    query_pre = low_back(product(normed_one, w_q)).reshape(full_span, HEADS, HEAD_DIM)
    key_pre = low_back(product(normed_one, w_k)).reshape(full_span, KV_HEADS, HEAD_DIM)
    value_low = low_back(low(product(normed_one, w_v))).reshape(full_span, KV_HEADS, HEAD_DIM)
    query_low = low_back(low(rotate(query_pre, cosine_table, sine_table)))
    key_low = low_back(low(rotate(key_pre, cosine_table, sine_table)))
    attended = attention(query_low, key_low, value_low)
    middle = state + low_back(product(attended, w_o))
    normed_two = low(norm_apply(middle, gain_two))
    gate_proj = low_back(product(normed_two, w_gate))
    up_proj = low_back(product(normed_two, w_up))
    hidden = low(gate_proj * jax.nn.sigmoid(gate_proj) * up_proj)
    return middle + low_back(product(hidden, w_down))

def reference(tokens, cotangent, w_query, w_key, w_value, w_out, w_gate, w_up, w_down, gain_attn, gain_mlp):
    params = (w_query.astype(jnp.float32), w_key.astype(jnp.float32), w_value.astype(jnp.float32), w_out.astype(jnp.float32), w_gate.astype(jnp.float32), w_up.astype(jnp.float32), w_down.astype(jnp.float32), gain_attn.astype(jnp.float32), gain_mlp.astype(jnp.float32))
    positions = jnp.arange(LENGTH).astype(jnp.float32)
    cosine_table, sine_table = rope_tables(positions, HEAD_DIM // 2)

    def forward(state, weights_all):
        for layer_index in range(LAYERS):
            layer_weights = tuple((weight_arr[layer_index] for weight_arr in weights_all))
            state = layer(state, layer_weights, cosine_table, sine_table)
        return state

    def one_sequence(totals, seq_pair):
        seq_in, seq_ct = seq_pair
        seq_out, pullback = jax.vjp(forward, seq_in.astype(jnp.float32), params)
        grad_in, grad_params = pullback(seq_ct.astype(jnp.float32))
        totals = jax.tree.map(lambda left, right: left + right, totals, grad_params)
        return (totals, (seq_out, grad_in))
    zeros_init = jax.tree.map(jnp.zeros_like, params)
    totals, (seq_outs, grads_in) = lax.scan(one_sequence, zeros_init, (tokens, cotangent))
    return (seq_outs, grads_in, totals[0], totals[1], totals[2], totals[3], totals[4], totals[5], totals[6], totals[7], totals[8])
```

```python
import functools

import jax
import jax.numpy as jnp
from jax import lax
from jax.experimental import pallas as pl
from jax.experimental.pallas import tpu as pltpu
from jax.sharding import PartitionSpec as P

HEADS = 16
KV_HEADS = 8
HEAD_DIM = 96
GROUP = HEADS // KV_HEADS
EPS = 1e-05
ROPE_BASE = 100000.0
BF = jnp.bfloat16
F32 = jnp.float32
NEG = -1e30
KV_STEP = 4
SCALE = HEAD_DIM ** (-0.5)


def dot(a, b, dims):
    return lax.dot_general(a, b, (dims, ((), ())), preferred_element_type=F32)


def nn(a, b):
    return dot(a, b, ((1,), (0,)))


def nt(a, b):
    return dot(a, b, ((1,), (1,)))


def tn(a, b):
    return dot(a, b, ((0,), (0,)))


def chunk_mask(tokens):
    row = lax.broadcasted_iota(jnp.int32, (tokens, tokens), 0)
    col = lax.broadcasted_iota(jnp.int32, (tokens, tokens), 1)
    mask = col <= row
    return jnp.concatenate([mask] * GROUP, axis=0)


def head_scores(place, q, keys, mask):
    scores = []
    for r, k in enumerate(keys):
        s = nt(q, k) * SCALE
        if r == 0:
            s = jnp.where(mask, s, NEG)
        else:
            s = jnp.where(place >= r, s, NEG)
        scores.append(s)
    return scores


def lanes(ref, head, width=HEAD_DIM):
    return ref[:, head * HEAD_DIM : head * HEAD_DIM + width]


def two_heads(ref, g):
    return jnp.concatenate([lanes(ref, GROUP * g + i) for i in range(GROUP)], axis=0)


def attend_body(chunks, place_ref, q_ref, *refs):
    k_refs, v_refs = refs[:chunks], refs[chunks : 2 * chunks]
    o_ref, lse_ref = refs[2 * chunks :]
    tokens = q_ref.shape[0]
    place = place_ref[0]
    mask = chunk_mask(tokens)
    lse_ref[...] = jnp.zeros_like(lse_ref)
    for g in range(KV_STEP):
        q = two_heads(q_ref, g)
        scores = head_scores(place, q, [lanes(k, g) for k in k_refs], mask)
        top = functools.reduce(
            jnp.maximum, [jnp.max(s, axis=1, keepdims=True) for s in scores]
        )
        weights = [jnp.exp(s - top) for s in scores]
        total = sum(jnp.sum(w, axis=1, keepdims=True) for w in weights)
        inverse = 1.0 / total
        out = sum(
            nn((w * inverse).astype(BF), lanes(v, g)) for w, v in zip(weights, v_refs)
        )
        lse = top + jnp.log(total)
        for i in range(GROUP):
            h = GROUP * g + i
            o_ref[:, h * HEAD_DIM : (h + 1) * HEAD_DIM] = out[
                i * tokens : (i + 1) * tokens
            ].astype(BF)
            lse_ref[0, :, h : h + 1] = lse[i * tokens : (i + 1) * tokens]


def attend_back_body(chunks, place_ref, q_ref, do_ref, lse_ref, *refs):
    k_refs, v_refs = refs[:chunks], refs[chunks : 2 * chunks]
    dq_ref = refs[2 * chunks]
    dk_refs = refs[2 * chunks + 1 : 3 * chunks + 1]
    dv_refs = refs[3 * chunks + 1 :]
    tokens = q_ref.shape[0]
    place = place_ref[0]
    mask = chunk_mask(tokens)
    for g in range(KV_STEP):
        q = two_heads(q_ref, g)
        do = two_heads(do_ref, g)
        lse = jnp.concatenate(
            [lse_ref[0, :, GROUP * g + i : GROUP * g + i + 1] for i in range(GROUP)],
            axis=0,
        )
        keys = [lanes(k, g) for k in k_refs]
        scores = head_scores(place, q, keys, mask)
        probs = [jnp.exp(s - lse) for s in scores]
        dprobs = [nt(do, lanes(v, g)) for v in v_refs]
        inner = sum(
            jnp.sum(p * d, axis=1, keepdims=True) for p, d in zip(probs, dprobs)
        )
        dq = jnp.zeros((GROUP * tokens, HEAD_DIM), F32)
        span = slice(g * HEAD_DIM, (g + 1) * HEAD_DIM)
        for r in range(chunks):
            ds = (probs[r] * (dprobs[r] - inner)).astype(BF)
            dq += nn(ds, keys[r])
            dk_refs[r][:, span] = (tn(ds, q) * SCALE).astype(BF)
            dv_refs[r][:, span] = tn(probs[r].astype(BF), do).astype(BF)
        dq = (dq * SCALE).astype(BF)
        for i in range(GROUP):
            h = GROUP * g + i
            dq_ref[:, h * HEAD_DIM : (h + 1) * HEAD_DIM] = dq[
                i * tokens : (i + 1) * tokens
            ]


def attention_specs(tokens):
    q_width = KV_STEP * GROUP * HEAD_DIM
    k_width = KV_STEP * HEAD_DIM
    steps = KV_HEADS // KV_STEP
    q_spec = pl.BlockSpec((tokens, q_width), lambda i, s: (0, i))
    k_spec = pl.BlockSpec((tokens, k_width), lambda i, s: (0, i))
    v_spec = pl.BlockSpec((tokens, k_width), lambda i, s: (0, i + steps))
    lse_spec = pl.BlockSpec((1, tokens, 128), lambda i, s: (i, 0, 0))
    return steps, q_spec, k_spec, v_spec, lse_spec


def attend(place, q, kvs):
    chunks, tokens = len(kvs), q.shape[0]
    steps, q_spec, k_spec, v_spec, lse_spec = attention_specs(tokens)
    span = chunks * tokens
    flops = 4 * HEADS * HEAD_DIM * tokens * span
    return pl.pallas_call(
        functools.partial(attend_body, chunks),
        grid_spec=pltpu.PrefetchScalarGridSpec(
            num_scalar_prefetch=1,
            grid=(steps,),
            in_specs=[q_spec] + [k_spec] * chunks + [v_spec] * chunks,
            out_specs=[q_spec, lse_spec],
        ),
        out_shape=[
            jax.ShapeDtypeStruct(q.shape, BF),
            jax.ShapeDtypeStruct((steps, tokens, 128), F32),
        ],
        cost_estimate=pl.CostEstimate(
            flops=flops, bytes_accessed=8 * q.size, transcendentals=HEADS * tokens * span
        ),
        name="attend",
    )(place, q, *kvs, *kvs)


def attend_back(place, q, do, lse, kvs):
    chunks, tokens = len(kvs), q.shape[0]
    steps, q_spec, k_spec, v_spec, lse_spec = attention_specs(tokens)
    span = chunks * tokens
    kvd = KV_HEADS * HEAD_DIM
    flops = 10 * HEADS * HEAD_DIM * tokens * span
    outs = pl.pallas_call(
        functools.partial(attend_back_body, chunks),
        grid_spec=pltpu.PrefetchScalarGridSpec(
            num_scalar_prefetch=1,
            grid=(steps,),
            in_specs=[q_spec, q_spec, lse_spec] + [k_spec] * chunks + [v_spec] * chunks,
            out_specs=[q_spec] + [k_spec] * (2 * chunks),
        ),
        out_shape=[jax.ShapeDtypeStruct(q.shape, BF)]
        + [jax.ShapeDtypeStruct((tokens, kvd), BF)] * (2 * chunks),
        cost_estimate=pl.CostEstimate(
            flops=flops, bytes_accessed=16 * q.size, transcendentals=HEADS * tokens * span
        ),
        name="attend_back",
    )(place, q, do, lse, *kvs, *kvs)
    return outs[0], outs[1 : chunks + 1], outs[chunks + 1 :]


def flip(value, axis, bit):
    size = lax.axis_size(axis)
    return lax.ppermute(value, axis, [(i, i ^ bit) for i in range(size)])


def gather_rows(shard, bits, me, parts):
    pieces = {0: shard}
    for bit in list(bits) + [1]:
        pieces.update({off ^ bit: flip(piece, "dp", bit) for off, piece in list(pieces.items())})
    rows = shard.shape[0]
    whole = jnp.zeros((parts * rows, shard.shape[1]), shard.dtype)
    for off, piece in pieces.items():
        whole = lax.dynamic_update_slice(whole, piece, ((me ^ off) * rows, 0))
    return whole


def xor_order(bits):
    order = [0]
    for bit in list(reversed(bits)) + [1]:
        order = order + [off ^ bit for off in order]
    return order


def scatter_term(left, right, bits):
    half = left.shape[1] // 2
    away = tn(left[:, half:], right).astype(BF)
    came = flip(away, "dp", 1)
    quarter = half // 2
    away = (tn(left[:, quarter:half], right) + came[quarter:]).astype(BF)
    kept = (tn(left[:, :quarter], right) + came[:quarter]).astype(BF)
    came = flip(away, "dp", bits[0])
    for bit in bits[1:]:
        size = kept.shape[0] // 2
        away = (kept[size:].astype(F32) + came[size:]).astype(BF)
        kept = (kept[:size].astype(F32) + came[:size]).astype(BF)
        came = flip(away, "dp", bit)
    return (kept.astype(F32) + came).astype(BF)


def line_sum(value, place):
    size = lax.axis_size("seq")
    rows = value.shape[0] // size

    def chunk(index):
        index = jnp.clip(index, 0, size - 1)
        return lax.dynamic_slice_in_dim(value, index * rows, rows, 0)

    total = chunk(place).astype(F32)
    for way in (1, -1):
        held = None
        for far in range(size - 1, 0, -1):
            mine = chunk(place + way * far)
            if held is not None:
                mine = (mine.astype(F32) + held).astype(BF)
            pairs = [(i, i + way) for i in range(size) if 0 <= i + way * far < size]
            held = lax.ppermute(mine, "seq", pairs)
        total = total + held
    total = total.astype(BF)
    out = jnp.zeros(value.shape, F32)
    out = lax.dynamic_update_slice(out, total.astype(F32), (place * rows, 0))
    for way in (1, -1):
        held = total
        for far in range(1, size):
            pairs = [
                (i, i + way) for i in range(size) if 0 <= i + way < size and 0 <= i - way * (far - 1) < size
            ]
            held = lax.ppermute(held, "seq", pairs)
            source = place - way * far
            index = jnp.clip(source, 0, size - 1) * rows
            old = lax.dynamic_slice(out, (index, 0), held.shape)
            good = (source >= 0) & (source < size)
            out = lax.dynamic_update_slice(
                out, jnp.where(good, held.astype(F32), old), (index, 0)
            )
    return out


def rope_tables(place, tokens, width):
    half = HEAD_DIM // 2
    positions = (place * tokens + jnp.arange(tokens, dtype=jnp.int32)).astype(F32)
    frequency = ROPE_BASE ** (-jnp.arange(half).astype(F32) / half)
    angles = positions[:, None] * frequency[None, :]
    cos, sin = jnp.cos(angles), jnp.sin(angles)
    zero = jnp.zeros_like(sin)
    heads = width // HEAD_DIM
    tile = lambda a, b: jnp.tile(jnp.concatenate([a, b], axis=1), (1, heads))
    return tile(cos, cos), tile(sin, zero), tile(zero, sin)


def rotate(field, tables, sign):
    cos, first, second = tables
    half = HEAD_DIM // 2
    width = field.shape[1]
    cos, first, second = cos[:, :width], first[:, :width], second[:, :width]
    ahead = jnp.concatenate([field[:, half:], field[:, :half]], axis=1)
    behind = jnp.concatenate([field[:, -half:], field[:, :-half]], axis=1)
    return field * cos + sign * (behind * second - ahead * first)


def norm_scale(values):
    return lax.rsqrt(jnp.mean(values * values, axis=-1, keepdims=True) + EPS)


def norm_back(values, scale, gain, grad):
    unit = values * scale
    grad_gain = jnp.sum(grad * unit, axis=0)
    scaled = grad * gain
    inner = jnp.mean(scaled * unit, axis=-1, keepdims=True)
    return scale * (scaled - unit * inner), grad_gain


def local(tokens, cotangent, w_query, w_key, w_value, w_out, w_gate, w_up, w_down, gain_attn, gain_mlp):
    dp, seq = lax.axis_size("dp"), lax.axis_size("seq")
    me, place = lax.axis_index("dp"), lax.axis_index("seq")
    bits = [1 << i for i in range(1, dp.bit_length() - 1)]
    turned = bits[1:] + bits[:1]
    model = tokens.shape[-1]
    rows = tokens.shape[1]
    kvd = w_key.shape[-1]
    place_arr = place.reshape(1).astype(jnp.int32)

    gains = {0: jnp.concatenate([gain_attn, gain_mlp], axis=0)}
    for bit in [1] + bits:
        gains.update({off ^ bit: flip(g, "dp", bit) for off, g in list(gains.items())})
    stacked = jnp.stack([gains[off] for off in range(dp)]).astype(F32)
    owner = (jnp.arange(dp)[:, None] ^ me) == jnp.arange(dp)[None, :]
    natural = jnp.sum(jnp.where(owner[:, :, None, None], stacked[None], 0.0), axis=1)
    natural = natural.transpose(1, 0, 2).reshape(2, 1, model)
    gain_one, gain_two = natural[0], natural[1]

    gather = functools.partial(gather_rows, me=me, parts=dp)
    w_q = gather(w_query[0], bits)
    w_k = gather(w_key[0], turned)
    w_v = gather(w_value[0], turned)
    w_o = gather(w_out[0], bits)
    w_g = gather(w_gate[0], bits)
    w_u = gather(w_up[0], turned)
    half_model = model // 2
    w_d = jnp.concatenate(
        [gather(w_down[0][:, :half_model], bits), gather(w_down[0][:, half_model:], turned)], axis=1
    )

    def xor_columns(value, way):
        width = value.shape[1] // dp
        cut = lambda off: lax.dynamic_slice_in_dim(value, (me ^ off) * width, width, 1)
        return jnp.concatenate([cut(off) for off in xor_order(way)], axis=1)

    tables = rope_tables(place, rows, model)
    x = tokens[0].astype(F32)
    scale_one = norm_scale(x)
    n1 = (x * scale_one * gain_one).astype(BF)
    q = rotate(nn(n1, w_q), tables, 1.0).astype(BF)
    kv = jnp.concatenate(
        [rotate(nn(n1, w_k), tables, 1.0).astype(BF), nn(n1, w_v).astype(BF)], axis=1
    )
    kvs = [kv]
    for far in range(1, seq):
        pairs = [(i, i + 1) for i in range(far - 1, seq - 1)]
        kvs.append(lax.ppermute(kvs[-1], "seq", pairs))
    mixed, lse = attend(place_arr, q, kvs)
    x2 = x + nn(mixed, w_o)
    scale_two = norm_scale(x2)
    n2 = (x2 * scale_two * gain_two).astype(BF)
    gate = nn(n2, w_g)
    up = nn(n2, w_u)
    sig = jax.nn.sigmoid(gate)
    hidden = (gate * sig * up).astype(BF)
    result = x2 + nn(hidden, w_d)

    e = cotangent[0].astype(F32)
    eb = cotangent[0]
    hidden_a = xor_columns(hidden, bits)
    hidden_b = xor_columns(hidden, turned)
    sum_down = jnp.concatenate(
        [
            scatter_term(hidden_a, eb[:, :half_model], bits),
            scatter_term(hidden_b, eb[:, half_model:], turned),
        ],
        axis=1,
    )
    dh = nt(eb, w_d)
    dgate = (dh * up * sig * (1.0 + gate * (1.0 - sig))).astype(BF)
    dup = (dh * gate * sig).astype(BF)
    n2_a, n2_b = xor_columns(n2, bits), xor_columns(n2, turned)
    sum_gate = scatter_term(n2_a, dgate, bits)
    sum_up = scatter_term(n2_b, dup, turned)
    dn2 = nt(dgate, w_g) + nt(dup, w_u)
    dx2, term_gain_two = norm_back(x2, scale_two, gain_two, dn2)
    e2 = e + dx2
    e2b = e2.astype(BF)
    mixed_a, mixed_b = xor_columns(mixed, bits), xor_columns(mixed, turned)
    sum_out = jnp.concatenate(
        [
            scatter_term(mixed_a, e2b[:, :half_model], bits),
            scatter_term(mixed_b, e2b[:, half_model:], turned),
        ],
        axis=1,
    )
    do = nt(e2b, w_o).astype(BF)
    dq, dks, dvs = attend_back(place_arr, q, do, lse, kvs)
    held = None
    for far in range(seq - 1, -1, -1):
        mine = jnp.concatenate([dks[far], dvs[far]], axis=1)
        if held is not None:
            mine = (mine.astype(F32) + held).astype(BF)
        if far:
            held = lax.ppermute(mine, "seq", [(i, i - 1) for i in range(far, seq)])
    dk, dv = mine[:, :kvd], mine[:, kvd:]
    dqp = rotate(dq.astype(F32), tables, -1.0).astype(BF)
    dkp = rotate(dk.astype(F32), tables, -1.0).astype(BF)
    n1_a, n1_b = xor_columns(n1, bits), xor_columns(n1, turned)
    sum_query = scatter_term(n1_a, dqp, bits)
    sum_kv = scatter_term(n1_b, jnp.concatenate([dkp, dv], axis=1), turned)
    dn1 = nt(dqp, w_q) + nt(dkp, w_k) + nt(dv, w_v)
    dx1, term_gain_one = norm_back(x, scale_one, gain_one, dn1)
    input_grad = e2 + dx1

    both = jnp.stack([term_gain_one, term_gain_two])
    for bit in [1] + bits:
        both = both + flip(both, "dp", bit)
    for bit in [1 << i for i in range(seq.bit_length() - 1)]:
        both = both + flip(both, "seq", bit)
    width = model // dp
    both = lax.dynamic_slice_in_dim(both, me * width, width, 1)

    g_down = line_sum(sum_down, place)
    g_gate = line_sum(sum_gate, place)
    g_up = line_sum(sum_up, place)
    g_out = line_sum(sum_out, place)
    g_query = line_sum(sum_query, place)
    g_kv = line_sum(sum_kv, place)
    return (
        result[None],
        input_grad[None],
        g_query[None],
        g_kv[None, :, :kvd],
        g_kv[None, :, kvd:],
        g_out[None],
        g_gate[None],
        g_up[None],
        g_down[None],
        both[0:1],
        both[1:2],
    )


def solution(mesh):
    by_token = P("dp", "seq", None)
    by_row = P(None, "dp", None)
    by_gain = P(None, "dp")
    in_specs = (by_token,) * 2 + (by_row,) * 7 + (by_gain,) * 2
    return jax.shard_map(local, mesh=mesh, in_specs=in_specs, out_specs=in_specs, check_vma=False)
```

```python
import functools

import jax
import jax.numpy as jnp
from jax import lax
from jax.experimental import pallas as pl
from jax.experimental.pallas import tpu as pltpu
from jax.sharding import PartitionSpec as P

HEADS = 16
KV_HEADS = 8
HEAD_DIM = 96
GROUP = HEADS // KV_HEADS
EPS = 1e-05
ROPE_BASE = 100000.0
BF = jnp.bfloat16
F32 = jnp.float32
NEG = -1e30
KV_STEP = 4
SCALE = HEAD_DIM ** (-0.5)


def dot(a, b, dims):
    return lax.dot_general(a, b, (dims, ((), ())), preferred_element_type=F32)


def nn(a, b):
    return dot(a, b, ((1,), (0,)))


def nt(a, b):
    return dot(a, b, ((1,), (1,)))


def tn(a, b):
    return dot(a, b, ((0,), (0,)))


def chunk_mask(tokens):
    row = lax.broadcasted_iota(jnp.int32, (tokens, tokens), 0)
    col = lax.broadcasted_iota(jnp.int32, (tokens, tokens), 1)
    mask = col <= row
    return jnp.concatenate([mask] * GROUP, axis=0)


def head_scores(place, q, keys, mask):
    scores = []
    for r, k in enumerate(keys):
        s = nt(q, k) * SCALE
        if r == 0:
            s = jnp.where(mask, s, NEG)
        else:
            s = jnp.where(place >= r, s, NEG)
        scores.append(s)
    return scores


def lanes(ref, head, width=HEAD_DIM):
    return ref[:, head * HEAD_DIM : head * HEAD_DIM + width]


def two_heads(ref, g):
    return jnp.concatenate([lanes(ref, GROUP * g + i) for i in range(GROUP)], axis=0)


def attend_back_body(chunks, place_ref, q_ref, do_ref, lse_ref, *refs):
    k_refs, v_refs = refs[:chunks], refs[chunks : 2 * chunks]
    dq_ref = refs[2 * chunks]
    dk_refs = refs[2 * chunks + 1 : 3 * chunks + 1]
    dv_refs = refs[3 * chunks + 1 :]
    tokens = q_ref.shape[0]
    place = place_ref[0]
    mask = chunk_mask(tokens)
    for g in range(KV_STEP):
        q = two_heads(q_ref, g)
        do = two_heads(do_ref, g)
        lse = jnp.concatenate(
            [lse_ref[0, :, GROUP * g + i : GROUP * g + i + 1] for i in range(GROUP)],
            axis=0,
        )
        keys = [lanes(k, g) for k in k_refs]
        scores = head_scores(place, q, keys, mask)
        probs = [jnp.exp(s - lse) for s in scores]
        dprobs = [nt(do, lanes(v, g)) for v in v_refs]
        inner = sum(
            jnp.sum(p * d, axis=1, keepdims=True) for p, d in zip(probs, dprobs)
        )
        dq = jnp.zeros((GROUP * tokens, HEAD_DIM), F32)
        span = slice(g * HEAD_DIM, (g + 1) * HEAD_DIM)
        for r in range(chunks):
            ds = (probs[r] * (dprobs[r] - inner)).astype(BF)
            dq += nn(ds, keys[r])
            dk_refs[r][:, span] = (tn(ds, q) * SCALE).astype(BF)
            dv_refs[r][:, span] = tn(probs[r].astype(BF), do).astype(BF)
        dq = (dq * SCALE).astype(BF)
        for i in range(GROUP):
            h = GROUP * g + i
            dq_ref[:, h * HEAD_DIM : (h + 1) * HEAD_DIM] = dq[
                i * tokens : (i + 1) * tokens
            ]


def attention_specs(tokens):
    q_width = KV_STEP * GROUP * HEAD_DIM
    k_width = KV_STEP * HEAD_DIM
    steps = KV_HEADS // KV_STEP
    q_spec = pl.BlockSpec((tokens, q_width), lambda i, s: (0, i))
    k_spec = pl.BlockSpec((tokens, k_width), lambda i, s: (0, i))

    def kv_spec(r, at):
        return pl.BlockSpec((None, tokens, k_width), lambda i, s: (r, 0, i + at))
    lse_spec = pl.BlockSpec((1, tokens, 128), lambda i, s: (i, 0, 0))
    return steps, q_spec, k_spec, kv_spec, lse_spec


def attend_back(place, q, do, lse, kvs):
    chunks, tokens = kvs.shape[0], q.shape[0]
    steps, q_spec, k_spec, kv_spec, lse_spec = attention_specs(tokens)
    span = chunks * tokens
    kvd = KV_HEADS * HEAD_DIM
    flops = 10 * HEADS * HEAD_DIM * tokens * span
    outs = pl.pallas_call(
        functools.partial(attend_back_body, chunks),
        grid_spec=pltpu.PrefetchScalarGridSpec(
            num_scalar_prefetch=1,
            grid=(steps,),
            in_specs=[q_spec, q_spec, lse_spec]
            + [kv_spec(r, 0) for r in range(chunks)]
            + [kv_spec(r, steps) for r in range(chunks)],
            out_specs=[q_spec] + [k_spec] * (2 * chunks),
        ),
        out_shape=[jax.ShapeDtypeStruct(q.shape, BF)]
        + [jax.ShapeDtypeStruct((tokens, kvd), BF)] * (2 * chunks),
        cost_estimate=pl.CostEstimate(
            flops=flops, bytes_accessed=16 * q.size, transcendentals=HEADS * tokens * span
        ),
        name="attend_back",
    )(place, q, do, lse, *[kvs] * (2 * chunks))
    return outs[0], outs[1 : chunks + 1], outs[chunks + 1 :]


MESH = pl.DeviceIdType.MESH
TILE = 4 * HEAD_DIM


class Gather:
    def __init__(self, me, place, bits, src, out, send, recv):
        self.me, self.bits, self.src, self.out = me, bits, src, out
        self.send, self.recv = send, recv
        self.rows = src.shape[0]
        self.quarter = -(-self.rows // 64) * 16
        self.most = self.rows - self.quarter
        units, parts = self.most // 16, len(bits)
        self.size = [16 * (units // parts + (i < units % parts)) for i in range(parts)]
        self.start = [sum(self.size[:i]) for i in range(parts)]
        self.odd = place % 2
        self.pair = place + 1 - 2 * self.odd
        self.count = 0
        self.waits = []
        own = {}
        for bit in bits:
            own[bit] = self.copy(self.src, 0, 1, self.most, bit, self.odd * self.quarter)
        self.own = own
        self.own_core = self.copy(self.src, 0, 0, self.rows, 1, 0)
        self.forwards = []
        self.arrival = {}
        for bit in bits:
            for i in range(len(bits)):
                self.arrival[(bit, i)] = own[bit]
        for step in range(1, len(bits)):
            for i in range(len(bits)):
                order = bits[i:] + bits[:i]
                bit = order[step]
                held = [0]
                for b in order[:step]:
                    held = held + [m | b for m in held]
                for m in held[1:]:
                    start = self.odd * self.quarter + self.start[i]
                    made = self.copy(out, m, 1, self.size[i], bit, start)
                    self.forwards.append((m, i, made))
                    self.arrival[(m | bit, i)] = made
        masks = list(range(2, 2 * max(bits), 2))
        self.masks = masks
        self.across = [
            self.copy(out, m, 2, self.quarter, 0, self.odd * self.most) for m in masks
        ]
        self.core = [self.copy(out, m, 1, self.rows, 1, 0) for m in masks]
        self.seen = set()

    def copy(self, ref, m, kind, rows, bit, start):
        at = (self.me ^ m) * self.rows + start
        source = ref.at[pl.ds(pl.multiple_of(start, 16), rows)] if ref is self.src else ref.at[pl.ds(pl.multiple_of(at, 16), rows)]
        target = {"seq": self.pair} if kind == 2 else {"dp": self.me ^ bit}
        index = self.count
        self.count += 1
        return pltpu.make_async_remote_copy(
            src_ref=source,
            dst_ref=self.out.at[pl.ds(pl.multiple_of(at, 16), rows)],
            send_sem=self.send.at[index],
            recv_sem=self.recv.at[index],
            device_id=target,
            device_id_type=MESH,
        )

    def begin(self):
        for bit in self.bits:
            self.own[bit].start()
        self.own_core.start()

    def arrived(self, copy):
        if id(copy) not in self.seen:
            self.seen.add(id(copy))
            copy.wait_recv()

    def forward(self):
        for m, i, made in self.forwards:
            self.arrived(self.arrival[(m, i)])
            made.start()

    def cross(self):
        for m, made in zip(self.masks, self.across):
            for i in range(len(self.bits)):
                self.arrived(self.arrival[(m, i)])
            made.start()

    def share(self):
        for across, made in zip(self.across, self.core):
            across.wait_recv()
            made.start()

    def finish(self):
        self.own_core.wait_recv()
        for made in self.core:
            made.wait_recv()

    def drain(self):
        for made in list(self.own.values()) + [self.own_core] + [f[2] for f in self.forwards] + self.across + self.core:
            made.wait_send()


def gather_copies(chip_bits):
    forwards = sum(chip_bits * (2**step - 1) for step in range(1, chip_bits))
    return chip_bits + 1 + forwards + 2 * (2**chip_bits - 1)


def forward_body(dp, seq, x_ref, gain_ref, cos_ref, first_ref, second_ref, *refs):
    w_in, refs = refs[:7], refs[7:]
    w_out, refs = refs[:7], refs[7:]
    q_ref, o_ref, lse_ref, n1_ref, gains_ref, kvs_ref = refs[:6]
    stage, refs = refs[6:13], refs[13:]
    wq, wk, wv, kvbuf, gbuf, qh, kh, vh, oh, send, recv, kv_send, kv_recv, g_send, g_recv, own_sem, load_sem, kv_out = refs
    me, place = lax.axis_index("dp"), lax.axis_index("seq")
    bits = [1 << i for i in range(1, dp.bit_length() - 1)]
    tokens, model = x_ref.shape
    block = model // dp

    for i in range(7):
        pltpu.make_async_copy(w_in[i], stage[i], own_sem.at[i]).start()
    for r in range(1, seq):
        kvbuf[r] = jnp.zeros_like(kvbuf[r])

    barrier = pltpu.get_barrier_semaphore()
    for off in range(1, dp):
        pl.semaphore_signal(barrier, inc=1, device_id={"dp": me ^ off}, device_id_type=MESH)
    up, down = place + 1, place - 1
    odd = place % 2
    pair = place + 1 - 2 * odd
    other = place - 1 + 2 * odd
    has_other = (other >= 0) & (other < seq)
    pl.semaphore_signal(barrier, inc=1, device_id={"seq": pair}, device_id_type=MESH)

    @pl.when(has_other)
    def _():
        pl.semaphore_signal(barrier, inc=1, device_id={"seq": other}, device_id_type=MESH)

        pl.semaphore_wait(barrier, dp + 1)

    @pl.when(jnp.logical_not(has_other))
    def _():
        pl.semaphore_wait(barrier, dp)

    gains = [
        pltpu.make_async_remote_copy(
            src_ref=gain_ref,
            dst_ref=gbuf.at[me],
            send_sem=g_send.at[off],
            recv_sem=g_recv.at[off],
            device_id={"dp": me ^ off},
            device_id_type=MESH,
        )
        for off in range(1, dp)
    ]
    for g in gains:
        g.start()
    turned = bits[1:] + bits[:1]
    jobs = [
        Gather(me, place, turned if i in (1, 2, 5) else bits, w_in[i], w_out[i], send.at[i], recv.at[i])
        for i in range(7)
    ]
    first = jobs[:3]
    job_o, job_g, job_u, job_d = jobs[3:]
    for job in first:
        job.begin()

    def own_out(i):
        rows = w_in[i].shape[0]
        return pltpu.make_async_copy(stage[i], w_out[i].at[pl.ds(pl.multiple_of(me * rows, 8), rows)], own_sem.at[i])

    for i in range(7):
        pltpu.make_async_copy(w_in[i], stage[i], own_sem.at[i]).wait()
        own_out(i).start()

    gbuf[me] = gain_ref[...]
    x = x_ref[...].astype(F32)
    scale = lax.rsqrt(jnp.mean(x * x, axis=1, keepdims=True) + EPS)
    for g in gains:
        g.wait_recv()
    for k in range(dp):
        gains_ref[:, k * block : (k + 1) * block] = gbuf[k, :, :block]
    n1_ref[...] = (x * scale * gains_ref[0:1, :]).astype(BF)

    for job in first:
        job.forward()
    job_o.begin()
    job_g.begin()
    for job in first:
        job.cross()
    for job in first:
        job.share()
    for i in range(7):
        own_out(i).wait()
    for job in first:
        job.finish()
    loads = [
        pltpu.make_async_copy(w_out[i], ref, load_sem.at[i]) for i, ref in enumerate((wq, wk, wv))
    ]
    for load in loads:
        load.start()

    def turn(value):
        ahead = pltpu.roll(value, TILE - HEAD_DIM // 2, 1)
        behind = pltpu.roll(value, HEAD_DIM // 2, 1)
        return value * cos_ref[...] + behind * second_ref[...] - ahead * first_ref[...]

    kvd = wk.shape[1]
    loads[1].wait()

    @pl.loop(0, kvd // TILE)
    def _(t):
        at = pl.multiple_of(t * TILE, 128)
        kvbuf[0, :, pl.ds(at, TILE)] = turn(nn(n1_ref[...], wk[:, pl.ds(at, TILE)])).astype(BF)

    loads[2].wait()

    @pl.loop(0, kvd // TILE)
    def _(t):
        at = pl.multiple_of(t * TILE, 128)
        kvbuf[0, :, pl.ds(kvd + at, TILE)] = nn(n1_ref[...], wv[:, pl.ds(at, TILE)]).astype(BF)

    def kv_copy(r):
        return pltpu.make_async_remote_copy(
            src_ref=kvbuf.at[r],
            dst_ref=kvbuf.at[r + 1],
            send_sem=kv_send.at[r],
            recv_sem=kv_recv.at[r],
            device_id={"seq": up},
            device_id_type=MESH,
        )

    def kv_send_on(r):
        @pl.when((place >= r) & (place < seq - 1))
        def _():
            kv_copy(r).start()

    def kv_wait(r):
        @pl.when(place >= r)
        def _():
            pltpu.make_async_remote_copy(
                src_ref=kvbuf.at[r - 1],
                dst_ref=kvbuf.at[r],
                send_sem=kv_send.at[r - 1],
                recv_sem=kv_recv.at[r - 1],
                device_id={"seq": down},
                device_id_type=MESH,
            ).wait_recv()

    kv_send_on(0)
    loads[0].wait()

    @pl.loop(0, model // TILE)
    def _(t):
        at = pl.multiple_of(t * TILE, 128)
        q_ref[:, pl.ds(at, TILE)] = turn(nn(n1_ref[...], wq[:, pl.ds(at, TILE)])).astype(BF)

    for h in range(HEADS):
        qh[h] = lanes(q_ref, h)

    def split_heads(r):
        for g in range(KV_HEADS):
            kh[g, r * tokens : (r + 1) * tokens, :] = kvbuf[r, :, g * HEAD_DIM : (g + 1) * HEAD_DIM]
            vh[g, r * tokens : (r + 1) * tokens, :] = kvbuf[r, :, kvd + g * HEAD_DIM : kvd + (g + 1) * HEAD_DIM]

    job_o.forward()
    job_u.begin()
    split_heads(0)
    for r in range(1, seq):
        kv_wait(r)
        if r < seq - 1:
            kv_send_on(r)
        if r == 1:
            job_o.cross()
            job_g.forward()
            job_d.begin()
            job_o.share()
        split_heads(r)
    job_g.cross()

    row = lax.broadcasted_iota(jnp.int32, (tokens, tokens), 0)
    col = lax.broadcasted_iota(jnp.int32, (tokens, tokens), 1)
    lse_ref[...] = jnp.zeros_like(lse_ref)
    lane = lax.broadcasted_iota(jnp.int32, (tokens, 128), 1)

    half = HEADS // 2

    def attend_heads(start, stop):
        @pl.loop(start, stop)
        def _(h):
            g = h // GROUP
            q = qh[h]
            scores = []
            for r in range(seq):
                s = nt(q, kh[g, r * tokens : (r + 1) * tokens, :]) * SCALE
                scores.append(jnp.where(col <= row if r == 0 else place >= r, s, NEG))
            top = functools.reduce(jnp.maximum, [jnp.max(s, axis=1, keepdims=True) for s in scores])
            weights = [jnp.exp(s - top) for s in scores]
            total = sum(jnp.sum(w, axis=1, keepdims=True) for w in weights)
            inverse = 1.0 / total
            oh[h] = sum(
                nn((w * inverse).astype(BF), vh[g, r * tokens : (r + 1) * tokens, :])
                for r, w in enumerate(weights)
            ).astype(BF)
            lse_ref[h // half] += jnp.where(lane == h % half, top + jnp.log(total), 0.0)

    attend_heads(0, half)
    job_g.share()
    job_u.forward()
    attend_heads(half, HEADS)
    for h in range(HEADS):
        o_ref[:, h * HEAD_DIM : (h + 1) * HEAD_DIM] = oh[h]
    job_u.cross()
    job_d.forward()
    job_u.share()
    job_d.cross()
    job_d.share()
    kv_save = pltpu.make_async_copy(kvbuf, kvs_ref, kv_out)
    kv_save.start()
    for job in (job_o, job_g, job_u, job_d):
        job.finish()
    for r in range(seq - 1):

        @pl.when((place >= r) & (place < seq - 1))
        def _():
            kv_copy(r).wait_send()

    for g in gains:
        g.wait_send()
    for job in jobs:
        job.drain()
    kv_save.wait()


def forward_call(dp, seq, x, gains, tables, weights):
    tokens, model = x.shape
    chip_bits = dp.bit_length() - 2
    copies = gather_copies(chip_bits)
    anyspec = pl.BlockSpec(memory_space=pl.ANY)
    vmem = pl.BlockSpec(memory_space=pltpu.VMEM)
    out_shape = [jax.ShapeDtypeStruct((dp * w.shape[0], w.shape[1]), BF) for w in weights]
    out_shape += [
        jax.ShapeDtypeStruct((tokens, model), BF),
        jax.ShapeDtypeStruct((tokens, model), BF),
        jax.ShapeDtypeStruct((2, tokens, 128), F32),
        jax.ShapeDtypeStruct((tokens, model), BF),
        jax.ShapeDtypeStruct((8, model), F32),
        jax.ShapeDtypeStruct((seq, tokens, model), BF),
    ]
    kvd = weights[1].shape[1]
    dma = pltpu.SemaphoreType.DMA
    return pl.pallas_call(
        functools.partial(forward_body, dp, seq),
        out_shape=out_shape,
        in_specs=[vmem] * 5 + [anyspec] * 7,
        out_specs=[anyspec] * 7 + [vmem] * 5 + [anyspec],
        scratch_shapes=[pltpu.VMEM(w.shape, BF) for w in weights]
        + [
            pltpu.VMEM((model, model), BF),
            pltpu.VMEM((model, kvd), BF),
            pltpu.VMEM((model, kvd), BF),
            pltpu.VMEM((seq, tokens, model), BF),
            pltpu.VMEM((dp, 8, 256), F32),
            pltpu.VMEM((HEADS, tokens, HEAD_DIM), BF),
            pltpu.VMEM((KV_HEADS, seq * tokens, HEAD_DIM), BF),
            pltpu.VMEM((KV_HEADS, seq * tokens, HEAD_DIM), BF),
            pltpu.VMEM((HEADS, tokens, HEAD_DIM), BF),
            dma((7, copies)),
            dma((7, copies)),
            dma((seq,)),
            dma((seq,)),
            dma((dp,)),
            dma((dp,)),
            dma((7,)),
            dma((3,)),
            dma(()),
        ],
        compiler_params=pltpu.CompilerParams(
            collective_id=0, has_side_effects=True, vmem_limit_bytes=60 * 1024 * 1024
        ),
        name="forward",
    )(x, gains, *tables, *weights)


def flip(value, axis, bit):
    size = lax.axis_size(axis)
    return lax.ppermute(value, axis, [(i, i ^ bit) for i in range(size)])


def xor_order(bits):
    order = [0]
    for bit in list(reversed(bits)) + [1]:
        order = order + [off ^ bit for off in order]
    return order


def scatter_term(left, right, bits):
    half = left.shape[1] // 2
    away = tn(left[:, half:], right).astype(BF)
    came = flip(away, "dp", 1)
    quarter = half // 2
    away = (tn(left[:, quarter:half], right) + came[quarter:]).astype(BF)
    kept = (tn(left[:, :quarter], right) + came[:quarter]).astype(BF)
    came = flip(away, "dp", bits[0])
    for bit in bits[1:]:
        size = kept.shape[0] // 2
        away = (kept[size:].astype(F32) + came[size:]).astype(BF)
        kept = (kept[:size].astype(F32) + came[:size]).astype(BF)
        came = flip(away, "dp", bit)
    return (kept.astype(F32) + came).astype(BF)


def line_sum(value, place):
    size = lax.axis_size("seq")
    rows = value.shape[0] // size

    def chunk(index):
        index = jnp.clip(index, 0, size - 1)
        return lax.dynamic_slice_in_dim(value, index * rows, rows, 0)

    total = chunk(place).astype(F32)
    for way in (1, -1):
        held = None
        for far in range(size - 1, 0, -1):
            mine = chunk(place + way * far)
            if held is not None:
                mine = (mine.astype(F32) + held).astype(BF)
            pairs = [(i, i + way) for i in range(size) if 0 <= i + way * far < size]
            held = lax.ppermute(mine, "seq", pairs)
        total = total + held
    total = total.astype(BF)
    out = jnp.zeros(value.shape, F32)
    out = lax.dynamic_update_slice(out, total.astype(F32), (place * rows, 0))
    for way in (1, -1):
        held = total
        for far in range(1, size):
            pairs = [
                (i, i + way) for i in range(size) if 0 <= i + way < size and 0 <= i - way * (far - 1) < size
            ]
            held = lax.ppermute(held, "seq", pairs)
            source = place - way * far
            index = jnp.clip(source, 0, size - 1) * rows
            old = lax.dynamic_slice(out, (index, 0), held.shape)
            good = (source >= 0) & (source < size)
            out = lax.dynamic_update_slice(
                out, jnp.where(good, held.astype(F32), old), (index, 0)
            )
    return out


def rope_tables(place, tokens, width):
    half = HEAD_DIM // 2
    positions = (place * tokens + jnp.arange(tokens, dtype=jnp.int32)).astype(F32)
    frequency = ROPE_BASE ** (-jnp.arange(half).astype(F32) / half)
    angles = positions[:, None] * frequency[None, :]
    cos, sin = jnp.cos(angles), jnp.sin(angles)
    zero = jnp.zeros_like(sin)
    heads = width // HEAD_DIM
    tile = lambda a, b: jnp.tile(jnp.concatenate([a, b], axis=1), (1, heads))
    return tile(cos, cos), tile(sin, zero), tile(zero, sin)


def rotate(field, tables, sign):
    cos, first, second = tables
    half = HEAD_DIM // 2
    width = field.shape[1]
    cos, first, second = cos[:, :width], first[:, :width], second[:, :width]
    ahead = jnp.concatenate([field[:, half:], field[:, :half]], axis=1)
    behind = jnp.concatenate([field[:, -half:], field[:, :-half]], axis=1)
    return field * cos + sign * (behind * second - ahead * first)


def norm_scale(values):
    return lax.rsqrt(jnp.mean(values * values, axis=-1, keepdims=True) + EPS)


def norm_back(values, scale, gain, grad):
    unit = values * scale
    grad_gain = jnp.sum(grad * unit, axis=0)
    scaled = grad * gain
    inner = jnp.mean(scaled * unit, axis=-1, keepdims=True)
    return scale * (scaled - unit * inner), grad_gain


def local(tokens, cotangent, w_query, w_key, w_value, w_out, w_gate, w_up, w_down, gain_attn, gain_mlp):
    dp, seq = lax.axis_size("dp"), lax.axis_size("seq")
    me, place = lax.axis_index("dp"), lax.axis_index("seq")
    bits = [1 << i for i in range(1, dp.bit_length() - 1)]
    turned = bits[1:] + bits[:1]
    model = tokens.shape[-1]
    rows = tokens.shape[1]
    kvd = w_key.shape[-1]
    place_arr = place.reshape(1).astype(jnp.int32)

    half_model = model // 2

    def xor_columns(value, way):
        width = value.shape[1] // dp
        cut = lambda off: lax.dynamic_slice_in_dim(value, (me ^ off) * width, width, 1)
        return jnp.concatenate([cut(off) for off in xor_order(way)], axis=1)

    tables = rope_tables(place, rows, model)
    x = tokens[0].astype(F32)
    packed = jnp.zeros((8, 256), F32)
    packed = packed.at[0, : gain_attn.shape[1]].set(gain_attn[0].astype(F32))
    packed = packed.at[1, : gain_mlp.shape[1]].set(gain_mlp[0].astype(F32))
    shards = [w[0] for w in (w_query, w_key, w_value, w_out, w_gate, w_up, w_down)]
    outs = forward_call(dp, seq, tokens[0], packed, [t[:, :TILE] for t in tables], shards)
    w_q, w_k, w_v, w_o, w_g, w_u, w_d = outs[:7]
    q, mixed, lse, n1, gains, kvs = outs[7:]
    gain_one, gain_two = gains[0:1], gains[1:2]
    scale_one = norm_scale(x)
    x2 = x + nn(mixed, w_o)
    scale_two = norm_scale(x2)
    n2 = (x2 * scale_two * gain_two).astype(BF)
    gate = nn(n2, w_g)
    up = nn(n2, w_u)
    sig = jax.nn.sigmoid(gate)
    hidden = (gate * sig * up).astype(BF)
    result = x2 + nn(hidden, w_d)

    e = cotangent[0].astype(F32)
    eb = cotangent[0]
    hidden_a = xor_columns(hidden, bits)
    hidden_b = xor_columns(hidden, turned)
    sum_down = jnp.concatenate(
        [
            scatter_term(hidden_a, eb[:, :half_model], bits),
            scatter_term(hidden_b, eb[:, half_model:], turned),
        ],
        axis=1,
    )
    dh = nt(eb, w_d)
    dgate = (dh * up * sig * (1.0 + gate * (1.0 - sig))).astype(BF)
    dup = (dh * gate * sig).astype(BF)
    n2_a, n2_b = xor_columns(n2, bits), xor_columns(n2, turned)
    sum_gate = scatter_term(n2_a, dgate, bits)
    sum_up = scatter_term(n2_b, dup, turned)
    dn2 = nt(dgate, w_g) + nt(dup, w_u)
    dx2, term_gain_two = norm_back(x2, scale_two, gain_two, dn2)
    e2 = e + dx2
    e2b = e2.astype(BF)
    mixed_a, mixed_b = xor_columns(mixed, bits), xor_columns(mixed, turned)
    sum_out = jnp.concatenate(
        [
            scatter_term(mixed_a, e2b[:, :half_model], bits),
            scatter_term(mixed_b, e2b[:, half_model:], turned),
        ],
        axis=1,
    )
    do = nt(e2b, w_o).astype(BF)
    dq, dks, dvs = attend_back(place_arr, q, do, lse, kvs)
    held = None
    for far in range(seq - 1, -1, -1):
        mine = jnp.concatenate([dks[far], dvs[far]], axis=1)
        if held is not None:
            mine = (mine.astype(F32) + held).astype(BF)
        if far:
            held = lax.ppermute(mine, "seq", [(i, i - 1) for i in range(far, seq)])
    dk, dv = mine[:, :kvd], mine[:, kvd:]
    dqp = rotate(dq.astype(F32), tables, -1.0).astype(BF)
    dkp = rotate(dk.astype(F32), tables, -1.0).astype(BF)
    n1_a, n1_b = xor_columns(n1, bits), xor_columns(n1, turned)
    sum_query = scatter_term(n1_a, dqp, bits)
    sum_kv = scatter_term(n1_b, jnp.concatenate([dkp, dv], axis=1), turned)
    dn1 = nt(dqp, w_q) + nt(dkp, w_k) + nt(dv, w_v)
    dx1, term_gain_one = norm_back(x, scale_one, gain_one, dn1)
    input_grad = e2 + dx1

    both = jnp.stack([term_gain_one, term_gain_two])
    for bit in [1] + bits:
        both = both + flip(both, "dp", bit)
    for bit in [1 << i for i in range(seq.bit_length() - 1)]:
        both = both + flip(both, "seq", bit)
    width = model // dp
    both = lax.dynamic_slice_in_dim(both, me * width, width, 1)

    g_down = line_sum(sum_down, place)
    g_gate = line_sum(sum_gate, place)
    g_up = line_sum(sum_up, place)
    g_out = line_sum(sum_out, place)
    g_query = line_sum(sum_query, place)
    g_kv = line_sum(sum_kv, place)
    return (
        result[None],
        input_grad[None],
        g_query[None],
        g_kv[None, :, :kvd],
        g_kv[None, :, kvd:],
        g_out[None],
        g_gate[None],
        g_up[None],
        g_down[None],
        both[0:1],
        both[1:2],
    )


def solution(mesh):
    by_token = P("dp", "seq", None)
    by_row = P(None, "dp", None)
    by_gain = P(None, "dp")
    in_specs = (by_token,) * 2 + (by_row,) * 7 + (by_gain,) * 2
    return jax.shard_map(local, mesh=mesh, in_specs=in_specs, out_specs=in_specs, check_vma=False)
```

```python
import functools

import jax
import jax.numpy as jnp
from jax import lax
from jax.experimental import pallas as pl
from jax.experimental.pallas import tpu as pltpu
from jax.sharding import PartitionSpec as P

HEADS = 16
KV_HEADS = 8
HEAD_DIM = 96
GROUP = HEADS // KV_HEADS
EPS = 1e-05
ROPE_BASE = 100000.0
BF = jnp.bfloat16
F32 = jnp.float32
NEG = -1e30
SCALE = HEAD_DIM ** (-0.5)


def dot(a, b, dims):
    return lax.dot_general(a, b, (dims, ((), ())), preferred_element_type=F32)


def nn(a, b):
    return dot(a, b, ((1,), (0,)))


def nt(a, b):
    return dot(a, b, ((1,), (1,)))


def tn(a, b):
    return dot(a, b, ((0,), (0,)))


def lanes(ref, head, width=HEAD_DIM):
    return ref[:, head * HEAD_DIM : head * HEAD_DIM + width]


MESH = pl.DeviceIdType.MESH
TILE = 4 * HEAD_DIM


class Gather:
    def __init__(self, me, place, bits, src, out, send, recv):
        self.me, self.bits, self.src, self.out = me, bits, src, out
        self.send, self.recv = send, recv
        self.rows = src.shape[0]
        self.quarter = -(-self.rows // 64) * 16
        self.most = self.rows - self.quarter
        units, parts = self.most // 16, len(bits)
        self.size = [16 * (units // parts + (i < units % parts)) for i in range(parts)]
        self.start = [sum(self.size[:i]) for i in range(parts)]
        self.odd = place % 2
        self.pair = place + 1 - 2 * self.odd
        self.count = 0
        self.waits = []
        own = {}
        for bit in bits:
            own[bit] = self.copy(self.src, 0, 1, self.most, bit, self.odd * self.quarter)
        self.own = own
        self.own_core = self.copy(self.src, 0, 0, self.rows, 1, 0)
        self.forwards = []
        self.arrival = {}
        for bit in bits:
            for i in range(len(bits)):
                self.arrival[(bit, i)] = own[bit]
        for step in range(1, len(bits)):
            for i in range(len(bits)):
                order = bits[i:] + bits[:i]
                bit = order[step]
                held = [0]
                for b in order[:step]:
                    held = held + [m | b for m in held]
                for m in held[1:]:
                    start = self.odd * self.quarter + self.start[i]
                    made = self.copy(out, m, 1, self.size[i], bit, start)
                    self.forwards.append((m, i, made))
                    self.arrival[(m | bit, i)] = made
        masks = list(range(2, 2 * max(bits), 2))
        self.masks = masks
        self.across = [
            self.copy(out, m, 2, self.quarter, 0, self.odd * self.most) for m in masks
        ]
        self.core = [self.copy(out, m, 1, self.rows, 1, 0) for m in masks]
        self.seen = set()

    def copy(self, ref, m, kind, rows, bit, start):
        at = (self.me ^ m) * self.rows + start
        source = ref.at[pl.ds(pl.multiple_of(start, 16), rows)] if ref is self.src else ref.at[pl.ds(pl.multiple_of(at, 16), rows)]
        target = {"seq": self.pair} if kind == 2 else {"dp": self.me ^ bit}
        index = self.count
        self.count += 1
        return pltpu.make_async_remote_copy(
            src_ref=source,
            dst_ref=self.out.at[pl.ds(pl.multiple_of(at, 16), rows)],
            send_sem=self.send.at[index],
            recv_sem=self.recv.at[index],
            device_id=target,
            device_id_type=MESH,
        )

    def begin(self):
        for bit in self.bits:
            self.own[bit].start()
        self.own_core.start()

    def arrived(self, copy):
        if id(copy) not in self.seen:
            self.seen.add(id(copy))
            copy.wait_recv()

    def forward(self):
        for m, i, made in self.forwards:
            self.arrived(self.arrival[(m, i)])
            made.start()

    def cross(self):
        for m, made in zip(self.masks, self.across):
            for i in range(len(self.bits)):
                self.arrived(self.arrival[(m, i)])
            made.start()

    def share(self):
        for across, made in zip(self.across, self.core):
            across.wait_recv()
            made.start()

    def finish(self):
        self.own_core.wait_recv()
        for made in self.core:
            made.wait_recv()

    def drain(self):
        for made in list(self.own.values()) + [self.own_core] + [f[2] for f in self.forwards] + self.across + self.core:
            made.wait_send()


def gather_copies(chip_bits):
    forwards = sum(chip_bits * (2**step - 1) for step in range(1, chip_bits))
    return chip_bits + 1 + forwards + 2 * (2**chip_bits - 1)


def forward_body(dp, seq, x_ref, gain_ref, cos_ref, first_ref, second_ref, *refs):
    w_in, refs = refs[:7], refs[7:]
    w_out, refs = refs[:7], refs[7:]
    qh, kh, vh, o_ref, lse_ref, n1_ref, gains_ref = refs[:7]
    stage, refs = refs[7:14], refs[14:]
    wq, wk, wv, kvbuf, gbuf, oh, send, recv, kv_send, kv_recv, g_send, g_recv, own_sem, load_sem = refs
    me, place = lax.axis_index("dp"), lax.axis_index("seq")
    bits = [1 << i for i in range(1, dp.bit_length() - 1)]
    tokens, model = x_ref.shape
    block = model // dp

    for i in range(7):
        pltpu.make_async_copy(w_in[i], stage[i], own_sem.at[i]).start()
    for r in range(1, seq):
        kvbuf[r] = jnp.zeros_like(kvbuf[r])

    barrier = pltpu.get_barrier_semaphore()
    for off in range(1, dp):
        pl.semaphore_signal(barrier, inc=1, device_id={"dp": me ^ off}, device_id_type=MESH)
    up, down = place + 1, place - 1
    odd = place % 2
    pair = place + 1 - 2 * odd
    other = place - 1 + 2 * odd
    has_other = (other >= 0) & (other < seq)
    pl.semaphore_signal(barrier, inc=1, device_id={"seq": pair}, device_id_type=MESH)

    @pl.when(has_other)
    def _():
        pl.semaphore_signal(barrier, inc=1, device_id={"seq": other}, device_id_type=MESH)

        pl.semaphore_wait(barrier, dp + 1)

    @pl.when(jnp.logical_not(has_other))
    def _():
        pl.semaphore_wait(barrier, dp)

    gains = [
        pltpu.make_async_remote_copy(
            src_ref=gain_ref,
            dst_ref=gbuf.at[me],
            send_sem=g_send.at[off],
            recv_sem=g_recv.at[off],
            device_id={"dp": me ^ off},
            device_id_type=MESH,
        )
        for off in range(1, dp)
    ]
    for g in gains:
        g.start()
    turned = bits[1:] + bits[:1]
    jobs = [
        Gather(me, place, turned if i in (1, 2, 5) else bits, w_in[i], w_out[i], send.at[i], recv.at[i])
        for i in range(7)
    ]
    first = jobs[:3]
    job_o, job_g, job_u, job_d = jobs[3:]
    for job in first:
        job.begin()

    def own_out(i):
        rows = w_in[i].shape[0]
        return pltpu.make_async_copy(stage[i], w_out[i].at[pl.ds(pl.multiple_of(me * rows, 8), rows)], own_sem.at[i])

    for i in range(7):
        pltpu.make_async_copy(w_in[i], stage[i], own_sem.at[i]).wait()
        own_out(i).start()

    gbuf[me] = gain_ref[...]
    x = x_ref[...].astype(F32)
    scale = lax.rsqrt(jnp.mean(x * x, axis=1, keepdims=True) + EPS)
    for g in gains:
        g.wait_recv()
    for k in range(dp):
        gains_ref[:, k * block : (k + 1) * block] = gbuf[k, :, :block]
    n1_ref[...] = (x * scale * gains_ref[0:1, :]).astype(BF)

    for job in first:
        job.forward()
    job_o.begin()
    job_g.begin()
    for job in first:
        job.cross()
    for job in first:
        job.share()
    for i in range(7):
        own_out(i).wait()
    for job in first:
        job.finish()
    loads = [
        pltpu.make_async_copy(w_out[i], ref, load_sem.at[i]) for i, ref in enumerate((wq, wk, wv))
    ]
    for load in loads:
        load.start()

    def turn(value):
        ahead = pltpu.roll(value, TILE - HEAD_DIM // 2, 1)
        behind = pltpu.roll(value, HEAD_DIM // 2, 1)
        return value * cos_ref[...] + behind * second_ref[...] - ahead * first_ref[...]

    kvd = wk.shape[1]
    loads[1].wait()

    @pl.loop(0, kvd // TILE)
    def _(t):
        at = pl.multiple_of(t * TILE, 128)
        kvbuf[0, :, pl.ds(at, TILE)] = turn(nn(n1_ref[...], wk[:, pl.ds(at, TILE)])).astype(BF)

    loads[2].wait()

    @pl.loop(0, kvd // TILE)
    def _(t):
        at = pl.multiple_of(t * TILE, 128)
        kvbuf[0, :, pl.ds(kvd + at, TILE)] = nn(n1_ref[...], wv[:, pl.ds(at, TILE)]).astype(BF)

    def kv_copy(r):
        return pltpu.make_async_remote_copy(
            src_ref=kvbuf.at[r],
            dst_ref=kvbuf.at[r + 1],
            send_sem=kv_send.at[r],
            recv_sem=kv_recv.at[r],
            device_id={"seq": up},
            device_id_type=MESH,
        )

    def kv_send_on(r):
        @pl.when((place >= r) & (place < seq - 1))
        def _():
            kv_copy(r).start()

    def kv_wait(r):
        @pl.when(place >= r)
        def _():
            pltpu.make_async_remote_copy(
                src_ref=kvbuf.at[r - 1],
                dst_ref=kvbuf.at[r],
                send_sem=kv_send.at[r - 1],
                recv_sem=kv_recv.at[r - 1],
                device_id={"seq": down},
                device_id_type=MESH,
            ).wait_recv()

    kv_send_on(0)
    loads[0].wait()

    @pl.loop(0, model // TILE)
    def _(t):
        at = pl.multiple_of(t * TILE, 128)
        q = turn(nn(n1_ref[...], wq[:, pl.ds(at, TILE)])).astype(BF)
        for i in range(TILE // HEAD_DIM):
            qh[t * (TILE // HEAD_DIM) + i] = q[:, i * HEAD_DIM : (i + 1) * HEAD_DIM]

    def split_heads(r):
        for g in range(KV_HEADS):
            kh[g, r * tokens : (r + 1) * tokens, :] = kvbuf[r, :, g * HEAD_DIM : (g + 1) * HEAD_DIM]
            vh[g, r * tokens : (r + 1) * tokens, :] = kvbuf[r, :, kvd + g * HEAD_DIM : kvd + (g + 1) * HEAD_DIM]

    job_o.forward()
    job_u.begin()
    split_heads(0)
    for r in range(1, seq):
        kv_wait(r)
        if r < seq - 1:
            kv_send_on(r)
        if r == 1:
            job_o.cross()
            job_g.forward()
            job_d.begin()
            job_o.share()
        split_heads(r)
    job_g.cross()

    row = lax.broadcasted_iota(jnp.int32, (tokens, tokens), 0)
    col = lax.broadcasted_iota(jnp.int32, (tokens, tokens), 1)
    lse_ref[...] = jnp.zeros_like(lse_ref)
    lane = lax.broadcasted_iota(jnp.int32, (tokens, 128), 1)

    half = HEADS // 2

    def attend_heads(start, stop):
        @pl.loop(start, stop)
        def _(h):
            g = h // GROUP
            q = qh[h]
            scores = []
            for r in range(seq):
                s = nt(q, kh[g, r * tokens : (r + 1) * tokens, :]) * SCALE
                scores.append(jnp.where(col <= row if r == 0 else place >= r, s, NEG))
            top = functools.reduce(jnp.maximum, [jnp.max(s, axis=1, keepdims=True) for s in scores])
            weights = [jnp.exp(s - top) for s in scores]
            total = sum(jnp.sum(w, axis=1, keepdims=True) for w in weights)
            inverse = 1.0 / total
            oh[h] = sum(
                nn((w * inverse).astype(BF), vh[g, r * tokens : (r + 1) * tokens, :])
                for r, w in enumerate(weights)
            ).astype(BF)
            lse_ref[...] += jnp.where(lane == h, top + jnp.log(total), 0.0)

    attend_heads(0, half)
    job_g.share()
    job_u.forward()
    attend_heads(half, HEADS)
    for h in range(HEADS):
        o_ref[:, h * HEAD_DIM : (h + 1) * HEAD_DIM] = oh[h]
    job_u.cross()
    job_d.forward()
    job_u.share()
    job_d.cross()
    job_d.share()
    for job in (job_o, job_g, job_u, job_d):
        job.finish()
    for r in range(seq - 1):

        @pl.when((place >= r) & (place < seq - 1))
        def _():
            kv_copy(r).wait_send()

    for g in gains:
        g.wait_send()
    for job in jobs:
        job.drain()


def forward_call(dp, seq, x, gains, tables, weights):
    tokens, model = x.shape
    chip_bits = dp.bit_length() - 2
    copies = gather_copies(chip_bits)
    anyspec = pl.BlockSpec(memory_space=pl.ANY)
    vmem = pl.BlockSpec(memory_space=pltpu.VMEM)
    out_shape = [jax.ShapeDtypeStruct((dp * w.shape[0], w.shape[1]), BF) for w in weights]
    heads = jax.ShapeDtypeStruct((HEADS, tokens, HEAD_DIM), BF)
    keys = jax.ShapeDtypeStruct((KV_HEADS, seq * tokens, HEAD_DIM), BF)
    out_shape += [
        heads,
        keys,
        keys,
        jax.ShapeDtypeStruct((tokens, model), BF),
        jax.ShapeDtypeStruct((tokens, 128), F32),
        jax.ShapeDtypeStruct((tokens, model), BF),
        jax.ShapeDtypeStruct((8, model), F32),
    ]
    kvd = weights[1].shape[1]
    dma = pltpu.SemaphoreType.DMA
    return pl.pallas_call(
        functools.partial(forward_body, dp, seq),
        out_shape=out_shape,
        in_specs=[vmem] * 5 + [anyspec] * 7,
        out_specs=[anyspec] * 7 + [vmem] * 7,
        scratch_shapes=[pltpu.VMEM(w.shape, BF) for w in weights]
        + [
            pltpu.VMEM((model, model), BF),
            pltpu.VMEM((model, kvd), BF),
            pltpu.VMEM((model, kvd), BF),
            pltpu.VMEM((seq, tokens, model), BF),
            pltpu.VMEM((dp, 8, 256), F32),
            pltpu.VMEM((HEADS, tokens, HEAD_DIM), BF),
            dma((7, copies)),
            dma((7, copies)),
            dma((seq,)),
            dma((seq,)),
            dma((dp,)),
            dma((dp,)),
            dma((7,)),
            dma((3,)),
        ],
        compiler_params=pltpu.CompilerParams(
            collective_id=0, has_side_effects=True, vmem_limit_bytes=60 * 1024 * 1024
        ),
        name="forward",
    )(x, gains, *tables, *weights)


def head_column(lse, h):
    lane = lax.broadcasted_iota(jnp.int32, lse.shape, 1)
    return jnp.sum(jnp.where(lane == h, lse, 0.0), axis=1, keepdims=True)


def back_group(place, chunks, g, q_ref, do_ref, lse, k, v, dq_ref, dk_ref, dv_ref, acc_k, acc_v):
    tokens = q_ref.shape[1]
    row = lax.broadcasted_iota(jnp.int32, (tokens, tokens), 0)
    col = lax.broadcasted_iota(jnp.int32, (tokens, tokens), 1)
    for i in range(GROUP):
        h = GROUP * g + i
        q, do = q_ref[h], do_ref[h]
        total = head_column(lse, h)
        probs, dprobs = [], []
        for r in range(chunks):
            span = slice(r * tokens, (r + 1) * tokens)
            s = nt(q, k[span, :]) * SCALE
            s = jnp.where(col <= row if r == 0 else place >= r, s, NEG)
            probs.append(jnp.exp(s - total))
            dprobs.append(nt(do, v[span, :]))
        inner = sum(jnp.sum(p * d, axis=1, keepdims=True) for p, d in zip(probs, dprobs))
        dq = jnp.zeros((tokens, HEAD_DIM), F32)
        for r in range(chunks):
            span = slice(r * tokens, (r + 1) * tokens)
            ds = (probs[r] * (dprobs[r] - inner)).astype(BF)
            dq += nn(ds, k[span, :])
            dk = tn(ds, q)
            dv = tn(probs[r].astype(BF), do)
            if i == 0:
                acc_k[span, :] = dk
                acc_v[span, :] = dv
            else:
                dk_ref[g, span, :] = ((acc_k[span, :] + dk) * SCALE).astype(BF)
                dv_ref[g, span, :] = (acc_v[span, :] + dv).astype(BF)
        dq_ref[h] = (dq * SCALE).astype(BF)


COLS = 512
LAG_B, LAG_C, LAG_D = 1, 3, 5
SLOTS_CORE, SLOTS, SLOTS_SUM, SLOTS_OUT = 2, 4, 10, 8


def backward_body(seq, x_ref, gains_ref, e2_ref, cos_ref, first_ref, second_ref, hidden_ref, eb_ref, lefts_ref,
                  qh, kh, vh, do_ref, lse_ref, gain2_ref, rights_in, wq_in, wk_in, wv_in, *refs):
    dx_ref, gain_out, res = refs[:3]
    (rights, doh, dqh, dkh, dvh, acc_k, acc_v, dkv, dkv_in, dn1, wt,
     cs, cr, sums, r0, r1, zs, zr, zt, gsend, grecv, gsum, gzrecv,
     load_sem, w_sem, core_s, core_r, s0_s, s0_r, s1_s, s1_r, z_s, z_r, a_s, a_r, t_sem, kv_s, kv_r,
     g_s, g_r, gz_s, gz_r, core_free, s0_free, s1_free, z_free) = refs[3:]
    me, place = lax.axis_index("dp"), lax.axis_index("seq")
    core, chip_x, chip_y = me % 2, (me // 2) % 2, me // 4
    tokens, model = x_ref.shape
    rows = model // 8
    sub = rows // seq
    kvd = wk_in.shape[1]
    d_rows = hidden_ref.shape[0] // 8
    d_chunks = d_rows * 3 // rows
    n_chunks = rights.shape[1] // COLS
    o_panels = model // COLS
    gu_panels = n_chunks - 3 * o_panels
    total_chunks = d_chunks + n_chunks

    def owner(x, y, c):
        return ((chip_y + y) % 2) * 4 + ((chip_x + x) % 2) * 2 + (core + c) % 2

    partner = owner(0, 0, 1)
    near = [[owner(1, 0, 0), owner(0, 1, 0)], [owner(0, 1, 0), owner(1, 0, 0)]]

    load = pltpu.make_async_copy(rights_in, rights.at[:, : rights_in.shape[1]], load_sem)
    load.start()

    barrier = pltpu.get_barrier_semaphore()
    for off in range(1, 8):
        pl.semaphore_signal(barrier, inc=1, device_id={"dp": me ^ off}, device_id_type=MESH)
    for far in range(1, seq):
        to = (place + far) % seq
        pl.semaphore_signal(barrier, inc=1, device_id={"seq": to}, device_id_type=MESH)
    pl.semaphore_wait(barrier, 7 + seq - 1)

    for h in range(HEADS):
        doh[h] = lanes(do_ref, h)
    load.wait()

    def remote(src, dst, send, recv, **target):
        return pltpu.make_async_remote_copy(
            src_ref=src, dst_ref=dst, send_sem=send, recv_sem=recv, device_id=target, device_id_type=MESH
        )

    def signal(sem, **target):
        pl.semaphore_signal(sem, inc=1, device_id=target, device_id_type=MESH)

    def core_copy(c):
        s = c % SLOTS_CORE
        return remote(cs.at[s], cr.at[s], core_s.at[s], core_r.at[s], dp=partner)

    def first_copy(c, parity):
        s = c % SLOTS
        return remote(sums.at[c % SLOTS_SUM, pl.ds(2 * rows, 2 * rows)], r0.at[s], s0_s.at[s], s0_r.at[s], dp=near[parity][0])

    def second_copy(c, parity):
        s = c % SLOTS
        return remote(sums.at[c % SLOTS_SUM, pl.ds(rows, rows)], r1.at[s], s1_s.at[s], s1_r.at[s], dp=near[parity][1])

    def offsets(index, parity):
        low, high = index % 2, index // 2
        return (high, low) if parity == 0 else (low, high)

    def stage_a(c, parity):
        s, t = c % SLOTS_CORE, c % SLOTS_SUM

        @pl.when(c >= SLOTS_CORE)
        def _():
            core_copy(c).wait_send()

        def put(away, term):
            @pl.loop(0, 4)
            def _(index):
                dx, dy = offsets(index, parity)
                at = pl.multiple_of(index * rows, 16)
                if away:
                    cs[s, pl.ds(at, rows), :] = term(owner(dx, dy, 1)).astype(BF)
                else:
                    sums[t, pl.ds(at, rows), :] = term(owner(dx, dy, 0)).astype(BF)

        def term_d(who):
            size = rows // 3
            at = pl.multiple_of(who * d_rows + c * size, 16)
            left = hidden_ref[pl.ds(at, size), :]
            return jnp.concatenate(
                [nn(left, eb_ref[:, i * COLS : (i + 1) * COLS]) for i in range(3)], axis=0
            )

        k = c - d_chunks
        which = (k >= gu_panels).astype(jnp.int32) + (k >= gu_panels + o_panels).astype(jnp.int32)

        def term_n(who):
            left = lefts_ref[pl.ds(pl.multiple_of(which * model + who * rows, 16), rows), :]
            return nn(left, rights[:, pl.ds(pl.multiple_of(k * COLS, 128), COLS)])

        def both(term):
            put(True, term)

            @pl.when(c >= SLOTS_CORE)
            def _():
                pl.semaphore_wait(core_free, 1)

            core_copy(c).start()
            put(False, term)

        @pl.when(c < d_chunks)
        def _():
            both(term_d)

        @pl.when(c >= d_chunks)
        def _():
            both(term_n)

    def add_rows(count, target, extra):
        @pl.loop(0, count // 64)
        def _(i):
            at = pl.multiple_of(i * 64, 16)
            target[pl.ds(at, 64), :] = (target[pl.ds(at, 64), :].astype(F32) + extra[pl.ds(at, 64), :].astype(F32)).astype(BF)

    def stage_b(c, parity):
        core_copy(c).wait_recv()
        add_rows(4 * rows, sums.at[c % SLOTS_SUM], cr.at[c % SLOTS_CORE])

        @pl.when(c < total_chunks - SLOTS_CORE)
        def _():
            signal(core_free, dp=partner)

        @pl.when(c >= SLOTS)
        def _():
            pl.semaphore_wait(s0_free.at[parity], 1)

        first_copy(c, parity).start()

    def stage_c(c, parity):
        first_copy(c, parity).wait_recv()
        add_rows(2 * rows, sums.at[c % SLOTS_SUM], r0.at[c % SLOTS])

        @pl.when(c < total_chunks - SLOTS)
        def _():
            signal(s0_free.at[parity], dp=near[parity][0])

        @pl.when(c >= SLOTS)
        def _():
            pl.semaphore_wait(s1_free.at[parity], 1)

        second_copy(c, parity).start()
        first_copy(c, parity).wait_send()

    def stage_d(c, parity):
        second_copy(c, parity).wait_recv()
        add_rows(rows, sums.at[c % SLOTS_SUM], r1.at[c % SLOTS])

        @pl.when(c < total_chunks - SLOTS)
        def _():
            signal(s1_free.at[parity], dp=near[parity][1])

        second_copy(c, parity).wait_send()

    def step_of(way):
        return 1 - 2 * way

    def inside(at):
        return (at >= 0) & (at < seq)

    def z_copy(c, way, hop):
        s = c % SLOTS
        slot = way * (seq - 1) + hop - 1
        return remote(zs.at[slot, s], zr.at[slot, s], z_s.at[slot, s], z_r.at[slot, s], seq=place + step_of(way))

    def z_sends(way, hop):
        return inside(place + step_of(way) * (seq - hop))

    def z_gets(way, hop):
        return inside(place - step_of(way)) & inside(place - step_of(way) + step_of(way) * (seq - hop))

    def part(c, index):
        index = jnp.minimum(jnp.maximum(index, 0), seq - 1)
        return sums[c % SLOTS_SUM, pl.ds(pl.multiple_of(index * sub, 16), sub), :].astype(F32)

    def z_take(c, way, hop):
        slot = way * (seq - 1) + hop - 1
        gets = z_gets(way, hop)

        @pl.when(gets)
        def _():
            z_copy(c, way, hop).wait_recv()

        return jnp.where(gets, zr[slot, c % SLOTS].astype(F32), 0.0)

    def z_release(c, way, hop):
        slot = way * (seq - 1) + hop - 1

        @pl.when(z_gets(way, hop) & (c < total_chunks - SLOTS))
        def _():
            signal(z_free.at[slot], seq=place - step_of(way))

    def stage_z(c, hop):
        for way in range(2):
            slot = way * (seq - 1) + hop - 1
            value = part(c, place + step_of(way) * (seq - hop))
            if hop > 1:
                value = value + z_take(c, way, hop - 1)
            sends = z_sends(way, hop)

            @pl.when(sends & (c >= SLOTS))
            def _():
                z_copy(c, way, hop).wait_send()

            zs[slot, c % SLOTS] = value.astype(BF)
            if hop > 1:
                z_release(c, way, hop - 1)

            @pl.when(sends & (c >= SLOTS))
            def _():
                pl.semaphore_wait(z_free.at[slot], 1)

            @pl.when(sends)
            def _():
                z_copy(c, way, hop).start()

    def res_at(c, source):
        index = jnp.minimum(jnp.maximum(source, 0), seq - 1)
        return res.at[pl.ds(pl.multiple_of(c * rows + index * sub, 16), sub)]

    def own_copy(c):
        s = c % SLOTS_OUT
        return pltpu.make_async_copy(zt.at[s], res_at(c, place), t_sem.at[s])

    def a_copy(c, way, hop):
        s = c % SLOTS_OUT
        slot = way * (seq - 1) + hop - 1
        source = place - step_of(way) * (hop - 1)
        src = zt.at[s] if hop == 1 else res_at(c, source)
        return remote(src, res_at(c, source), a_s.at[slot, s], a_r.at[slot, s], seq=place + step_of(way))

    def a_sends(way, hop):
        return inside(place + step_of(way)) & inside(place - step_of(way) * (hop - 1))

    def a_gets(way, hop):
        return inside(place - step_of(way) * hop)

    def stage_total(c):
        value = part(c, place)
        for way in range(2):
            value = value + z_take(c, way, seq - 1)

        @pl.when(c >= SLOTS_OUT)
        def _():
            own_copy(c).wait()

        for way in range(2):
            @pl.when((c >= SLOTS_OUT) & a_sends(way, 1))
            def _():
                a_copy(c, way, 1).wait_send()

        zt[c % SLOTS_OUT] = value.astype(BF)
        for way in range(2):
            z_release(c, way, seq - 1)
        own_copy(c).start()
        stage_out(c, 1)

    def stage_out(c, hop):
        for way in range(2):
            if hop > 1:
                @pl.when(a_gets(way, hop - 1))
                def _():
                    a_copy(c, way, hop - 1).wait_recv()

            if hop < seq:
                if hop > 1:
                    @pl.when((c >= SLOTS_OUT) & a_sends(way, hop))
                    def _():
                        a_copy(c, way, hop).wait_send()

                @pl.when(a_sends(way, hop))
                def _():
                    a_copy(c, way, hop).start()

    lag_total = LAG_D + seq - 1
    stages = [(LAG_B, stage_b), (LAG_C, stage_c), (LAG_D, stage_d), (LAG_D, lambda c, parity: stage_z(c, 1))]
    stages += [(LAG_D + hop - 1, lambda c, parity, hop=hop: stage_z(c, hop)) for hop in range(2, seq)]
    stages += [(lag_total, lambda c, parity: stage_total(c))]
    stages += [(lag_total + hop - 1, lambda c, parity, hop=hop: stage_out(c, hop)) for hop in range(2, seq + 1)]
    last_lag = lag_total + seq - 1

    def tick(c, parity):
        for lag, stage in sorted(stages, key=lambda pair: -pair[0]):
            then = c - lag

            @pl.when((then >= 0) & (then < total_chunks))
            def _():
                stage(then, (parity + lag) % 2)

        @pl.when(c < total_chunks)
        def _():
            stage_a(c, parity)

    def kv_copy(r):
        return remote(dkv.at[r], dkv_in.at[r - 1], kv_s.at[r], kv_r.at[r], seq=place - 1)

    def kv_send(r):
        @pl.when(place >= r)
        def _():
            kv_copy(r).start()

    def kv_take(r):
        gets = (place + 1 >= r) & (place + 1 < seq)

        @pl.when(gets)
        def _():
            kv_copy(r).wait_recv()
            add_rows(tokens, dkv.at[r - 1], dkv_in.at[r - 1])

    def turn_back(value):
        ahead = pltpu.roll(value, TILE - HEAD_DIM // 2, 1)
        behind = pltpu.roll(value, HEAD_DIM // 2, 1)
        return (value * cos_ref[...] - behind * second_ref[...] + ahead * first_ref[...]).astype(BF)

    q_at = (gu_panels + o_panels) * COLS

    def w_load(t, i):
        at = pl.multiple_of(t * TILE, 16)
        s = t % 2
        src, lo, width = ((wq_in, 0, model), (wk_in, model, kvd), (wv_in, model + kvd, kvd))[i]
        return pltpu.make_async_copy(src.at[pl.ds(at, TILE)], wt.at[s, :, pl.ds(lo, width)], w_sem.at[s, i])

    def last_norm():
        for h in range(HEADS):
            rights[:, q_at + h * HEAD_DIM : q_at + (h + 1) * HEAD_DIM] = dqh[h]
        for t in range(model // TILE):
            at = q_at + t * TILE
            rights[:, at : at + TILE] = turn_back(rights[:, at : at + TILE].astype(F32))
        for t in range(kvd // TILE):
            at = q_at + model + t * TILE
            rights[:, at : at + TILE] = turn_back(dkv[0, :, t * TILE : (t + 1) * TILE].astype(F32))
        rights[:, q_at + model + kvd :] = dkv[0, :, kvd:]
        for i in range(3):
            w_load(0, i).start()

        @pl.loop(0, model // TILE)
        def _(t):
            for i in range(3):
                w_load(t, i).wait()

            @pl.when(t + 1 < model // TILE)
            def _():
                for i in range(3):
                    w_load(t + 1, i).start()

            dn1[:, pl.ds(pl.multiple_of(t * TILE, 128), TILE)] = nt(rights[:, q_at:], wt[t % 2])

        x = x_ref[...].astype(F32)
        scale = lax.rsqrt(jnp.mean(x * x, axis=1, keepdims=True) + EPS)
        unit = x * scale
        grad = dn1[...]
        term = jnp.sum(grad * unit, axis=0, keepdims=True)
        scaled = grad * gains_ref[0:1, :]
        inner = jnp.mean(scaled * unit, axis=1, keepdims=True)
        dx_ref[...] = e2_ref[...] + scale * (scaled - unit * inner)
        for k in range(8):
            gsend[k, 0:1, :rows] = term[:, k * rows : (k + 1) * rows]
            gsend[k, 1:2, :rows] = gain2_ref[0:1, k * rows : (k + 1) * rows]

    def gain_copies():
        return [
            remote(gsend.at[me ^ off], grecv.at[me], g_s.at[off], g_r.at[off], dp=me ^ off) for off in range(1, 8)
        ]

    def gain_line():
        return [
            remote(gsum, gzrecv.at[place], gz_s.at[far], gz_r.at[far], seq=(place + far) % seq) for far in range(1, seq)
        ]

    ticks = total_chunks + last_lag
    d_pairs = KV_HEADS // 2

    @pl.loop(0, -(-ticks // 2))
    def _(p):
        for parity in range(2):
            tick(2 * p + parity, parity)

        @pl.when(p < d_pairs)
        def _():
            for i in range(2):
                g = 2 * p + i
                back_group(place, seq, g, qh, doh, lse_ref[...], kh.at[g], vh.at[g], dqh, dkh, dvh, acc_k, acc_v)

        @pl.when(p == d_pairs - 1)
        def _():
            for r in range(seq):
                for g in range(KV_HEADS):
                    lo = g * HEAD_DIM
                    dkv[r, :, lo : lo + HEAD_DIM] = dkh[g, r * tokens : (r + 1) * tokens, :]
                    dkv[r, :, kvd + lo : kvd + lo + HEAD_DIM] = dvh[g, r * tokens : (r + 1) * tokens, :]
            kv_send(seq - 1)

        for r in range(seq - 1, 0, -1):
            @pl.when(p == d_pairs - 1 + 2 * (seq - r))
            def _():
                kv_take(r)
                if r > 1:
                    kv_send(r - 1)
                else:
                    last_norm()
                    for made in gain_copies():
                        made.start()
                    grecv[me] = gsend[me]

        @pl.when(p == d_pairs + 2 * seq - 2)
        def _():
            for made in gain_copies():
                made.wait_recv()
            gsum[...] = sum(grecv[k] for k in range(1, 8)) + grecv[0]
            gzrecv[place] = gsum[...]
            for made in gain_line():
                made.start()

        @pl.when(p == d_pairs + 2 * seq - 1)
        def _():
            for made in gain_line():
                made.wait_recv()
            gain_out[...] = sum(gzrecv[k] for k in range(seq))

    for made in gain_copies() + gain_line():
        made.wait_send()
    for r in range(1, seq):
        @pl.when(place >= r)
        def _():
            kv_copy(r).wait_send()
    for c in range(total_chunks - SLOTS_CORE, total_chunks):
        core_copy(c).wait_send()
    for way in range(2):
        for hop in range(1, seq):
            for c in range(total_chunks - SLOTS, total_chunks):
                @pl.when(z_sends(way, hop))
                def _():
                    z_copy(c, way, hop).wait_send()
            for c in range(total_chunks - SLOTS_OUT, total_chunks):
                @pl.when(a_sends(way, hop))
                def _():
                    a_copy(c, way, hop).wait_send()
    for c in range(total_chunks - SLOTS_OUT, total_chunks):
        own_copy(c).wait()


def backward_call(seq, x, gains, e2, tables, hidden_t, eb, lefts, qh, kh, vh, do, lse, gain2, rights, w_q, w_k, w_v):
    tokens, model = x.shape
    rows = model // 8
    sub = rows // seq
    kvd = w_k.shape[1]
    wide = rights.shape[1] + model + 2 * kvd
    chunks = hidden_t.shape[0] // 8 * 3 // rows + wide // COLS
    anyspec = pl.BlockSpec(memory_space=pl.ANY)
    vmem = pl.BlockSpec(memory_space=pltpu.VMEM)
    dma, regular = pltpu.SemaphoreType.DMA, pltpu.SemaphoreType.REGULAR
    hops = 2 * (seq - 1)
    heads = pltpu.VMEM((HEADS, tokens, HEAD_DIM), BF)
    keys = pltpu.VMEM((KV_HEADS, seq * tokens, HEAD_DIM), BF)
    return pl.pallas_call(
        functools.partial(backward_body, seq),
        out_shape=[
            jax.ShapeDtypeStruct((tokens, model), F32),
            jax.ShapeDtypeStruct((8, 256), F32),
            jax.ShapeDtypeStruct((chunks * rows, COLS), BF),
        ],
        in_specs=[vmem] * 15 + [anyspec] * 4,
        out_specs=[vmem, vmem, anyspec],
        scratch_shapes=[
            pltpu.VMEM((tokens, wide), BF),
            heads, heads, keys, keys,
            pltpu.VMEM((seq * tokens, HEAD_DIM), F32),
            pltpu.VMEM((seq * tokens, HEAD_DIM), F32),
            pltpu.VMEM((seq, tokens, model), BF),
            pltpu.VMEM((seq - 1, tokens, model), BF),
            pltpu.VMEM((tokens, model), F32),
            pltpu.VMEM((2, TILE, model + 2 * kvd), BF),
            pltpu.VMEM((SLOTS_CORE, 4 * rows, COLS), BF),
            pltpu.VMEM((SLOTS_CORE, 4 * rows, COLS), BF),
            pltpu.VMEM((SLOTS_SUM, 4 * rows, COLS), BF),
            pltpu.VMEM((SLOTS, 2 * rows, COLS), BF),
            pltpu.VMEM((SLOTS, rows, COLS), BF),
            pltpu.VMEM((hops, SLOTS, sub, COLS), BF),
            pltpu.VMEM((hops, SLOTS, sub, COLS), BF),
            pltpu.VMEM((SLOTS_OUT, sub, COLS), BF),
            pltpu.VMEM((8, 8, 256), F32),
            pltpu.VMEM((8, 8, 256), F32),
            pltpu.VMEM((8, 256), F32),
            pltpu.VMEM((seq, 8, 256), F32),
            dma(()), dma((2, 3)),
            dma((SLOTS_CORE,)), dma((SLOTS_CORE,)),
            dma((SLOTS,)), dma((SLOTS,)),
            dma((SLOTS,)), dma((SLOTS,)),
            dma((hops, SLOTS)), dma((hops, SLOTS)),
            dma((hops, SLOTS_OUT)), dma((hops, SLOTS_OUT)),
            dma((SLOTS_OUT,)),
            dma((seq,)), dma((seq,)),
            dma((8,)), dma((8,)),
            dma((seq,)), dma((seq,)),
            regular, regular((2,)), regular((2,)), regular((hops,)),
        ],
        compiler_params=pltpu.CompilerParams(
            collective_id=1, has_side_effects=True, vmem_limit_bytes=62 * 1024 * 1024
        ),
        name="backward",
    )(x, gains, e2, *tables, hidden_t, eb, lefts, qh, kh, vh, do, lse, gain2, rights, w_q, w_k, w_v)


def attend_back(place, qh, kh, vh, doh, lse):
    chunks = kh.shape[1] // qh.shape[1]

    def body(place_ref, q_ref, k_ref, v_ref, do_ref, lse_ref, dq_ref, dk_ref, dv_ref, acc_k, acc_v):
        @pl.loop(0, KV_HEADS)
        def _(g):
            back_group(place_ref[0], chunks, g, q_ref, do_ref, lse_ref[...], k_ref.at[g], v_ref.at[g], dq_ref, dk_ref, dv_ref, acc_k, acc_v)

    vmem = pl.BlockSpec(memory_space=pltpu.VMEM)
    acc = pltpu.VMEM(kh.shape[1:], F32)
    return pl.pallas_call(
        body,
        in_specs=[pl.BlockSpec(memory_space=pltpu.SMEM)] + [vmem] * 5,
        out_specs=[vmem] * 3,
        out_shape=[jax.ShapeDtypeStruct(a.shape, BF) for a in (qh, kh, vh)],
        scratch_shapes=[acc, acc],
        name="attend_back",
    )(place, qh, kh, vh, doh, lse)


def flip(value, axis, bit):
    size = lax.axis_size(axis)
    return lax.ppermute(value, axis, [(i, i ^ bit) for i in range(size)])


def xor_order(bits):
    order = [0]
    for bit in list(reversed(bits)) + [1]:
        order = order + [off ^ bit for off in order]
    return order


def scatter_term(left, right, bits):
    half = left.shape[1] // 2
    away = tn(left[:, half:], right).astype(BF)
    came = flip(away, "dp", 1)
    quarter = half // 2
    away = (tn(left[:, quarter:half], right) + came[quarter:]).astype(BF)
    kept = (tn(left[:, :quarter], right) + came[:quarter]).astype(BF)
    came = flip(away, "dp", bits[0])
    for bit in bits[1:]:
        size = kept.shape[0] // 2
        away = (kept[size:].astype(F32) + came[size:]).astype(BF)
        kept = (kept[:size].astype(F32) + came[:size]).astype(BF)
        came = flip(away, "dp", bit)
    return (kept.astype(F32) + came).astype(BF)


def line_sum(value, place):
    size = lax.axis_size("seq")
    rows = value.shape[0] // size

    def chunk(index):
        index = jnp.clip(index, 0, size - 1)
        return lax.dynamic_slice_in_dim(value, index * rows, rows, 0)

    total = chunk(place).astype(F32)
    for way in (1, -1):
        held = None
        for far in range(size - 1, 0, -1):
            mine = chunk(place + way * far)
            if held is not None:
                mine = (mine.astype(F32) + held).astype(BF)
            pairs = [(i, i + way) for i in range(size) if 0 <= i + way * far < size]
            held = lax.ppermute(mine, "seq", pairs)
        total = total + held
    total = total.astype(BF)
    out = jnp.zeros(value.shape, F32)
    out = lax.dynamic_update_slice(out, total.astype(F32), (place * rows, 0))
    for way in (1, -1):
        held = total
        for far in range(1, size):
            pairs = [
                (i, i + way) for i in range(size) if 0 <= i + way < size and 0 <= i - way * (far - 1) < size
            ]
            held = lax.ppermute(held, "seq", pairs)
            source = place - way * far
            index = jnp.clip(source, 0, size - 1) * rows
            old = lax.dynamic_slice(out, (index, 0), held.shape)
            good = (source >= 0) & (source < size)
            out = lax.dynamic_update_slice(
                out, jnp.where(good, held.astype(F32), old), (index, 0)
            )
    return out


def rope_tables(place, tokens, width):
    half = HEAD_DIM // 2
    positions = (place * tokens + jnp.arange(tokens, dtype=jnp.int32)).astype(F32)
    frequency = ROPE_BASE ** (-jnp.arange(half).astype(F32) / half)
    angles = positions[:, None] * frequency[None, :]
    cos, sin = jnp.cos(angles), jnp.sin(angles)
    zero = jnp.zeros_like(sin)
    heads = width // HEAD_DIM
    tile = lambda a, b: jnp.tile(jnp.concatenate([a, b], axis=1), (1, heads))
    return tile(cos, cos), tile(sin, zero), tile(zero, sin)


def rotate(field, tables, sign):
    cos, first, second = tables
    half = HEAD_DIM // 2
    width = field.shape[1]
    cos, first, second = cos[:, :width], first[:, :width], second[:, :width]
    ahead = jnp.concatenate([field[:, half:], field[:, :half]], axis=1)
    behind = jnp.concatenate([field[:, -half:], field[:, :-half]], axis=1)
    return field * cos + sign * (behind * second - ahead * first)


def norm_scale(values):
    return lax.rsqrt(jnp.mean(values * values, axis=-1, keepdims=True) + EPS)


def norm_back(values, scale, gain, grad):
    unit = values * scale
    grad_gain = jnp.sum(grad * unit, axis=0)
    scaled = grad * gain
    inner = jnp.mean(scaled * unit, axis=-1, keepdims=True)
    return scale * (scaled - unit * inner), grad_gain


def local(tokens, cotangent, w_query, w_key, w_value, w_out, w_gate, w_up, w_down, gain_attn, gain_mlp):
    dp, seq = lax.axis_size("dp"), lax.axis_size("seq")
    me, place = lax.axis_index("dp"), lax.axis_index("seq")
    bits = [1 << i for i in range(1, dp.bit_length() - 1)]
    turned = bits[1:] + bits[:1]
    model = tokens.shape[-1]
    rows = tokens.shape[1]
    kvd = w_key.shape[-1]
    place_arr = place.reshape(1).astype(jnp.int32)

    half_model = model // 2

    def xor_columns(value, way):
        width = value.shape[1] // dp
        cut = lambda off: lax.dynamic_slice_in_dim(value, (me ^ off) * width, width, 1)
        return jnp.concatenate([cut(off) for off in xor_order(way)], axis=1)

    tables = rope_tables(place, rows, model)
    x = tokens[0].astype(F32)
    packed = jnp.zeros((8, 256), F32)
    packed = packed.at[0, : gain_attn.shape[1]].set(gain_attn[0].astype(F32))
    packed = packed.at[1, : gain_mlp.shape[1]].set(gain_mlp[0].astype(F32))
    shards = [w[0] for w in (w_query, w_key, w_value, w_out, w_gate, w_up, w_down)]
    outs = forward_call(dp, seq, tokens[0], packed, [t[:, :TILE] for t in tables], shards)
    w_q, w_k, w_v, w_o, w_g, w_u, w_d = outs[:7]
    qh, kh, vh, mixed, lse, n1, gains = outs[7:]
    gain_one, gain_two = gains[0:1], gains[1:2]
    scale_one = norm_scale(x)
    x2 = x + nn(mixed, w_o)
    scale_two = norm_scale(x2)
    n2 = (x2 * scale_two * gain_two).astype(BF)
    gate = nn(n2, w_g)
    up = nn(n2, w_u)
    sig = jax.nn.sigmoid(gate)
    hidden = (gate * sig * up).astype(BF)
    result = x2 + nn(hidden, w_d)

    e = cotangent[0].astype(F32)
    eb = cotangent[0]
    dh = nt(eb, w_d)
    dgate = (dh * up * sig * (1.0 + gate * (1.0 - sig))).astype(BF)
    dup = (dh * gate * sig).astype(BF)
    dn2 = nt(dgate, w_g) + nt(dup, w_u)
    dx2, term_gain_two = norm_back(x2, scale_two, gain_two, dn2)
    e2 = e + dx2
    e2b = e2.astype(BF)
    do = nt(e2b, w_o).astype(BF)
    if len(bits) == 2 and (model // dp) % (16 * seq) == 0:
        lefts = jnp.concatenate([n2.T, mixed.T, n1.T], axis=0)
        rights = jnp.concatenate([dgate, dup, e2b], axis=1)
        dx, grads, res = backward_call(
            seq, tokens[0], gains, e2, [t[:, :TILE] for t in tables], hidden.T, eb, lefts,
            qh, kh, vh, do, lse, term_gain_two[None], rights, w_q, w_k, w_v,
        )
        block = model // dp
        res = res.reshape(-1, block, COLS)
        n_down = w_down.shape[1] * 3 // block
        n_ff, n_model = w_gate.shape[2] // COLS, model // COLS

        def columns(lo, count):
            return res[lo : lo + count].transpose(1, 0, 2).reshape(block, count * COLS).astype(F32)

        down = res[:n_down].reshape(n_down, 3, block // 3, COLS).transpose(0, 2, 1, 3)
        at = n_down + 2 * n_ff
        attn = columns(at + n_model, 2 * n_model)
        return (
            result[None],
            dx[None],
            attn[None, :, :model],
            attn[None, :, model : model + kvd],
            attn[None, :, model + kvd :],
            columns(at, n_model)[None],
            columns(n_down, n_ff)[None],
            columns(n_down + n_ff, n_ff)[None],
            down.reshape(1, w_down.shape[1], model).astype(F32),
            grads[0:1, :block],
            grads[1:2, :block],
        )

    hidden_a = xor_columns(hidden, bits)
    hidden_b = xor_columns(hidden, turned)
    sum_down = jnp.concatenate(
        [
            scatter_term(hidden_a, eb[:, :half_model], bits),
            scatter_term(hidden_b, eb[:, half_model:], turned),
        ],
        axis=1,
    )
    n2_a, n2_b = xor_columns(n2, bits), xor_columns(n2, turned)
    sum_gate = scatter_term(n2_a, dgate, bits)
    sum_up = scatter_term(n2_b, dup, turned)
    mixed_a, mixed_b = xor_columns(mixed, bits), xor_columns(mixed, turned)
    sum_out = jnp.concatenate(
        [
            scatter_term(mixed_a, e2b[:, :half_model], bits),
            scatter_term(mixed_b, e2b[:, half_model:], turned),
        ],
        axis=1,
    )
    doh = do.reshape(rows, HEADS, HEAD_DIM).transpose(1, 0, 2)
    dqh, dkh, dvh = attend_back(place_arr, qh, kh, vh, doh, lse)
    dq = dqh.transpose(1, 0, 2).reshape(rows, model)
    dks, dvs = (a.reshape(KV_HEADS, seq, rows, HEAD_DIM).transpose(1, 2, 0, 3).reshape(seq, rows, kvd) for a in (dkh, dvh))
    held = None
    for far in range(seq - 1, -1, -1):
        mine = jnp.concatenate([dks[far], dvs[far]], axis=1)
        if held is not None:
            mine = (mine.astype(F32) + held).astype(BF)
        if far:
            held = lax.ppermute(mine, "seq", [(i, i - 1) for i in range(far, seq)])
    dk, dv = mine[:, :kvd], mine[:, kvd:]
    dqp = rotate(dq.astype(F32), tables, -1.0).astype(BF)
    dkp = rotate(dk.astype(F32), tables, -1.0).astype(BF)
    n1_a, n1_b = xor_columns(n1, bits), xor_columns(n1, turned)
    sum_query = scatter_term(n1_a, dqp, bits)
    sum_kv = scatter_term(n1_b, jnp.concatenate([dkp, dv], axis=1), turned)
    dn1 = nt(dqp, w_q) + nt(dkp, w_k) + nt(dv, w_v)
    dx1, term_gain_one = norm_back(x, scale_one, gain_one, dn1)
    input_grad = e2 + dx1

    both = jnp.stack([term_gain_one, term_gain_two])
    for bit in [1] + bits:
        both = both + flip(both, "dp", bit)
    for bit in [1 << i for i in range(seq.bit_length() - 1)]:
        both = both + flip(both, "seq", bit)
    width = model // dp
    both = lax.dynamic_slice_in_dim(both, me * width, width, 1)

    g_down = line_sum(sum_down, place)
    g_gate = line_sum(sum_gate, place)
    g_up = line_sum(sum_up, place)
    g_out = line_sum(sum_out, place)
    g_query = line_sum(sum_query, place)
    g_kv = line_sum(sum_kv, place)
    return (
        result[None],
        input_grad[None],
        g_query[None],
        g_kv[None, :, :kvd],
        g_kv[None, :, kvd:],
        g_out[None],
        g_gate[None],
        g_up[None],
        g_down[None],
        both[0:1],
        both[1:2],
    )


def solution(mesh):
    by_token = P("dp", "seq", None)
    by_row = P(None, "dp", None)
    by_gain = P(None, "dp")
    in_specs = (by_token,) * 2 + (by_row,) * 7 + (by_gain,) * 2
    return jax.shard_map(local, mesh=mesh, in_specs=in_specs, out_specs=in_specs, check_vma=False)
```

```python
import functools

import jax
import jax.numpy as jnp
from jax import lax
from jax.experimental import pallas as pl
from jax.experimental.pallas import tpu as pltpu
from jax.sharding import PartitionSpec as P

HEADS = 16
KV_HEADS = 8
HEAD_DIM = 96
GROUP = HEADS // KV_HEADS
EPS = 1e-05
ROPE_BASE = 100000.0
BF = jnp.bfloat16
F32 = jnp.float32
NEG = -1e30
SCALE = HEAD_DIM ** (-0.5)


def dot(a, b, dims):
    return lax.dot_general(a, b, (dims, ((), ())), preferred_element_type=F32)


def nn(a, b):
    return dot(a, b, ((1,), (0,)))


def nt(a, b):
    return dot(a, b, ((1,), (1,)))


def tn(a, b):
    return dot(a, b, ((0,), (0,)))


def lanes(ref, head, width=HEAD_DIM):
    return ref[:, head * HEAD_DIM : head * HEAD_DIM + width]


MESH = pl.DeviceIdType.MESH
TILE = 4 * HEAD_DIM


class Gather:
    def __init__(self, me, place, bits, src, out, send, recv):
        self.me, self.bits, self.src, self.out = me, bits, src, out
        self.send, self.recv = send, recv
        self.rows = src.shape[0]
        self.quarter = -(-self.rows // 64) * 16
        self.most = self.rows - self.quarter
        units, parts = self.most // 16, len(bits)
        self.size = [16 * (units // parts + (i < units % parts)) for i in range(parts)]
        self.start = [sum(self.size[:i]) for i in range(parts)]
        self.odd = place % 2
        self.pair = place + 1 - 2 * self.odd
        self.count = 0
        self.waits = []
        own = {}
        for bit in bits:
            own[bit] = self.copy(self.src, 0, 1, self.most, bit, self.odd * self.quarter)
        self.own = own
        self.own_core = self.copy(self.src, 0, 0, self.rows, 1, 0)
        self.forwards = []
        self.arrival = {}
        for bit in bits:
            for i in range(len(bits)):
                self.arrival[(bit, i)] = own[bit]
        for step in range(1, len(bits)):
            for i in range(len(bits)):
                order = bits[i:] + bits[:i]
                bit = order[step]
                held = [0]
                for b in order[:step]:
                    held = held + [m | b for m in held]
                for m in held[1:]:
                    start = self.odd * self.quarter + self.start[i]
                    made = self.copy(out, m, 1, self.size[i], bit, start)
                    self.forwards.append((m, i, made))
                    self.arrival[(m | bit, i)] = made
        masks = list(range(2, 2 * max(bits), 2))
        self.masks = masks
        self.across = [
            self.copy(out, m, 2, self.quarter, 0, self.odd * self.most) for m in masks
        ]
        self.core = [self.copy(out, m, 1, self.rows, 1, 0) for m in masks]
        self.seen = set()

    def copy(self, ref, m, kind, rows, bit, start):
        at = (self.me ^ m) * self.rows + start
        source = ref.at[pl.ds(pl.multiple_of(start, 16), rows)] if ref is self.src else ref.at[pl.ds(pl.multiple_of(at, 16), rows)]
        target = {"seq": self.pair} if kind == 2 else {"dp": self.me ^ bit}
        index = self.count
        self.count += 1
        return pltpu.make_async_remote_copy(
            src_ref=source,
            dst_ref=self.out.at[pl.ds(pl.multiple_of(at, 16), rows)],
            send_sem=self.send.at[index],
            recv_sem=self.recv.at[index],
            device_id=target,
            device_id_type=MESH,
        )

    def begin(self):
        for bit in self.bits:
            self.own[bit].start()
        self.own_core.start()

    def arrived(self, copy):
        if id(copy) not in self.seen:
            self.seen.add(id(copy))
            copy.wait_recv()

    def forward(self):
        for m, i, made in self.forwards:
            self.arrived(self.arrival[(m, i)])
            made.start()

    def cross(self):
        for m, made in zip(self.masks, self.across):
            for i in range(len(self.bits)):
                self.arrived(self.arrival[(m, i)])
            made.start()

    def share(self):
        for across, made in zip(self.across, self.core):
            across.wait_recv()
            made.start()

    def finish(self):
        self.own_core.wait_recv()
        for made in self.core:
            made.wait_recv()

    def drain(self):
        for made in list(self.own.values()) + [self.own_core] + [f[2] for f in self.forwards] + self.across + self.core:
            made.wait_send()


def gather_copies(chip_bits):
    forwards = sum(chip_bits * (2**step - 1) for step in range(1, chip_bits))
    return chip_bits + 1 + forwards + 2 * (2**chip_bits - 1)


def forward_body(dp, seq, x_ref, gain_ref, cos_ref, first_ref, second_ref, *refs):
    w_in, refs = refs[:7], refs[7:]
    w_out, refs = refs[:7], refs[7:]
    qh, kh, vh, o_ref, lse_ref, n1_ref, gains_ref = refs[:7]
    stage, refs = refs[7:14], refs[14:]
    wq, wk, wv, kvbuf, gbuf, oh, send, recv, kv_send, kv_recv, g_send, g_recv, own_sem, load_sem = refs
    me, place = lax.axis_index("dp"), lax.axis_index("seq")
    bits = [1 << i for i in range(1, dp.bit_length() - 1)]
    tokens, model = x_ref.shape
    block = model // dp

    for i in range(7):
        pltpu.make_async_copy(w_in[i], stage[i], own_sem.at[i]).start()
    for r in range(1, seq):
        kvbuf[r] = jnp.zeros_like(kvbuf[r])

    barrier = pltpu.get_barrier_semaphore()
    for off in range(1, dp):
        pl.semaphore_signal(barrier, inc=1, device_id={"dp": me ^ off}, device_id_type=MESH)
    up, down = place + 1, place - 1
    odd = place % 2
    pair = place + 1 - 2 * odd
    other = place - 1 + 2 * odd
    has_other = (other >= 0) & (other < seq)
    pl.semaphore_signal(barrier, inc=1, device_id={"seq": pair}, device_id_type=MESH)

    @pl.when(has_other)
    def _():
        pl.semaphore_signal(barrier, inc=1, device_id={"seq": other}, device_id_type=MESH)

        pl.semaphore_wait(barrier, dp + 1)

    @pl.when(jnp.logical_not(has_other))
    def _():
        pl.semaphore_wait(barrier, dp)

    gains = [
        pltpu.make_async_remote_copy(
            src_ref=gain_ref,
            dst_ref=gbuf.at[me],
            send_sem=g_send.at[off],
            recv_sem=g_recv.at[off],
            device_id={"dp": me ^ off},
            device_id_type=MESH,
        )
        for off in range(1, dp)
    ]
    for g in gains:
        g.start()
    turned = bits[1:] + bits[:1]
    jobs = [
        Gather(me, place, turned if i in (1, 2, 5) else bits, w_in[i], w_out[i], send.at[i], recv.at[i])
        for i in range(7)
    ]
    first = jobs[:3]
    job_o, job_g, job_u, job_d = jobs[3:]
    for job in first:
        job.begin()

    def own_out(i):
        rows = w_in[i].shape[0]
        return pltpu.make_async_copy(stage[i], w_out[i].at[pl.ds(pl.multiple_of(me * rows, 8), rows)], own_sem.at[i])

    for i in range(7):
        pltpu.make_async_copy(w_in[i], stage[i], own_sem.at[i]).wait()
        own_out(i).start()

    gbuf[me] = gain_ref[...]
    x = x_ref[...].astype(F32)
    scale = lax.rsqrt(jnp.mean(x * x, axis=1, keepdims=True) + EPS)
    for g in gains:
        g.wait_recv()
    for k in range(dp):
        gains_ref[:, k * block : (k + 1) * block] = gbuf[k, :, :block]
    n1_ref[...] = (x * scale * gains_ref[0:1, :]).astype(BF)

    for job in first:
        job.forward()
    job_o.begin()
    job_g.begin()
    for job in first:
        job.cross()
    for job in first:
        job.share()
    for i in range(7):
        own_out(i).wait()
    for job in first:
        job.finish()
    loads = [
        pltpu.make_async_copy(w_out[i], ref, load_sem.at[i]) for i, ref in enumerate((wq, wk, wv))
    ]
    for load in loads:
        load.start()

    def turn(value):
        ahead = pltpu.roll(value, TILE - HEAD_DIM // 2, 1)
        behind = pltpu.roll(value, HEAD_DIM // 2, 1)
        return value * cos_ref[...] + behind * second_ref[...] - ahead * first_ref[...]

    kvd = wk.shape[1]
    loads[1].wait()

    @pl.loop(0, kvd // TILE)
    def _(t):
        at = pl.multiple_of(t * TILE, 128)
        kvbuf[0, :, pl.ds(at, TILE)] = turn(nn(n1_ref[...], wk[:, pl.ds(at, TILE)])).astype(BF)

    loads[2].wait()

    @pl.loop(0, kvd // TILE)
    def _(t):
        at = pl.multiple_of(t * TILE, 128)
        kvbuf[0, :, pl.ds(kvd + at, TILE)] = nn(n1_ref[...], wv[:, pl.ds(at, TILE)]).astype(BF)

    def kv_copy(r):
        return pltpu.make_async_remote_copy(
            src_ref=kvbuf.at[r],
            dst_ref=kvbuf.at[r + 1],
            send_sem=kv_send.at[r],
            recv_sem=kv_recv.at[r],
            device_id={"seq": up},
            device_id_type=MESH,
        )

    def kv_send_on(r):
        @pl.when((place >= r) & (place < seq - 1))
        def _():
            kv_copy(r).start()

    def kv_wait(r):
        @pl.when(place >= r)
        def _():
            pltpu.make_async_remote_copy(
                src_ref=kvbuf.at[r - 1],
                dst_ref=kvbuf.at[r],
                send_sem=kv_send.at[r - 1],
                recv_sem=kv_recv.at[r - 1],
                device_id={"seq": down},
                device_id_type=MESH,
            ).wait_recv()

    kv_send_on(0)
    loads[0].wait()

    @pl.loop(0, model // TILE)
    def _(t):
        at = pl.multiple_of(t * TILE, 128)
        q = turn(nn(n1_ref[...], wq[:, pl.ds(at, TILE)])).astype(BF)
        for i in range(TILE // HEAD_DIM):
            qh[t * (TILE // HEAD_DIM) + i] = q[:, i * HEAD_DIM : (i + 1) * HEAD_DIM]

    def split_heads(r):
        for g in range(KV_HEADS):
            kh[g, r * tokens : (r + 1) * tokens, :] = kvbuf[r, :, g * HEAD_DIM : (g + 1) * HEAD_DIM]
            vh[g, r * tokens : (r + 1) * tokens, :] = kvbuf[r, :, kvd + g * HEAD_DIM : kvd + (g + 1) * HEAD_DIM]

    job_o.forward()
    job_u.begin()
    split_heads(0)
    for r in range(1, seq):
        kv_wait(r)
        if r < seq - 1:
            kv_send_on(r)
        if r == 1:
            job_o.cross()
            job_g.forward()
            job_d.begin()
            job_o.share()
        split_heads(r)
    job_g.cross()

    row = lax.broadcasted_iota(jnp.int32, (tokens, tokens), 0)
    col = lax.broadcasted_iota(jnp.int32, (tokens, tokens), 1)
    lse_ref[...] = jnp.zeros_like(lse_ref)
    lane = lax.broadcasted_iota(jnp.int32, (tokens, 128), 1)

    half = HEADS // 2

    def attend_heads(start, stop):
        @pl.loop(start, stop)
        def _(h):
            g = h // GROUP
            q = qh[h]
            scores = []
            for r in range(seq):
                s = nt(q, kh[g, r * tokens : (r + 1) * tokens, :]) * SCALE
                scores.append(jnp.where(col <= row if r == 0 else place >= r, s, NEG))
            top = functools.reduce(jnp.maximum, [jnp.max(s, axis=1, keepdims=True) for s in scores])
            weights = [jnp.exp(s - top) for s in scores]
            total = sum(jnp.sum(w, axis=1, keepdims=True) for w in weights)
            inverse = 1.0 / total
            oh[h] = sum(
                nn((w * inverse).astype(BF), vh[g, r * tokens : (r + 1) * tokens, :])
                for r, w in enumerate(weights)
            ).astype(BF)
            lse_ref[...] += jnp.where(lane == h, top + jnp.log(total), 0.0)

    attend_heads(0, half)
    job_g.share()
    job_u.forward()
    attend_heads(half, HEADS)
    for h in range(HEADS):
        o_ref[:, h * HEAD_DIM : (h + 1) * HEAD_DIM] = oh[h]
    job_u.cross()
    job_d.forward()
    job_u.share()
    job_d.cross()
    job_d.share()
    for job in (job_o, job_g, job_u, job_d):
        job.finish()
    for r in range(seq - 1):

        @pl.when((place >= r) & (place < seq - 1))
        def _():
            kv_copy(r).wait_send()

    for g in gains:
        g.wait_send()
    for job in jobs:
        job.drain()


def forward_call(dp, seq, x, gains, tables, weights):
    tokens, model = x.shape
    chip_bits = dp.bit_length() - 2
    copies = gather_copies(chip_bits)
    anyspec = pl.BlockSpec(memory_space=pl.ANY)
    vmem = pl.BlockSpec(memory_space=pltpu.VMEM)
    out_shape = [jax.ShapeDtypeStruct((dp * w.shape[0], w.shape[1]), BF) for w in weights]
    heads = jax.ShapeDtypeStruct((HEADS, tokens, HEAD_DIM), BF)
    keys = jax.ShapeDtypeStruct((KV_HEADS, seq * tokens, HEAD_DIM), BF)
    out_shape += [
        heads,
        keys,
        keys,
        jax.ShapeDtypeStruct((tokens, model), BF),
        jax.ShapeDtypeStruct((tokens, 128), F32),
        jax.ShapeDtypeStruct((tokens, model), BF),
        jax.ShapeDtypeStruct((8, model), F32),
    ]
    kvd = weights[1].shape[1]
    dma = pltpu.SemaphoreType.DMA
    return pl.pallas_call(
        functools.partial(forward_body, dp, seq),
        out_shape=out_shape,
        in_specs=[vmem] * 5 + [anyspec] * 7,
        out_specs=[anyspec] * 7 + [vmem] * 7,
        scratch_shapes=[pltpu.VMEM(w.shape, BF) for w in weights]
        + [
            pltpu.VMEM((model, model), BF),
            pltpu.VMEM((model, kvd), BF),
            pltpu.VMEM((model, kvd), BF),
            pltpu.VMEM((seq, tokens, model), BF),
            pltpu.VMEM((dp, 8, 256), F32),
            pltpu.VMEM((HEADS, tokens, HEAD_DIM), BF),
            dma((7, copies)),
            dma((7, copies)),
            dma((seq,)),
            dma((seq,)),
            dma((dp,)),
            dma((dp,)),
            dma((7,)),
            dma((3,)),
        ],
        compiler_params=pltpu.CompilerParams(
            collective_id=0, has_side_effects=True, vmem_limit_bytes=60 * 1024 * 1024
        ),
        name="forward",
    )(x, gains, *tables, *weights)


def head_column(lse, h):
    lane = lax.broadcasted_iota(jnp.int32, lse.shape, 1)
    return jnp.sum(jnp.where(lane == h, lse, 0.0), axis=1, keepdims=True)


def back_group(place, chunks, g, q_ref, do_ref, lse, k, v, dq_ref, dk_ref, dv_ref, acc_k, acc_v):
    tokens = q_ref.shape[1]
    row = lax.broadcasted_iota(jnp.int32, (tokens, tokens), 0)
    col = lax.broadcasted_iota(jnp.int32, (tokens, tokens), 1)
    for i in range(GROUP):
        h = GROUP * g + i
        q, do = q_ref[h], do_ref[h]
        total = head_column(lse, h)
        probs, dprobs = [], []
        for r in range(chunks):
            span = slice(r * tokens, (r + 1) * tokens)
            s = nt(q, k[span, :]) * SCALE
            s = jnp.where(col <= row if r == 0 else place >= r, s, NEG)
            probs.append(jnp.exp(s - total))
            dprobs.append(nt(do, v[span, :]))
        inner = sum(jnp.sum(p * d, axis=1, keepdims=True) for p, d in zip(probs, dprobs))
        dq = jnp.zeros((tokens, HEAD_DIM), F32)
        for r in range(chunks):
            span = slice(r * tokens, (r + 1) * tokens)
            ds = (probs[r] * (dprobs[r] - inner)).astype(BF)
            dq += nn(ds, k[span, :])
            dk = tn(ds, q)
            dv = tn(probs[r].astype(BF), do)
            if i == 0:
                acc_k[span, :] = dk
                acc_v[span, :] = dv
            else:
                dk_ref[g, span, :] = ((acc_k[span, :] + dk) * SCALE).astype(BF)
                dv_ref[g, span, :] = (acc_v[span, :] + dv).astype(BF)
        dq_ref[h] = (dq * SCALE).astype(BF)


COLS = 512
LAG_B, LAG_C, LAG_D = 1, 3, 5
SLOTS_CORE, SLOTS, SLOTS_SUM, SLOTS_OUT = 2, 4, 10, 8


def backward_body(seq, x_ref, gains_ref, e2_ref, cos_ref, first_ref, second_ref, hidden_ref, eb_ref, lefts_ref,
                  qh, kh, vh, do_ref, lse_ref, gain2_ref, rights_in, wq_in, wk_in, wv_in, *refs):
    dx_ref, gain_out, res = refs[:3]
    (rights, doh, dqh, dkh, dvh, acc_k, acc_v, dkv, dkv_in, dn1, wt,
     cs, cr, sums, r0, r1, zs, zr, zt, gsend, grecv, gsum, gzrecv,
     load_sem, w_sem, core_s, core_r, s0_s, s0_r, s1_s, s1_r, z_s, z_r, a_s, a_r, t_sem, kv_s, kv_r,
     g_s, g_r, gz_s, gz_r, core_free, s0_free, s1_free, z_free) = refs[3:]
    me, place = lax.axis_index("dp"), lax.axis_index("seq")
    core, chip_x, chip_y = me % 2, (me // 2) % 2, me // 4
    tokens, model = x_ref.shape
    rows = model // 8
    sub = rows // seq
    kvd = wk_in.shape[1]
    d_rows = hidden_ref.shape[0] // 8
    d_chunks = d_rows * 3 // rows
    n_chunks = rights.shape[1] // COLS
    o_panels = model // COLS
    gu_panels = n_chunks - 3 * o_panels
    total_chunks = d_chunks + n_chunks

    def owner(x, y, c):
        return ((chip_y + y) % 2) * 4 + ((chip_x + x) % 2) * 2 + (core + c) % 2

    partner = owner(0, 0, 1)
    near = [[owner(1, 0, 0), owner(0, 1, 0)], [owner(0, 1, 0), owner(1, 0, 0)]]

    load = pltpu.make_async_copy(rights_in, rights.at[:, : rights_in.shape[1]], load_sem)
    load.start()

    barrier = pltpu.get_barrier_semaphore()
    for off in range(1, 8):
        pl.semaphore_signal(barrier, inc=1, device_id={"dp": me ^ off}, device_id_type=MESH)
    for far in range(1, seq):
        to = (place + far) % seq
        pl.semaphore_signal(barrier, inc=1, device_id={"seq": to}, device_id_type=MESH)
    pl.semaphore_wait(barrier, 7 + seq - 1)

    for h in range(HEADS):
        doh[h] = lanes(do_ref, h)
    load.wait()

    def remote(src, dst, send, recv, **target):
        return pltpu.make_async_remote_copy(
            src_ref=src, dst_ref=dst, send_sem=send, recv_sem=recv, device_id=target, device_id_type=MESH
        )

    def signal(sem, **target):
        pl.semaphore_signal(sem, inc=1, device_id=target, device_id_type=MESH)

    def core_copy(c):
        s = c % SLOTS_CORE
        return remote(cs.at[s], cr.at[s], core_s.at[s], core_r.at[s], dp=partner)

    def first_copy(c, parity):
        s = c % SLOTS
        return remote(sums.at[c % SLOTS_SUM, pl.ds(2 * rows, 2 * rows)], r0.at[s], s0_s.at[s], s0_r.at[s], dp=near[parity][0])

    def second_copy(c, parity):
        s = c % SLOTS
        return remote(sums.at[c % SLOTS_SUM, pl.ds(rows, rows)], r1.at[s], s1_s.at[s], s1_r.at[s], dp=near[parity][1])

    def offsets(index, parity):
        low, high = index % 2, index // 2
        return (high, low) if parity == 0 else (low, high)

    def stage_a(c, parity):
        s, t = c % SLOTS_CORE, c % SLOTS_SUM

        @pl.when(c >= SLOTS_CORE)
        def _():
            core_copy(c).wait_send()

        def put(away, term):
            @pl.loop(0, 4)
            def _(index):
                dx, dy = offsets(index, parity)
                at = pl.multiple_of(index * rows, 16)
                if away:
                    cs[s, pl.ds(at, rows), :] = term(owner(dx, dy, 1)).astype(BF)
                else:
                    sums[t, pl.ds(at, rows), :] = term(owner(dx, dy, 0)).astype(BF)

        def term_d(who):
            size = rows // 3
            at = pl.multiple_of(who * d_rows + c * size, 16)
            left = hidden_ref[pl.ds(at, size), :]
            return jnp.concatenate(
                [nn(left, eb_ref[:, i * COLS : (i + 1) * COLS]) for i in range(3)], axis=0
            )

        k = c - d_chunks
        which = (k >= gu_panels).astype(jnp.int32) + (k >= gu_panels + o_panels).astype(jnp.int32)

        def term_n(who):
            left = lefts_ref[pl.ds(pl.multiple_of(which * model + who * rows, 16), rows), :]
            return nn(left, rights[:, pl.ds(pl.multiple_of(k * COLS, 128), COLS)])

        def both(term):
            put(True, term)

            @pl.when(c >= SLOTS_CORE)
            def _():
                pl.semaphore_wait(core_free, 1)

            core_copy(c).start()
            put(False, term)

        @pl.when(c < d_chunks)
        def _():
            both(term_d)

        @pl.when(c >= d_chunks)
        def _():
            both(term_n)

    def add_rows(count, target, extra):
        @pl.loop(0, count // 64)
        def _(i):
            at = pl.multiple_of(i * 64, 16)
            target[pl.ds(at, 64), :] = (target[pl.ds(at, 64), :].astype(F32) + extra[pl.ds(at, 64), :].astype(F32)).astype(BF)

    def stage_b(c, parity):
        core_copy(c).wait_recv()
        add_rows(4 * rows, sums.at[c % SLOTS_SUM], cr.at[c % SLOTS_CORE])

        @pl.when(c < total_chunks - SLOTS_CORE)
        def _():
            signal(core_free, dp=partner)

        @pl.when(c >= SLOTS)
        def _():
            pl.semaphore_wait(s0_free.at[parity], 1)

        first_copy(c, parity).start()

    def stage_c(c, parity):
        first_copy(c, parity).wait_recv()
        add_rows(2 * rows, sums.at[c % SLOTS_SUM], r0.at[c % SLOTS])

        @pl.when(c < total_chunks - SLOTS)
        def _():
            signal(s0_free.at[parity], dp=near[parity][0])

        @pl.when(c >= SLOTS)
        def _():
            pl.semaphore_wait(s1_free.at[parity], 1)

        second_copy(c, parity).start()
        first_copy(c, parity).wait_send()

    def stage_d(c, parity):
        second_copy(c, parity).wait_recv()
        add_rows(rows, sums.at[c % SLOTS_SUM], r1.at[c % SLOTS])

        @pl.when(c < total_chunks - SLOTS)
        def _():
            signal(s1_free.at[parity], dp=near[parity][1])

        second_copy(c, parity).wait_send()

    def step_of(way):
        return 1 - 2 * way

    def inside(at):
        return (at >= 0) & (at < seq)

    def z_copy(c, way, hop):
        s = c % SLOTS
        slot = way * (seq - 1) + hop - 1
        return remote(zs.at[slot, s], zr.at[slot, s], z_s.at[slot, s], z_r.at[slot, s], seq=place + step_of(way))

    def z_sends(way, hop):
        return inside(place + step_of(way) * (seq - hop))

    def z_gets(way, hop):
        return inside(place - step_of(way)) & inside(place - step_of(way) + step_of(way) * (seq - hop))

    def part(c, index):
        index = jnp.minimum(jnp.maximum(index, 0), seq - 1)
        return sums[c % SLOTS_SUM, pl.ds(pl.multiple_of(index * sub, 16), sub), :].astype(F32)

    def z_take(c, way, hop):
        slot = way * (seq - 1) + hop - 1
        gets = z_gets(way, hop)

        @pl.when(gets)
        def _():
            z_copy(c, way, hop).wait_recv()

        return jnp.where(gets, zr[slot, c % SLOTS].astype(F32), 0.0)

    def z_release(c, way, hop):
        slot = way * (seq - 1) + hop - 1

        @pl.when(z_gets(way, hop) & (c < total_chunks - SLOTS))
        def _():
            signal(z_free.at[slot], seq=place - step_of(way))

    def stage_z(c, hop):
        for way in range(2):
            slot = way * (seq - 1) + hop - 1
            value = part(c, place + step_of(way) * (seq - hop))
            if hop > 1:
                value = value + z_take(c, way, hop - 1)
            sends = z_sends(way, hop)

            @pl.when(sends & (c >= SLOTS))
            def _():
                z_copy(c, way, hop).wait_send()

            zs[slot, c % SLOTS] = value.astype(BF)
            if hop > 1:
                z_release(c, way, hop - 1)

            @pl.when(sends & (c >= SLOTS))
            def _():
                pl.semaphore_wait(z_free.at[slot], 1)

            @pl.when(sends)
            def _():
                z_copy(c, way, hop).start()

    def res_at(c, source):
        index = jnp.minimum(jnp.maximum(source, 0), seq - 1)
        return res.at[pl.ds(pl.multiple_of(c * rows + index * sub, 16), sub)]

    def own_copy(c):
        s = c % SLOTS_OUT
        return pltpu.make_async_copy(zt.at[s], res_at(c, place), t_sem.at[s])

    def a_copy(c, way, hop):
        s = c % SLOTS_OUT
        slot = way * (seq - 1) + hop - 1
        source = place - step_of(way) * (hop - 1)
        src = zt.at[s] if hop == 1 else res_at(c, source)
        return remote(src, res_at(c, source), a_s.at[slot, s], a_r.at[slot, s], seq=place + step_of(way))

    def a_sends(way, hop):
        return inside(place + step_of(way)) & inside(place - step_of(way) * (hop - 1))

    def a_gets(way, hop):
        return inside(place - step_of(way) * hop)

    def stage_total(c):
        value = part(c, place)
        for way in range(2):
            value = value + z_take(c, way, seq - 1)

        @pl.when(c >= SLOTS_OUT)
        def _():
            own_copy(c).wait()

        for way in range(2):
            @pl.when((c >= SLOTS_OUT) & a_sends(way, 1))
            def _():
                a_copy(c, way, 1).wait_send()

        zt[c % SLOTS_OUT] = value.astype(BF)
        for way in range(2):
            z_release(c, way, seq - 1)
        own_copy(c).start()
        stage_out(c, 1)

    def stage_out(c, hop):
        for way in range(2):
            if hop > 1:
                @pl.when(a_gets(way, hop - 1))
                def _():
                    a_copy(c, way, hop - 1).wait_recv()

            if hop < seq:
                if hop > 1:
                    @pl.when((c >= SLOTS_OUT) & a_sends(way, hop))
                    def _():
                        a_copy(c, way, hop).wait_send()

                @pl.when(a_sends(way, hop))
                def _():
                    a_copy(c, way, hop).start()

    lag_total = LAG_D + seq - 1
    stages = [(LAG_B, stage_b), (LAG_C, stage_c), (LAG_D, stage_d), (LAG_D, lambda c, parity: stage_z(c, 1))]
    stages += [(LAG_D + hop - 1, lambda c, parity, hop=hop: stage_z(c, hop)) for hop in range(2, seq)]
    stages += [(lag_total, lambda c, parity: stage_total(c))]
    stages += [(lag_total + hop - 1, lambda c, parity, hop=hop: stage_out(c, hop)) for hop in range(2, seq + 1)]
    last_lag = lag_total + seq - 1

    def tick(c, parity):
        for lag, stage in sorted(stages, key=lambda pair: -pair[0]):
            then = c - lag

            @pl.when((then >= 0) & (then < total_chunks))
            def _():
                stage(then, (parity + lag) % 2)

        @pl.when(c < total_chunks)
        def _():
            stage_a(c, parity)

    def kv_copy(r):
        return remote(dkv.at[r], dkv_in.at[r - 1], kv_s.at[r], kv_r.at[r], seq=place - 1)

    def kv_send(r):
        @pl.when(place >= r)
        def _():
            kv_copy(r).start()

    def kv_take(r):
        gets = (place + 1 >= r) & (place + 1 < seq)

        @pl.when(gets)
        def _():
            kv_copy(r).wait_recv()
            add_rows(tokens, dkv.at[r - 1], dkv_in.at[r - 1])

    def turn_back(value):
        ahead = pltpu.roll(value, TILE - HEAD_DIM // 2, 1)
        behind = pltpu.roll(value, HEAD_DIM // 2, 1)
        return (value * cos_ref[...] - behind * second_ref[...] + ahead * first_ref[...]).astype(BF)

    q_at = (gu_panels + o_panels) * COLS

    def w_load(t, i):
        at = pl.multiple_of(t * TILE, 16)
        s = t % 2
        src, lo, width = ((wq_in, 0, model), (wk_in, model, kvd), (wv_in, model + kvd, kvd))[i]
        return pltpu.make_async_copy(src.at[pl.ds(at, TILE)], wt.at[s, :, pl.ds(lo, width)], w_sem.at[s, i])

    def last_norm():
        for h in range(HEADS):
            rights[:, q_at + h * HEAD_DIM : q_at + (h + 1) * HEAD_DIM] = dqh[h]
        for t in range(model // TILE):
            at = q_at + t * TILE
            rights[:, at : at + TILE] = turn_back(rights[:, at : at + TILE].astype(F32))
        for t in range(kvd // TILE):
            at = q_at + model + t * TILE
            rights[:, at : at + TILE] = turn_back(dkv[0, :, t * TILE : (t + 1) * TILE].astype(F32))
        rights[:, q_at + model + kvd :] = dkv[0, :, kvd:]
        for i in range(3):
            w_load(0, i).start()

        @pl.loop(0, model // TILE)
        def _(t):
            for i in range(3):
                w_load(t, i).wait()

            @pl.when(t + 1 < model // TILE)
            def _():
                for i in range(3):
                    w_load(t + 1, i).start()

            dn1[:, pl.ds(pl.multiple_of(t * TILE, 128), TILE)] = nt(rights[:, q_at:], wt[t % 2])

        x = x_ref[...].astype(F32)
        scale = lax.rsqrt(jnp.mean(x * x, axis=1, keepdims=True) + EPS)
        unit = x * scale
        grad = dn1[...]
        term = jnp.sum(grad * unit, axis=0, keepdims=True)
        scaled = grad * gains_ref[0:1, :]
        inner = jnp.mean(scaled * unit, axis=1, keepdims=True)
        dx_ref[...] = e2_ref[...] + scale * (scaled - unit * inner)
        for k in range(8):
            gsend[k, 0:1, :rows] = term[:, k * rows : (k + 1) * rows]
            gsend[k, 1:2, :rows] = gain2_ref[0:1, k * rows : (k + 1) * rows]

    def gain_copies():
        return [
            remote(gsend.at[me ^ off], grecv.at[me], g_s.at[off], g_r.at[off], dp=me ^ off) for off in range(1, 8)
        ]

    def gain_line():
        return [
            remote(gsum, gzrecv.at[place], gz_s.at[far], gz_r.at[far], seq=(place + far) % seq) for far in range(1, seq)
        ]

    ticks = total_chunks + last_lag
    d_pairs = KV_HEADS // 2

    @pl.loop(0, -(-ticks // 2))
    def _(p):
        for parity in range(2):
            tick(2 * p + parity, parity)

        @pl.when(p < d_pairs)
        def _():
            for i in range(2):
                g = 2 * p + i
                back_group(place, seq, g, qh, doh, lse_ref[...], kh.at[g], vh.at[g], dqh, dkh, dvh, acc_k, acc_v)

        @pl.when(p == d_pairs - 1)
        def _():
            for r in range(seq):
                for g in range(KV_HEADS):
                    lo = g * HEAD_DIM
                    dkv[r, :, lo : lo + HEAD_DIM] = dkh[g, r * tokens : (r + 1) * tokens, :]
                    dkv[r, :, kvd + lo : kvd + lo + HEAD_DIM] = dvh[g, r * tokens : (r + 1) * tokens, :]
            kv_send(seq - 1)

        for r in range(seq - 1, 0, -1):
            @pl.when(p == d_pairs - 1 + 2 * (seq - r))
            def _():
                kv_take(r)
                if r > 1:
                    kv_send(r - 1)
                else:
                    last_norm()
                    for made in gain_copies():
                        made.start()
                    grecv[me] = gsend[me]

        @pl.when(p == d_pairs + 2 * seq - 2)
        def _():
            for made in gain_copies():
                made.wait_recv()
            gsum[...] = sum(grecv[k] for k in range(1, 8)) + grecv[0]
            gzrecv[place] = gsum[...]
            for made in gain_line():
                made.start()

        @pl.when(p == d_pairs + 2 * seq - 1)
        def _():
            for made in gain_line():
                made.wait_recv()
            gain_out[...] = sum(gzrecv[k] for k in range(seq))

    for made in gain_copies() + gain_line():
        made.wait_send()
    for r in range(1, seq):
        @pl.when(place >= r)
        def _():
            kv_copy(r).wait_send()
    for c in range(total_chunks - SLOTS_CORE, total_chunks):
        core_copy(c).wait_send()
    for way in range(2):
        for hop in range(1, seq):
            for c in range(total_chunks - SLOTS, total_chunks):
                @pl.when(z_sends(way, hop))
                def _():
                    z_copy(c, way, hop).wait_send()
            for c in range(total_chunks - SLOTS_OUT, total_chunks):
                @pl.when(a_sends(way, hop))
                def _():
                    a_copy(c, way, hop).wait_send()
    for c in range(total_chunks - SLOTS_OUT, total_chunks):
        own_copy(c).wait()


def backward_call(seq, x, gains, e2, tables, hidden_t, eb, lefts, qh, kh, vh, do, lse, gain2, rights, w_q, w_k, w_v):
    tokens, model = x.shape
    rows = model // 8
    sub = rows // seq
    kvd = w_k.shape[1]
    wide = rights.shape[1] + model + 2 * kvd
    chunks = hidden_t.shape[0] // 8 * 3 // rows + wide // COLS
    anyspec = pl.BlockSpec(memory_space=pl.ANY)
    vmem = pl.BlockSpec(memory_space=pltpu.VMEM)
    dma, regular = pltpu.SemaphoreType.DMA, pltpu.SemaphoreType.REGULAR
    hops = 2 * (seq - 1)
    heads = pltpu.VMEM((HEADS, tokens, HEAD_DIM), BF)
    keys = pltpu.VMEM((KV_HEADS, seq * tokens, HEAD_DIM), BF)
    return pl.pallas_call(
        functools.partial(backward_body, seq),
        out_shape=[
            jax.ShapeDtypeStruct((tokens, model), F32),
            jax.ShapeDtypeStruct((8, 256), F32),
            jax.ShapeDtypeStruct((chunks * rows, COLS), BF),
        ],
        in_specs=[vmem] * 15 + [anyspec] * 4,
        out_specs=[vmem, vmem, anyspec],
        scratch_shapes=[
            pltpu.VMEM((tokens, wide), BF),
            heads, heads, keys, keys,
            pltpu.VMEM((seq * tokens, HEAD_DIM), F32),
            pltpu.VMEM((seq * tokens, HEAD_DIM), F32),
            pltpu.VMEM((seq, tokens, model), BF),
            pltpu.VMEM((seq - 1, tokens, model), BF),
            pltpu.VMEM((tokens, model), F32),
            pltpu.VMEM((2, TILE, model + 2 * kvd), BF),
            pltpu.VMEM((SLOTS_CORE, 4 * rows, COLS), BF),
            pltpu.VMEM((SLOTS_CORE, 4 * rows, COLS), BF),
            pltpu.VMEM((SLOTS_SUM, 4 * rows, COLS), BF),
            pltpu.VMEM((SLOTS, 2 * rows, COLS), BF),
            pltpu.VMEM((SLOTS, rows, COLS), BF),
            pltpu.VMEM((hops, SLOTS, sub, COLS), BF),
            pltpu.VMEM((hops, SLOTS, sub, COLS), BF),
            pltpu.VMEM((SLOTS_OUT, sub, COLS), BF),
            pltpu.VMEM((8, 8, 256), F32),
            pltpu.VMEM((8, 8, 256), F32),
            pltpu.VMEM((8, 256), F32),
            pltpu.VMEM((seq, 8, 256), F32),
            dma(()), dma((2, 3)),
            dma((SLOTS_CORE,)), dma((SLOTS_CORE,)),
            dma((SLOTS,)), dma((SLOTS,)),
            dma((SLOTS,)), dma((SLOTS,)),
            dma((hops, SLOTS)), dma((hops, SLOTS)),
            dma((hops, SLOTS_OUT)), dma((hops, SLOTS_OUT)),
            dma((SLOTS_OUT,)),
            dma((seq,)), dma((seq,)),
            dma((8,)), dma((8,)),
            dma((seq,)), dma((seq,)),
            regular, regular((2,)), regular((2,)), regular((hops,)),
        ],
        compiler_params=pltpu.CompilerParams(
            collective_id=1, has_side_effects=True, vmem_limit_bytes=62 * 1024 * 1024
        ),
        name="backward",
    )(x, gains, e2, *tables, hidden_t, eb, lefts, qh, kh, vh, do, lse, gain2, rights, w_q, w_k, w_v)


def finish_call(res, dx, d_rows, ff, kvd):
    tokens, model = dx.shape
    block = res.shape[1]
    steps = 4
    per_d, per_f, per_m = d_rows * 3 // block // steps, ff // COLS // steps, model // COLS
    at_f = per_d * steps // per_f
    at_m = per_d * steps + 2 * per_f * steps
    panel = block // 3
    assert per_d and per_f and per_d * steps % per_f == 0 and per_m < steps

    def body(d_in, g_in, u_in, o_in, q_in, kv_in, dx_in, down, gate, up, out, query, key, value, dx_out):
        s = pl.program_id(0)
        dx_out[...] = dx_in[...]
        for i in range(per_d):
            for j in range(3):
                down[i * panel : (i + 1) * panel, j * COLS : (j + 1) * COLS] = d_in[i, j * panel : (j + 1) * panel, :].astype(F32)
        for i in range(per_f):
            gate[:, i * COLS : (i + 1) * COLS] = g_in[i].astype(F32)
            up[:, i * COLS : (i + 1) * COLS] = u_in[i].astype(F32)
        for i in range(per_m):

            @pl.when(s == i)
            def _():
                out[:, i * COLS : (i + 1) * COLS] = o_in[0].astype(F32)
                query[:, i * COLS : (i + 1) * COLS] = q_in[0].astype(F32)
                mid = min(max(kvd - i * COLS, 0), COLS)
                if mid:
                    key[:, i * COLS : i * COLS + mid] = kv_in[0, :, :mid].astype(F32)
                if mid < COLS:
                    lo = i * COLS + mid - kvd
                    value[:, lo : lo + COLS - mid] = kv_in[0, :, mid:].astype(F32)

    def chunk(count, at):
        return pl.BlockSpec((count, block, COLS), at)

    wide = lambda base: chunk(per_f, lambda s: (base + s, 0, 0))
    thin = lambda base: chunk(1, lambda s: (base + jnp.minimum(s, per_m - 1), 0, 0))
    whole = lambda width: pl.BlockSpec((block, width), lambda s: (0, 0))
    return pl.pallas_call(
        body,
        grid=(steps,),
        in_specs=[
            chunk(per_d, lambda s: (s, 0, 0)),
            wide(at_f),
            wide(at_f + steps),
            thin(at_m),
            thin(at_m + per_m),
            thin(at_m + 2 * per_m),
            pl.BlockSpec((tokens // steps, model), lambda s: (s, 0)),
        ],
        out_specs=[
            pl.BlockSpec((d_rows // steps, model), lambda s: (s, 0)),
            pl.BlockSpec((block, ff // steps), lambda s: (0, s)),
            pl.BlockSpec((block, ff // steps), lambda s: (0, s)),
            whole(model),
            whole(model),
            whole(kvd),
            whole(kvd),
            pl.BlockSpec((tokens // steps, model), lambda s: (s, 0)),
        ],
        out_shape=[
            jax.ShapeDtypeStruct((d_rows, model), F32),
            jax.ShapeDtypeStruct((block, ff), F32),
            jax.ShapeDtypeStruct((block, ff), F32),
            jax.ShapeDtypeStruct((block, model), F32),
            jax.ShapeDtypeStruct((block, model), F32),
            jax.ShapeDtypeStruct((block, kvd), F32),
            jax.ShapeDtypeStruct((block, kvd), F32),
            jax.ShapeDtypeStruct((tokens, model), F32),
        ],
        compiler_params=pltpu.CompilerParams(vmem_limit_bytes=60 * 1024 * 1024),
        name="finish",
    )(*[res] * 6, dx)


def attend_back(place, qh, kh, vh, doh, lse):
    chunks = kh.shape[1] // qh.shape[1]

    def body(place_ref, q_ref, k_ref, v_ref, do_ref, lse_ref, dq_ref, dk_ref, dv_ref, acc_k, acc_v):
        @pl.loop(0, KV_HEADS)
        def _(g):
            back_group(place_ref[0], chunks, g, q_ref, do_ref, lse_ref[...], k_ref.at[g], v_ref.at[g], dq_ref, dk_ref, dv_ref, acc_k, acc_v)

    vmem = pl.BlockSpec(memory_space=pltpu.VMEM)
    acc = pltpu.VMEM(kh.shape[1:], F32)
    return pl.pallas_call(
        body,
        in_specs=[pl.BlockSpec(memory_space=pltpu.SMEM)] + [vmem] * 5,
        out_specs=[vmem] * 3,
        out_shape=[jax.ShapeDtypeStruct(a.shape, BF) for a in (qh, kh, vh)],
        scratch_shapes=[acc, acc],
        name="attend_back",
    )(place, qh, kh, vh, doh, lse)


def flip(value, axis, bit):
    size = lax.axis_size(axis)
    return lax.ppermute(value, axis, [(i, i ^ bit) for i in range(size)])


def xor_order(bits):
    order = [0]
    for bit in list(reversed(bits)) + [1]:
        order = order + [off ^ bit for off in order]
    return order


def scatter_term(left, right, bits):
    half = left.shape[1] // 2
    away = tn(left[:, half:], right).astype(BF)
    came = flip(away, "dp", 1)
    quarter = half // 2
    away = (tn(left[:, quarter:half], right) + came[quarter:]).astype(BF)
    kept = (tn(left[:, :quarter], right) + came[:quarter]).astype(BF)
    came = flip(away, "dp", bits[0])
    for bit in bits[1:]:
        size = kept.shape[0] // 2
        away = (kept[size:].astype(F32) + came[size:]).astype(BF)
        kept = (kept[:size].astype(F32) + came[:size]).astype(BF)
        came = flip(away, "dp", bit)
    return (kept.astype(F32) + came).astype(BF)


def line_sum(value, place):
    size = lax.axis_size("seq")
    rows = value.shape[0] // size

    def chunk(index):
        index = jnp.clip(index, 0, size - 1)
        return lax.dynamic_slice_in_dim(value, index * rows, rows, 0)

    total = chunk(place).astype(F32)
    for way in (1, -1):
        held = None
        for far in range(size - 1, 0, -1):
            mine = chunk(place + way * far)
            if held is not None:
                mine = (mine.astype(F32) + held).astype(BF)
            pairs = [(i, i + way) for i in range(size) if 0 <= i + way * far < size]
            held = lax.ppermute(mine, "seq", pairs)
        total = total + held
    total = total.astype(BF)
    out = jnp.zeros(value.shape, F32)
    out = lax.dynamic_update_slice(out, total.astype(F32), (place * rows, 0))
    for way in (1, -1):
        held = total
        for far in range(1, size):
            pairs = [
                (i, i + way) for i in range(size) if 0 <= i + way < size and 0 <= i - way * (far - 1) < size
            ]
            held = lax.ppermute(held, "seq", pairs)
            source = place - way * far
            index = jnp.clip(source, 0, size - 1) * rows
            old = lax.dynamic_slice(out, (index, 0), held.shape)
            good = (source >= 0) & (source < size)
            out = lax.dynamic_update_slice(
                out, jnp.where(good, held.astype(F32), old), (index, 0)
            )
    return out


def rope_tables(place, tokens, width):
    half = HEAD_DIM // 2
    positions = (place * tokens + jnp.arange(tokens, dtype=jnp.int32)).astype(F32)
    frequency = ROPE_BASE ** (-jnp.arange(half).astype(F32) / half)
    angles = positions[:, None] * frequency[None, :]
    cos, sin = jnp.cos(angles), jnp.sin(angles)
    zero = jnp.zeros_like(sin)
    heads = width // HEAD_DIM
    tile = lambda a, b: jnp.tile(jnp.concatenate([a, b], axis=1), (1, heads))
    return tile(cos, cos), tile(sin, zero), tile(zero, sin)


def rotate(field, tables, sign):
    cos, first, second = tables
    half = HEAD_DIM // 2
    width = field.shape[1]
    cos, first, second = cos[:, :width], first[:, :width], second[:, :width]
    ahead = jnp.concatenate([field[:, half:], field[:, :half]], axis=1)
    behind = jnp.concatenate([field[:, -half:], field[:, :-half]], axis=1)
    return field * cos + sign * (behind * second - ahead * first)


def norm_scale(values):
    return lax.rsqrt(jnp.mean(values * values, axis=-1, keepdims=True) + EPS)


def norm_back(values, scale, gain, grad):
    unit = values * scale
    grad_gain = jnp.sum(grad * unit, axis=0)
    scaled = grad * gain
    inner = jnp.mean(scaled * unit, axis=-1, keepdims=True)
    return scale * (scaled - unit * inner), grad_gain


def local(tokens, cotangent, w_query, w_key, w_value, w_out, w_gate, w_up, w_down, gain_attn, gain_mlp):
    dp, seq = lax.axis_size("dp"), lax.axis_size("seq")
    me, place = lax.axis_index("dp"), lax.axis_index("seq")
    bits = [1 << i for i in range(1, dp.bit_length() - 1)]
    turned = bits[1:] + bits[:1]
    model = tokens.shape[-1]
    rows = tokens.shape[1]
    kvd = w_key.shape[-1]
    place_arr = place.reshape(1).astype(jnp.int32)

    half_model = model // 2

    def xor_columns(value, way):
        width = value.shape[1] // dp
        cut = lambda off: lax.dynamic_slice_in_dim(value, (me ^ off) * width, width, 1)
        return jnp.concatenate([cut(off) for off in xor_order(way)], axis=1)

    tables = rope_tables(place, rows, model)
    x = tokens[0].astype(F32)
    packed = jnp.zeros((8, 256), F32)
    packed = packed.at[0, : gain_attn.shape[1]].set(gain_attn[0].astype(F32))
    packed = packed.at[1, : gain_mlp.shape[1]].set(gain_mlp[0].astype(F32))
    shards = [w[0] for w in (w_query, w_key, w_value, w_out, w_gate, w_up, w_down)]
    outs = forward_call(dp, seq, tokens[0], packed, [t[:, :TILE] for t in tables], shards)
    w_q, w_k, w_v, w_o, w_g, w_u, w_d = outs[:7]
    qh, kh, vh, mixed, lse, n1, gains = outs[7:]
    gain_one, gain_two = gains[0:1], gains[1:2]
    scale_one = norm_scale(x)
    x2 = x + nn(mixed, w_o)
    scale_two = norm_scale(x2)
    n2 = (x2 * scale_two * gain_two).astype(BF)
    gate = nn(n2, w_g)
    up = nn(n2, w_u)
    sig = jax.nn.sigmoid(gate)
    hidden = (gate * sig * up).astype(BF)
    result = x2 + nn(hidden, w_d)

    e = cotangent[0].astype(F32)
    eb = cotangent[0]
    dh = nt(eb, w_d)
    dgate = (dh * up * sig * (1.0 + gate * (1.0 - sig))).astype(BF)
    dup = (dh * gate * sig).astype(BF)
    dn2 = nt(dgate, w_g) + nt(dup, w_u)
    dx2, term_gain_two = norm_back(x2, scale_two, gain_two, dn2)
    e2 = e + dx2
    e2b = e2.astype(BF)
    do = nt(e2b, w_o).astype(BF)
    if len(bits) == 2 and (model // dp) % (16 * seq) == 0:
        lefts = jnp.concatenate([n2.T, mixed.T, n1.T], axis=0)
        rights = jnp.concatenate([dgate, dup, e2b], axis=1)
        dx, grads, res = backward_call(
            seq, tokens[0], gains, e2, [t[:, :TILE] for t in tables], hidden.T, eb, lefts,
            qh, kh, vh, do, lse, term_gain_two[None], rights, w_q, w_k, w_v,
        )
        block = model // dp
        g_down, g_gate, g_up, g_out, g_query, g_key, g_value, dx = finish_call(
            res.reshape(-1, block, COLS), dx, w_down.shape[1], w_gate.shape[2], kvd
        )
        return (
            result[None],
            dx[None],
            g_query[None],
            g_key[None],
            g_value[None],
            g_out[None],
            g_gate[None],
            g_up[None],
            g_down[None],
            grads[0:1, :block],
            grads[1:2, :block],
        )

    hidden_a = xor_columns(hidden, bits)
    hidden_b = xor_columns(hidden, turned)
    sum_down = jnp.concatenate(
        [
            scatter_term(hidden_a, eb[:, :half_model], bits),
            scatter_term(hidden_b, eb[:, half_model:], turned),
        ],
        axis=1,
    )
    n2_a, n2_b = xor_columns(n2, bits), xor_columns(n2, turned)
    sum_gate = scatter_term(n2_a, dgate, bits)
    sum_up = scatter_term(n2_b, dup, turned)
    mixed_a, mixed_b = xor_columns(mixed, bits), xor_columns(mixed, turned)
    sum_out = jnp.concatenate(
        [
            scatter_term(mixed_a, e2b[:, :half_model], bits),
            scatter_term(mixed_b, e2b[:, half_model:], turned),
        ],
        axis=1,
    )
    doh = do.reshape(rows, HEADS, HEAD_DIM).transpose(1, 0, 2)
    dqh, dkh, dvh = attend_back(place_arr, qh, kh, vh, doh, lse)
    dq = dqh.transpose(1, 0, 2).reshape(rows, model)
    dks, dvs = (a.reshape(KV_HEADS, seq, rows, HEAD_DIM).transpose(1, 2, 0, 3).reshape(seq, rows, kvd) for a in (dkh, dvh))
    held = None
    for far in range(seq - 1, -1, -1):
        mine = jnp.concatenate([dks[far], dvs[far]], axis=1)
        if held is not None:
            mine = (mine.astype(F32) + held).astype(BF)
        if far:
            held = lax.ppermute(mine, "seq", [(i, i - 1) for i in range(far, seq)])
    dk, dv = mine[:, :kvd], mine[:, kvd:]
    dqp = rotate(dq.astype(F32), tables, -1.0).astype(BF)
    dkp = rotate(dk.astype(F32), tables, -1.0).astype(BF)
    n1_a, n1_b = xor_columns(n1, bits), xor_columns(n1, turned)
    sum_query = scatter_term(n1_a, dqp, bits)
    sum_kv = scatter_term(n1_b, jnp.concatenate([dkp, dv], axis=1), turned)
    dn1 = nt(dqp, w_q) + nt(dkp, w_k) + nt(dv, w_v)
    dx1, term_gain_one = norm_back(x, scale_one, gain_one, dn1)
    input_grad = e2 + dx1

    both = jnp.stack([term_gain_one, term_gain_two])
    for bit in [1] + bits:
        both = both + flip(both, "dp", bit)
    for bit in [1 << i for i in range(seq.bit_length() - 1)]:
        both = both + flip(both, "seq", bit)
    width = model // dp
    both = lax.dynamic_slice_in_dim(both, me * width, width, 1)

    g_down = line_sum(sum_down, place)
    g_gate = line_sum(sum_gate, place)
    g_up = line_sum(sum_up, place)
    g_out = line_sum(sum_out, place)
    g_query = line_sum(sum_query, place)
    g_kv = line_sum(sum_kv, place)
    return (
        result[None],
        input_grad[None],
        g_query[None],
        g_kv[None, :, :kvd],
        g_kv[None, :, kvd:],
        g_out[None],
        g_gate[None],
        g_up[None],
        g_down[None],
        both[0:1],
        both[1:2],
    )


def solution(mesh):
    by_token = P("dp", "seq", None)
    by_row = P(None, "dp", None)
    by_gain = P(None, "dp")
    in_specs = (by_token,) * 2 + (by_row,) * 7 + (by_gain,) * 2
    return jax.shard_map(local, mesh=mesh, in_specs=in_specs, out_specs=in_specs, check_vma=False)
```

```python
import functools

import jax
import jax.numpy as jnp
from jax import lax
from jax.experimental import pallas as pl
from jax.experimental.pallas import tpu as pltpu
from jax.sharding import PartitionSpec as P

HEADS = 16
KV_HEADS = 8
HEAD_DIM = 96
GROUP = HEADS // KV_HEADS
EPS = 1e-05
ROPE_BASE = 100000.0
BF = jnp.bfloat16
F32 = jnp.float32
NEG = -1e30
SCALE = HEAD_DIM ** (-0.5)


def dot(a, b, dims):
    return lax.dot_general(a, b, (dims, ((), ())), preferred_element_type=F32)


def nn(a, b):
    return dot(a, b, ((1,), (0,)))


def nt(a, b):
    return dot(a, b, ((1,), (1,)))


def tn(a, b):
    return dot(a, b, ((0,), (0,)))


def lanes(ref, head, width=HEAD_DIM):
    return ref[:, head * HEAD_DIM : head * HEAD_DIM + width]


MESH = pl.DeviceIdType.MESH
TILE = 4 * HEAD_DIM
COLS = 512


class Gather:
    def __init__(self, me, place, bits, src, out, send, recv):
        self.me, self.bits, self.src, self.out = me, bits, src, out
        self.send, self.recv = send, recv
        self.rows = src.shape[0]
        self.quarter = -(-self.rows // 96) * 16
        self.most = self.rows - self.quarter
        units, parts = self.most // 16, len(bits)
        self.size = [16 * (units // parts + (i < units % parts)) for i in range(parts)]
        self.start = [sum(self.size[:i]) for i in range(parts)]
        self.odd = place % 2
        self.pair = place + 1 - 2 * self.odd
        self.count = 0
        self.waits = []
        own = {}
        for bit in bits:
            own[bit] = self.copy(self.src, 0, 1, self.most, bit, self.odd * self.quarter)
        self.own = own
        self.own_core = self.copy(self.src, 0, 0, self.rows, 1, 0)
        self.forwards = []
        self.arrival = {}
        for bit in bits:
            for i in range(len(bits)):
                self.arrival[(bit, i)] = own[bit]
        for step in range(1, len(bits)):
            for i in range(len(bits)):
                order = bits[i:] + bits[:i]
                bit = order[step]
                held = [0]
                for b in order[:step]:
                    held = held + [m | b for m in held]
                for m in held[1:]:
                    start = self.odd * self.quarter + self.start[i]
                    made = self.copy(out, m, 1, self.size[i], bit, start)
                    self.forwards.append((m, i, made))
                    self.arrival[(m | bit, i)] = made
        masks = list(range(2, 2 * max(bits), 2))
        self.masks = masks
        self.across = [
            self.copy(out, m, 2, self.quarter, 0, self.odd * self.most) for m in masks
        ]
        self.core = [self.copy(out, m, 1, self.rows, 1, 0) for m in masks]
        self.seen = set()

    def copy(self, ref, m, kind, rows, bit, start):
        at = (self.me ^ m) * self.rows + start
        source = ref.at[pl.ds(pl.multiple_of(start, 16), rows)] if ref is self.src else ref.at[pl.ds(pl.multiple_of(at, 16), rows)]
        target = {"seq": self.pair} if kind == 2 else {"dp": self.me ^ bit}
        index = self.count
        self.count += 1
        return pltpu.make_async_remote_copy(
            src_ref=source,
            dst_ref=self.out.at[pl.ds(pl.multiple_of(at, 16), rows)],
            send_sem=self.send.at[index],
            recv_sem=self.recv.at[index],
            device_id=target,
            device_id_type=MESH,
        )

    def begin(self):
        for bit in self.bits:
            self.own[bit].start()
        self.own_core.start()

    def arrived(self, copy):
        if id(copy) not in self.seen:
            self.seen.add(id(copy))
            copy.wait_recv()

    def forward(self):
        for m, i, made in self.forwards:
            self.arrived(self.arrival[(m, i)])
            made.start()

    def cross(self):
        for m, made in zip(self.masks, self.across):
            for i in range(len(self.bits)):
                self.arrived(self.arrival[(m, i)])
            made.start()

    def share(self):
        for across, made in zip(self.across, self.core):
            across.wait_recv()
            made.start()

    def finish(self):
        self.own_core.wait_recv()
        for made in self.core:
            made.wait_recv()

    def drain(self):
        for made in list(self.own.values()) + [self.own_core] + [f[2] for f in self.forwards] + self.across + self.core:
            made.wait_send()


def gather_copies(chip_bits):
    forwards = sum(chip_bits * (2**step - 1) for step in range(1, chip_bits))
    return chip_bits + 1 + forwards + 2 * (2**chip_bits - 1)


def forward_body(dp, seq, x_ref, gain_ref, cos_ref, first_ref, second_ref, *refs):
    w_in, refs = refs[:7], refs[7:]
    w_out, refs = refs[:7], refs[7:]
    kept, lse_ref, gains_ref, refs = refs[:9], refs[9], refs[10], refs[11:]
    made, stage, refs = refs[:9], refs[9:16], refs[16:]
    qh, kh, vh, lefts, x2_ref, hidden, hidden_t, slope, swish = made
    (wq, wk, wv, kvbuf, gbuf, oh, n1_ref, n2_ref, o_ref, wt, send, recv, kv_send, kv_recv, g_send, g_recv, own_sem,
     load_sem, tile_sem, keep_sem) = refs
    me, place = lax.axis_index("dp"), lax.axis_index("seq")
    bits = [1 << i for i in range(1, dp.bit_length() - 1)]
    tokens, model = x_ref.shape
    block = model // dp

    for i in range(7):
        pltpu.make_async_copy(w_in[i], stage[i], own_sem.at[i]).start()
    for r in range(1, seq):
        kvbuf[r] = jnp.zeros_like(kvbuf[r])

    barrier = pltpu.get_barrier_semaphore()
    for off in range(1, dp):
        pl.semaphore_signal(barrier, inc=1, device_id={"dp": me ^ off}, device_id_type=MESH)
    up, down = place + 1, place - 1
    odd = place % 2
    pair = place + 1 - 2 * odd
    other = place - 1 + 2 * odd
    has_other = (other >= 0) & (other < seq)
    pl.semaphore_signal(barrier, inc=1, device_id={"seq": pair}, device_id_type=MESH)

    @pl.when(has_other)
    def _():
        pl.semaphore_signal(barrier, inc=1, device_id={"seq": other}, device_id_type=MESH)

        pl.semaphore_wait(barrier, dp + 1)

    @pl.when(jnp.logical_not(has_other))
    def _():
        pl.semaphore_wait(barrier, dp)

    gains = [
        pltpu.make_async_remote_copy(
            src_ref=gain_ref,
            dst_ref=gbuf.at[me],
            send_sem=g_send.at[off],
            recv_sem=g_recv.at[off],
            device_id={"dp": me ^ off},
            device_id_type=MESH,
        )
        for off in range(1, dp)
    ]
    for g in gains:
        g.start()
    turned = bits[1:] + bits[:1]
    jobs = [
        Gather(me, place, turned if i in (1, 2, 5) else bits, w_in[i], w_out[i], send.at[i], recv.at[i])
        for i in range(7)
    ]
    first = jobs[:3]
    job_o, job_g, job_u, job_d = jobs[3:]
    for job in first:
        job.begin()

    def own_out(i):
        rows = w_in[i].shape[0]
        return pltpu.make_async_copy(stage[i], w_out[i].at[pl.ds(pl.multiple_of(me * rows, 8), rows)], own_sem.at[i])

    for i in range(7):
        pltpu.make_async_copy(w_in[i], stage[i], own_sem.at[i]).wait()
        own_out(i).start()

    gbuf[me] = gain_ref[...]
    x = x_ref[...].astype(F32)
    scale = lax.rsqrt(jnp.mean(x * x, axis=1, keepdims=True) + EPS)
    for g in gains:
        g.wait_recv()
    for k in range(dp):
        gains_ref[:, k * block : (k + 1) * block] = gbuf[k, :, :block]
    n1_ref[...] = (x * scale * gains_ref[0:1, :]).astype(BF)

    def keep(i):
        return pltpu.make_async_copy(made[i], kept[i], keep_sem.at[i])

    def put_left(which, source):
        @pl.loop(0, model // TILE)
        def _(t):
            at = pl.multiple_of(t * TILE, 128)
            lefts[pl.ds(pl.multiple_of(which * model + at, 16), TILE), :] = source[:, pl.ds(at, TILE)].T

    for job in first:
        job.forward()
    job_o.begin()
    job_g.begin()
    for job in first:
        job.cross()
    for job in first:
        job.share()
    for i in range(7):
        own_out(i).wait()
    for job in first:
        job.finish()
    loads = [
        pltpu.make_async_copy(w_out[i], ref, load_sem.at[i]) for i, ref in enumerate((wq, wk, wv))
    ]
    for load in loads:
        load.start()

    def turn(value):
        ahead = pltpu.roll(value, TILE - HEAD_DIM // 2, 1)
        behind = pltpu.roll(value, HEAD_DIM // 2, 1)
        return value * cos_ref[...] + behind * second_ref[...] - ahead * first_ref[...]

    kvd = wk.shape[1]
    loads[1].wait()

    @pl.loop(0, kvd // TILE)
    def _(t):
        at = pl.multiple_of(t * TILE, 128)
        kvbuf[0, :, pl.ds(at, TILE)] = turn(nn(n1_ref[...], wk[:, pl.ds(at, TILE)])).astype(BF)

    loads[2].wait()

    @pl.loop(0, kvd // TILE)
    def _(t):
        at = pl.multiple_of(t * TILE, 128)
        kvbuf[0, :, pl.ds(kvd + at, TILE)] = nn(n1_ref[...], wv[:, pl.ds(at, TILE)]).astype(BF)

    def kv_copy(r):
        return pltpu.make_async_remote_copy(
            src_ref=kvbuf.at[r],
            dst_ref=kvbuf.at[r + 1],
            send_sem=kv_send.at[r],
            recv_sem=kv_recv.at[r],
            device_id={"seq": up},
            device_id_type=MESH,
        )

    def kv_send_on(r):
        @pl.when((place >= r) & (place < seq - 1))
        def _():
            kv_copy(r).start()

    def kv_wait(r):
        @pl.when(place >= r)
        def _():
            pltpu.make_async_remote_copy(
                src_ref=kvbuf.at[r - 1],
                dst_ref=kvbuf.at[r],
                send_sem=kv_send.at[r - 1],
                recv_sem=kv_recv.at[r - 1],
                device_id={"seq": down},
                device_id_type=MESH,
            ).wait_recv()

    kv_send_on(0)
    loads[0].wait()

    @pl.loop(0, model // TILE)
    def _(t):
        at = pl.multiple_of(t * TILE, 128)
        q = turn(nn(n1_ref[...], wq[:, pl.ds(at, TILE)])).astype(BF)
        for i in range(TILE // HEAD_DIM):
            qh[t * (TILE // HEAD_DIM) + i] = q[:, i * HEAD_DIM : (i + 1) * HEAD_DIM]

    def split_heads(r):
        for g in range(KV_HEADS):
            kh[g, r * tokens : (r + 1) * tokens, :] = kvbuf[r, :, g * HEAD_DIM : (g + 1) * HEAD_DIM]
            vh[g, r * tokens : (r + 1) * tokens, :] = kvbuf[r, :, kvd + g * HEAD_DIM : kvd + (g + 1) * HEAD_DIM]

    job_o.forward()
    job_u.begin()
    split_heads(0)
    for r in range(1, seq):
        kv_wait(r)
        if r < seq - 1:
            kv_send_on(r)
        if r == 1:
            job_o.cross()
            job_g.forward()
            job_d.begin()
            job_o.share()
        split_heads(r)
    job_g.cross()

    row = lax.broadcasted_iota(jnp.int32, (tokens, tokens), 0)
    col = lax.broadcasted_iota(jnp.int32, (tokens, tokens), 1)
    lse_ref[...] = jnp.zeros_like(lse_ref)
    lane = lax.broadcasted_iota(jnp.int32, (tokens, 128), 1)

    half = HEADS // 2

    def attend_heads(start, stop):
        @pl.loop(start, stop)
        def _(h):
            g = h // GROUP
            q = qh[h]
            scores = []
            for r in range(seq):
                s = nt(q, kh[g, r * tokens : (r + 1) * tokens, :]) * SCALE
                scores.append(jnp.where(col <= row if r == 0 else place >= r, s, NEG))
            top = functools.reduce(jnp.maximum, [jnp.max(s, axis=1, keepdims=True) for s in scores])
            weights = [jnp.exp(s - top) for s in scores]
            total = sum(jnp.sum(w, axis=1, keepdims=True) for w in weights)
            inverse = 1.0 / total
            oh[h] = sum(
                nn((w * inverse).astype(BF), vh[g, r * tokens : (r + 1) * tokens, :])
                for r, w in enumerate(weights)
            ).astype(BF)
            lse_ref[...] += jnp.where(lane == h, top + jnp.log(total), 0.0)

    attend_heads(0, half)
    job_g.share()
    job_u.forward()
    attend_heads(half, HEADS)
    for i in range(3):
        keep(i).start()
    for h in range(HEADS):
        o_ref[:, h * HEAD_DIM : (h + 1) * HEAD_DIM] = oh[h]

    job_o.finish()
    load_o = pltpu.make_async_copy(w_out[3], wq, load_sem.at[0])
    load_o.start()
    put_left(2, n1_ref)
    put_left(1, o_ref)
    load_o.wait()

    @pl.loop(0, model // TILE)
    def _(t):
        at = pl.multiple_of(t * TILE, 128)
        x2_ref[:, pl.ds(at, TILE)] = x_ref[:, pl.ds(at, TILE)].astype(F32) + nn(o_ref[...], wq[:, pl.ds(at, TILE)])

    x2 = x2_ref[...]
    n2_ref[...] = (x2 * lax.rsqrt(jnp.mean(x2 * x2, axis=1, keepdims=True) + EPS) * gains_ref[1:2, :]).astype(BF)
    put_left(0, n2_ref)
    for i in (3, 4):
        keep(i).start()

    def project(weight, take):
        panels = weight.shape[1] // COLS

        def panel(t):
            at = pl.multiple_of(t * COLS, 128)
            return pltpu.make_async_copy(weight.at[:, pl.ds(at, COLS)], wt.at[t % 2], tile_sem.at[t % 2])

        panel(0).start()

        @pl.loop(0, panels)
        def _(t):
            panel(t).wait()

            @pl.when(t + 1 < panels)
            def _():
                panel(t + 1).start()

            take(pl.multiple_of(t * COLS, 128), nn(n2_ref[...], wt[t % 2]))

    def take_gate(at, gate):
        swish[:, pl.ds(at, COLS)] = gate

    def take_up(at, up):
        gate = swish[:, pl.ds(at, COLS)]
        sig = jax.nn.sigmoid(gate)
        act = gate * sig
        value = (act * up).astype(BF)
        hidden[:, pl.ds(at, COLS)] = value
        hidden_t[pl.ds(at, COLS), :] = value.T
        slope[:, pl.ds(at, COLS)] = up * sig * (1.0 + gate * (1.0 - sig))
        swish[:, pl.ds(at, COLS)] = act

    job_u.cross()
    job_d.forward()
    job_g.finish()
    project(w_out[4], take_gate)
    job_u.share()
    job_u.finish()
    project(w_out[5], take_up)
    for i in range(5, 9):
        keep(i).start()
    job_d.cross()
    job_d.share()
    job_d.finish()
    for i in range(9):
        keep(i).wait()
    for r in range(seq - 1):

        @pl.when((place >= r) & (place < seq - 1))
        def _():
            kv_copy(r).wait_send()

    for g in gains:
        g.wait_send()
    for job in jobs:
        job.drain()


def forward_call(dp, seq, x, gains, tables, weights):
    tokens, model = x.shape
    chip_bits = dp.bit_length() - 2
    copies = gather_copies(chip_bits)
    anyspec = pl.BlockSpec(memory_space=pl.ANY)
    vmem = pl.BlockSpec(memory_space=pltpu.VMEM)
    out_shape = [jax.ShapeDtypeStruct((dp * w.shape[0], w.shape[1]), BF) for w in weights]
    heads = jax.ShapeDtypeStruct((HEADS, tokens, HEAD_DIM), BF)
    keys = jax.ShapeDtypeStruct((KV_HEADS, seq * tokens, HEAD_DIM), BF)
    kvd, ff = weights[1].shape[1], weights[4].shape[1]
    made = [
        heads,
        keys,
        keys,
        jax.ShapeDtypeStruct((3 * model, tokens), BF),
        jax.ShapeDtypeStruct((tokens, model), F32),
        jax.ShapeDtypeStruct((tokens, ff), BF),
        jax.ShapeDtypeStruct((ff, tokens), BF),
        jax.ShapeDtypeStruct((tokens, ff), F32),
        jax.ShapeDtypeStruct((tokens, ff), F32),
    ]
    out_shape += made + [jax.ShapeDtypeStruct((tokens, 128), F32), jax.ShapeDtypeStruct((8, model), F32)]
    line = pltpu.VMEM((tokens, model), BF)
    dma = pltpu.SemaphoreType.DMA
    return pl.pallas_call(
        functools.partial(forward_body, dp, seq),
        out_shape=out_shape,
        in_specs=[vmem] * 5 + [anyspec] * 7,
        out_specs=[anyspec] * 16 + [vmem] * 2,
        scratch_shapes=[pltpu.VMEM(a.shape, a.dtype) for a in made]
        + [pltpu.VMEM(w.shape, BF) for w in weights]
        + [
            pltpu.VMEM((model, model), BF),
            pltpu.VMEM((model, kvd), BF),
            pltpu.VMEM((model, kvd), BF),
            pltpu.VMEM((seq, tokens, model), BF),
            pltpu.VMEM((dp, 8, 256), F32),
            pltpu.VMEM((HEADS, tokens, HEAD_DIM), BF),
            line,
            line,
            line,
            pltpu.VMEM((2, model, COLS), BF),
            dma((7, copies)),
            dma((7, copies)),
            dma((seq,)),
            dma((seq,)),
            dma((dp,)),
            dma((dp,)),
            dma((7,)),
            dma((3,)),
            dma((2,)),
            dma((9,)),
        ],
        compiler_params=pltpu.CompilerParams(
            collective_id=0, has_side_effects=True, vmem_limit_bytes=60 * 1024 * 1024
        ),
        name="forward",
    )(x, gains, *tables, *weights)


def head_column(lse, h):
    lane = lax.broadcasted_iota(jnp.int32, lse.shape, 1)
    return jnp.sum(jnp.where(lane == h, lse, 0.0), axis=1, keepdims=True)


def back_group(place, chunks, g, slot, q_ref, do_ref, lse, k, v, dq_ref, dk_ref, dv_ref, acc_k, acc_v):
    tokens = q_ref.shape[1]
    row = lax.broadcasted_iota(jnp.int32, (tokens, tokens), 0)
    col = lax.broadcasted_iota(jnp.int32, (tokens, tokens), 1)
    for i in range(GROUP):
        h = GROUP * g + i
        q, do = q_ref[h], do_ref[h]
        total = head_column(lse, h)
        probs, dprobs = [], []
        for r in range(chunks):
            span = slice(r * tokens, (r + 1) * tokens)
            s = nt(q, k[span, :]) * SCALE
            s = jnp.where(col <= row if r == 0 else place >= r, s, NEG)
            probs.append(jnp.exp(s - total))
            dprobs.append(nt(do, v[span, :]))
        inner = sum(jnp.sum(p * d, axis=1, keepdims=True) for p, d in zip(probs, dprobs))
        dq = jnp.zeros((tokens, HEAD_DIM), F32)
        for r in range(chunks):
            span = slice(r * tokens, (r + 1) * tokens)
            ds = (probs[r] * (dprobs[r] - inner)).astype(BF)
            dq += nn(ds, k[span, :])
            dk = tn(ds, q)
            dv = tn(probs[r].astype(BF), do)
            if i == 0:
                acc_k[span, :] = dk
                acc_v[span, :] = dv
            else:
                dk_ref[slot, span, :] = ((acc_k[span, :] + dk) * SCALE).astype(BF)
                dv_ref[slot, span, :] = (acc_v[span, :] + dv).astype(BF)
        dq_ref[h] = (dq * SCALE).astype(BF)


LAG_B, LAG_C, LAG_D = 1, 3, 5
SLOTS_CORE, SLOTS, SLOTS_SUM, SLOTS_OUT = 2, 4, 10, 8


def backward_body(seq, x_ref, gains_ref, x2_ref, cos_ref, first_ref, second_ref, hidden_ref, eb_ref, lefts_ref,
                  qh, kh, vh, lse_ref, wq_in, wk_in, wv_in, wo_in, wg_in, wu_in, wd_in, hid_in, slope_in, swish_in, *refs):
    dx_ref, gain_out, out_ref, res = refs[:4]
    (rights, doh, dqh, dkh, dvh, acc_k, acc_v, dkv, dkv_in, dn1, wt, hid, slope, swish, term2,
     cs, cr, sums, r0, r1, zs, zr, zt, gsend, grecv, gsum, gzrecv,
     mid_sem, w_sem, core_s, core_r, s0_s, s0_r, s1_s, s1_r, z_s, z_r, a_s, a_r, t_sem, kv_s, kv_r,
     g_s, g_r, gz_s, gz_r, core_free, s0_free, s1_free, z_free) = refs[4:]
    me, place = lax.axis_index("dp"), lax.axis_index("seq")
    core, chip_x, chip_y = me % 2, (me // 2) % 2, me // 4
    tokens, model = x_ref.shape
    rows = model // 8
    sub = rows // seq
    kvd = wk_in.shape[1]
    d_rows = hidden_ref.shape[0] // 8
    d_chunks = d_rows * 3 // rows
    n_chunks = rights.shape[1] // COLS
    o_panels = model // COLS
    gu_panels = n_chunks - 3 * o_panels
    total_chunks = d_chunks + n_chunks

    def owner(x, y, c):
        return ((chip_y + y) % 2) * 4 + ((chip_x + x) % 2) * 2 + (core + c) % 2

    partner = owner(0, 0, 1)
    near = [[owner(1, 0, 0), owner(0, 1, 0)], [owner(0, 1, 0), owner(1, 0, 0)]]

    ff = wg_in.shape[1]
    part_d = COLS // 2

    def mid_loads(k):
        s = k % 2
        at = pl.multiple_of(k * COLS, 128)
        pairs = [
            (wd_in.at[pl.ds(at, part_d)], wt.at[s, pl.ds(0, part_d), pl.ds(0, model)]),
            (wd_in.at[pl.ds(at + part_d, part_d)], wt.at[s, pl.ds(0, part_d), pl.ds(model, model)]),
            (hid_in.at[:, pl.ds(at, COLS)], hid.at[s]),
            (slope_in.at[:, pl.ds(at, COLS)], slope.at[s]),
            (swish_in.at[:, pl.ds(at, COLS)], swish.at[s]),
        ]
        return [pltpu.make_async_copy(a, b, mid_sem.at[s, i]) for i, (a, b) in enumerate(pairs)]

    def ff_load(j, i):
        return pltpu.make_async_copy(
            (wg_in, wu_in)[i].at[pl.ds(pl.multiple_of(j * TILE, 16), TILE)], wt.at[i, :, pl.ds(0, ff)], w_sem.at[i, 0]
        )

    def o_load(t):
        return pltpu.make_async_copy(
            wo_in.at[pl.ds(t * TILE, TILE)], wt.at[t % 2, :, pl.ds(t // 2 * model, model)], w_sem.at[t % 2, t // 2]
        )

    for k in range(2):
        for made in mid_loads(k):
            made.start()
    out_ref[...] = x2_ref[...]

    barrier = pltpu.get_barrier_semaphore()
    for off in range(1, 8):
        pl.semaphore_signal(barrier, inc=1, device_id={"dp": me ^ off}, device_id_type=MESH)
    for far in range(1, seq):
        to = (place + far) % seq
        pl.semaphore_signal(barrier, inc=1, device_id={"seq": to}, device_id_type=MESH)
    pl.semaphore_wait(barrier, 7 + seq - 1)

    def remote(src, dst, send, recv, **target):
        return pltpu.make_async_remote_copy(
            src_ref=src, dst_ref=dst, send_sem=send, recv_sem=recv, device_id=target, device_id_type=MESH
        )

    def signal(sem, **target):
        pl.semaphore_signal(sem, inc=1, device_id=target, device_id_type=MESH)

    def core_copy(c):
        s = c % SLOTS_CORE
        return remote(cs.at[s], cr.at[s], core_s.at[s], core_r.at[s], dp=partner)

    def first_copy(c, parity):
        s = c % SLOTS
        return remote(sums.at[c % SLOTS_SUM, pl.ds(2 * rows, 2 * rows)], r0.at[s], s0_s.at[s], s0_r.at[s], dp=near[parity][0])

    def second_copy(c, parity):
        s = c % SLOTS
        return remote(sums.at[c % SLOTS_SUM, pl.ds(rows, rows)], r1.at[s], s1_s.at[s], s1_r.at[s], dp=near[parity][1])

    def offsets(index, parity):
        low, high = index % 2, index // 2
        return (high, low) if parity == 0 else (low, high)

    def stage_a(c, parity):
        s, t = c % SLOTS_CORE, c % SLOTS_SUM

        @pl.when(c >= SLOTS_CORE)
        def _():
            core_copy(c).wait_send()

        def put(away, term):
            @pl.loop(0, 4)
            def _(index):
                dx, dy = offsets(index, parity)
                at = pl.multiple_of(index * rows, 16)
                if away:
                    cs[s, pl.ds(at, rows), :] = term(owner(dx, dy, 1)).astype(BF)
                else:
                    sums[t, pl.ds(at, rows), :] = term(owner(dx, dy, 0)).astype(BF)

        def term_d(who):
            size = rows // 3
            at = pl.multiple_of(who * d_rows + c * size, 16)
            left = hidden_ref[pl.ds(at, size), :]
            return jnp.concatenate(
                [nn(left, eb_ref[:, i * COLS : (i + 1) * COLS]) for i in range(3)], axis=0
            )

        k = c - d_chunks
        which = (k >= gu_panels).astype(jnp.int32) + (k >= gu_panels + o_panels).astype(jnp.int32)

        def term_n(who):
            left = lefts_ref[pl.ds(pl.multiple_of(which * model + who * rows, 16), rows), :]
            return nn(left, rights[:, pl.ds(pl.multiple_of(k * COLS, 128), COLS)])

        def both(term):
            put(True, term)

            @pl.when(c >= SLOTS_CORE)
            def _():
                pl.semaphore_wait(core_free, 1)

            core_copy(c).start()
            put(False, term)

        @pl.when(c < d_chunks)
        def _():
            both(term_d)

        @pl.when(c >= d_chunks)
        def _():
            both(term_n)

    def add_rows(count, target, extra):
        @pl.loop(0, count // 64)
        def _(i):
            at = pl.multiple_of(i * 64, 16)
            target[pl.ds(at, 64), :] = (target[pl.ds(at, 64), :].astype(F32) + extra[pl.ds(at, 64), :].astype(F32)).astype(BF)

    def stage_b(c, parity):
        core_copy(c).wait_recv()
        add_rows(4 * rows, sums.at[c % SLOTS_SUM], cr.at[c % SLOTS_CORE])

        @pl.when(c < total_chunks - SLOTS_CORE)
        def _():
            signal(core_free, dp=partner)

        @pl.when(c >= SLOTS)
        def _():
            pl.semaphore_wait(s0_free.at[parity], 1)

        first_copy(c, parity).start()

    def stage_c(c, parity):
        first_copy(c, parity).wait_recv()
        add_rows(2 * rows, sums.at[c % SLOTS_SUM], r0.at[c % SLOTS])

        @pl.when(c < total_chunks - SLOTS)
        def _():
            signal(s0_free.at[parity], dp=near[parity][0])

        @pl.when(c >= SLOTS)
        def _():
            pl.semaphore_wait(s1_free.at[parity], 1)

        second_copy(c, parity).start()
        first_copy(c, parity).wait_send()

    def stage_d(c, parity):
        second_copy(c, parity).wait_recv()
        add_rows(rows, sums.at[c % SLOTS_SUM], r1.at[c % SLOTS])

        @pl.when(c < total_chunks - SLOTS)
        def _():
            signal(s1_free.at[parity], dp=near[parity][1])

        second_copy(c, parity).wait_send()

    def step_of(way):
        return 1 - 2 * way

    def inside(at):
        return (at >= 0) & (at < seq)

    def z_copy(c, way, hop):
        s = c % SLOTS
        slot = way * (seq - 1) + hop - 1
        return remote(zs.at[slot, s], zr.at[slot, s], z_s.at[slot, s], z_r.at[slot, s], seq=place + step_of(way))

    def z_sends(way, hop):
        return inside(place + step_of(way) * (seq - hop))

    def z_gets(way, hop):
        return inside(place - step_of(way)) & inside(place - step_of(way) + step_of(way) * (seq - hop))

    def part(c, index):
        index = jnp.minimum(jnp.maximum(index, 0), seq - 1)
        return sums[c % SLOTS_SUM, pl.ds(pl.multiple_of(index * sub, 16), sub), :].astype(F32)

    def z_take(c, way, hop):
        slot = way * (seq - 1) + hop - 1
        gets = z_gets(way, hop)

        @pl.when(gets)
        def _():
            z_copy(c, way, hop).wait_recv()

        return jnp.where(gets, zr[slot, c % SLOTS].astype(F32), 0.0)

    def z_release(c, way, hop):
        slot = way * (seq - 1) + hop - 1

        @pl.when(z_gets(way, hop) & (c < total_chunks - SLOTS))
        def _():
            signal(z_free.at[slot], seq=place - step_of(way))

    def stage_z(c, hop):
        for way in range(2):
            slot = way * (seq - 1) + hop - 1
            value = part(c, place + step_of(way) * (seq - hop))
            if hop > 1:
                value = value + z_take(c, way, hop - 1)
            sends = z_sends(way, hop)

            @pl.when(sends & (c >= SLOTS))
            def _():
                z_copy(c, way, hop).wait_send()

            zs[slot, c % SLOTS] = value.astype(BF)
            if hop > 1:
                z_release(c, way, hop - 1)

            @pl.when(sends & (c >= SLOTS))
            def _():
                pl.semaphore_wait(z_free.at[slot], 1)

            @pl.when(sends)
            def _():
                z_copy(c, way, hop).start()

    def res_at(c, source):
        index = jnp.minimum(jnp.maximum(source, 0), seq - 1)
        return res.at[pl.ds(pl.multiple_of(c * rows + index * sub, 16), sub)]

    def own_copy(c):
        s = c % SLOTS_OUT
        return pltpu.make_async_copy(zt.at[s], res_at(c, place), t_sem.at[s])

    def a_copy(c, way, hop):
        s = c % SLOTS_OUT
        slot = way * (seq - 1) + hop - 1
        source = place - step_of(way) * (hop - 1)
        src = zt.at[s] if hop == 1 else res_at(c, source)
        return remote(src, res_at(c, source), a_s.at[slot, s], a_r.at[slot, s], seq=place + step_of(way))

    def a_sends(way, hop):
        return inside(place + step_of(way)) & inside(place - step_of(way) * (hop - 1))

    def a_gets(way, hop):
        return inside(place - step_of(way) * hop)

    def stage_total(c):
        value = part(c, place)
        for way in range(2):
            value = value + z_take(c, way, seq - 1)

        @pl.when(c >= SLOTS_OUT)
        def _():
            own_copy(c).wait()

        for way in range(2):
            @pl.when((c >= SLOTS_OUT) & a_sends(way, 1))
            def _():
                a_copy(c, way, 1).wait_send()

        zt[c % SLOTS_OUT] = value.astype(BF)
        for way in range(2):
            z_release(c, way, seq - 1)
        own_copy(c).start()
        stage_out(c, 1)

    def stage_out(c, hop):
        for way in range(2):
            if hop > 1:
                @pl.when(a_gets(way, hop - 1))
                def _():
                    a_copy(c, way, hop - 1).wait_recv()

            if hop < seq:
                if hop > 1:
                    @pl.when((c >= SLOTS_OUT) & a_sends(way, hop))
                    def _():
                        a_copy(c, way, hop).wait_send()

                @pl.when(a_sends(way, hop))
                def _():
                    a_copy(c, way, hop).start()

    lag_total = LAG_D + seq - 1
    stages = [(LAG_B, stage_b), (LAG_C, stage_c), (LAG_D, stage_d), (LAG_D, lambda c, parity: stage_z(c, 1))]
    stages += [(LAG_D + hop - 1, lambda c, parity, hop=hop: stage_z(c, hop)) for hop in range(2, seq)]
    stages += [(lag_total, lambda c, parity: stage_total(c))]
    stages += [(lag_total + hop - 1, lambda c, parity, hop=hop: stage_out(c, hop)) for hop in range(2, seq + 1)]
    last_lag = lag_total + seq - 1

    def tick(c, parity):
        for lag, stage in sorted(stages, key=lambda pair: -pair[0]):
            then = c - lag

            @pl.when((then >= 0) & (then < total_chunks))
            def _():
                stage(then, (parity + lag) % 2)

        @pl.when(c < total_chunks)
        def _():
            stage_a(c, parity)

    pair_width = 2 * HEAD_DIM

    def kv_copy(r, i):
        return remote(dkv.at[r, i], dkv_in.at[r - 1, i], kv_s.at[r, i], kv_r.at[r, i], seq=place - 1)

    def kv_send(r, i):
        @pl.when(place >= r)
        def _():
            kv_copy(r, i).start()

    def kv_take(r, i):
        gets = (place + 1 >= r) & (place + 1 < seq)

        @pl.when(gets)
        def _():
            kv_copy(r, i).wait_recv()
            add_rows(tokens, dkv.at[r - 1, i], dkv_in.at[r - 1, i])

    def mid_down(k):
        s = k % 2
        at = pl.multiple_of(k * COLS, 128)
        for made in mid_loads(k):
            made.wait()
        for half in range(2):
            lo = half * part_d
            dh = nt(eb_ref[...], wt[s, :part_d, half * model : (half + 1) * model])
            rights[:, pl.ds(at + lo, part_d)] = (dh * slope[s, :, lo : lo + part_d]).astype(BF)
            rights[:, pl.ds(ff + at + lo, part_d)] = (dh * swish[s, :, lo : lo + part_d]).astype(BF)
        for j in range(model // COLS):
            span = slice(j * COLS, (j + 1) * COLS)
            out_ref[:, span] += sum(
                nn(
                    hid[s, :, half * part_d : (half + 1) * part_d],
                    wt[s, :part_d, half * model + j * COLS : half * model + (j + 1) * COLS],
                )
                for half in range(2)
            )

        @pl.when(k + 2 < ff // COLS)
        def _():
            for made in mid_loads(k + 2):
                made.start()

    def mid_ff(j):
        at = pl.multiple_of(j * TILE, 128)
        for i in range(2):
            ff_load(j, i).wait()
        dn1[:, pl.ds(at, TILE)] = nt(rights[:, :ff], wt[0, :, :ff]) + nt(rights[:, ff : 2 * ff], wt[1, :, :ff])

        @pl.when(j + 1 < model // TILE)
        def _():
            for i in range(2):
                ff_load(j + 1, i).start()

    def mid_out():
        x2 = x2_ref[...]
        scale = lax.rsqrt(jnp.mean(x2 * x2, axis=1, keepdims=True) + EPS)
        unit = x2 * scale
        grad = dn1[...]
        term2[0:1, :] = jnp.sum(grad * unit, axis=0, keepdims=True)
        scaled = grad * gains_ref[1:2, :]
        inner = jnp.mean(scaled * unit, axis=1, keepdims=True)
        e2 = eb_ref[...].astype(F32) + scale * (scaled - unit * inner)
        dx_ref[...] = e2
        rights[:, 2 * ff : 2 * ff + model] = e2.astype(BF)
        for t in range(model // TILE):
            o_load(t).wait()
            do = nt(rights[:, 2 * ff : 2 * ff + model], wt[t % 2, :, t // 2 * model : (t // 2 + 1) * model]).astype(BF)
            for i in range(TILE // HEAD_DIM):
                doh[t * (TILE // HEAD_DIM) + i] = do[:, i * HEAD_DIM : (i + 1) * HEAD_DIM]

    def turn_back(value):
        ahead = pltpu.roll(value, TILE - HEAD_DIM // 2, 1)
        behind = pltpu.roll(value, HEAD_DIM // 2, 1)
        return (value * cos_ref[...] - behind * second_ref[...] + ahead * first_ref[...]).astype(BF)

    q_at = (gu_panels + o_panels) * COLS

    def w_load(t, i):
        at = pl.multiple_of(t * TILE, 16)
        s = t % 2
        src, lo, width = ((wq_in, 0, model), (wk_in, model, kvd), (wv_in, model + kvd, kvd))[i]
        return pltpu.make_async_copy(src.at[pl.ds(at, TILE)], wt.at[s, :, pl.ds(lo, width)], w_sem.at[s, i])

    def last_norm():
        for h in range(HEADS):
            rights[:, q_at + h * HEAD_DIM : q_at + (h + 1) * HEAD_DIM] = dqh[h]
        for t in range(model // TILE):
            at = q_at + t * TILE
            rights[:, at : at + TILE] = turn_back(rights[:, at : at + TILE].astype(F32))
        for t in range(kvd // TILE):
            at = q_at + model + t * TILE
            pieces = [dkv[0, 2 * t + i, :, :pair_width] for i in range(2)]
            rights[:, at : at + TILE] = turn_back(jnp.concatenate(pieces, axis=1).astype(F32))
        for i in range(KV_HEADS // 2):
            at = q_at + model + kvd + i * pair_width
            rights[:, at : at + pair_width] = dkv[0, i, :, pair_width:]
        for i in range(3):
            w_load(0, i).start()

        @pl.loop(0, model // TILE)
        def _(t):
            for i in range(3):
                w_load(t, i).wait()

            @pl.when(t + 1 < model // TILE)
            def _():
                for i in range(3):
                    w_load(t + 1, i).start()

            dn1[:, pl.ds(pl.multiple_of(t * TILE, 128), TILE)] = nt(rights[:, q_at:], wt[t % 2, :, : model + 2 * kvd])

        x = x_ref[...].astype(F32)
        scale = lax.rsqrt(jnp.mean(x * x, axis=1, keepdims=True) + EPS)
        unit = x * scale
        grad = dn1[...]
        term = jnp.sum(grad * unit, axis=0, keepdims=True)
        scaled = grad * gains_ref[0:1, :]
        inner = jnp.mean(scaled * unit, axis=1, keepdims=True)
        dx_ref[...] += scale * (scaled - unit * inner)
        for k in range(8):
            gsend[k, 0:1, :rows] = term[:, k * rows : (k + 1) * rows]
            gsend[k, 1:2, :rows] = term2[0:1, k * rows : (k + 1) * rows]

    def gain_copies():
        return [
            remote(gsend.at[me ^ off], grecv.at[me], g_s.at[off], g_r.at[off], dp=me ^ off) for off in range(1, 8)
        ]

    def gain_line():
        return [
            remote(gsum, gzrecv.at[place], gz_s.at[far], gz_r.at[far], seq=(place + far) % seq) for far in range(1, seq)
        ]

    ticks = total_chunks + last_lag
    pairs = KV_HEADS // 2
    d_steps, f_steps = ff // COLS, model // TILE
    d_ticks = d_steps // 2
    out_at = (d_ticks + f_steps) // 2
    first_at = out_at + 1
    norm_at = first_at + pairs + seq - 2
    assert d_ticks <= d_chunks and 2 * norm_at + 1 < total_chunks - 2 * o_panels

    @pl.loop(0, -(-ticks // 2))
    def _(p):
        for parity in range(2):
            c = 2 * p + parity
            tick(c, parity)

            @pl.when(c < d_ticks)
            def _():
                @pl.loop(0, 2)
                def _(i):
                    mid_down(2 * c + i)

            @pl.when(c == d_ticks - 1)
            def _():
                for i in range(2):
                    ff_load(0, i).start()

            @pl.when((c >= d_ticks) & (c < d_ticks + f_steps))
            def _():
                mid_ff(c - d_ticks)

        @pl.when(p == out_at - 1)
        def _():
            for t in range(f_steps):
                o_load(t).start()

        @pl.when(p == out_at)
        def _():
            mid_out()

        for r in range(seq - 1, 0, -1):
            piece = p - first_at - (seq - r)

            @pl.when((piece >= 0) & (piece < pairs))
            def _():
                kv_take(r, piece)
                if r > 1:
                    kv_send(r - 1, piece)

        @pl.when((p >= first_at) & (p < first_at + pairs))
        def _():
            piece = p - first_at
            for i in range(2):
                g = 2 * piece + i
                back_group(place, seq, g, i, qh, doh, lse_ref[...], kh.at[g], vh.at[g], dqh, dkh, dvh, acc_k, acc_v)
            for r in range(seq):
                for i in range(2):
                    span = slice(r * tokens, (r + 1) * tokens)
                    dkv[r, piece, :, i * HEAD_DIM : (i + 1) * HEAD_DIM] = dkh[i, span, :]
                    lo = pair_width + i * HEAD_DIM
                    dkv[r, piece, :, lo : lo + HEAD_DIM] = dvh[i, span, :]
            kv_send(seq - 1, piece)

        @pl.when(p == norm_at)
        def _():
            last_norm()
            for made in gain_copies():
                made.start()
            grecv[me] = gsend[me]

        @pl.when(p == norm_at + 1)
        def _():
            for made in gain_copies():
                made.wait_recv()
            gsum[...] = sum(grecv[k] for k in range(1, 8)) + grecv[0]
            gzrecv[place] = gsum[...]
            for made in gain_line():
                made.start()

        @pl.when(p == norm_at + 2)
        def _():
            for made in gain_line():
                made.wait_recv()
            gain_out[...] = sum(gzrecv[k] for k in range(seq))

    for made in gain_copies() + gain_line():
        made.wait_send()
    for r in range(1, seq):
        @pl.when(place >= r)
        def _():
            for i in range(pairs):
                kv_copy(r, i).wait_send()
    for c in range(total_chunks - SLOTS_CORE, total_chunks):
        core_copy(c).wait_send()
    for way in range(2):
        for hop in range(1, seq):
            for c in range(total_chunks - SLOTS, total_chunks):
                @pl.when(z_sends(way, hop))
                def _():
                    z_copy(c, way, hop).wait_send()
            for c in range(total_chunks - SLOTS_OUT, total_chunks):
                @pl.when(a_sends(way, hop))
                def _():
                    a_copy(c, way, hop).wait_send()
    for c in range(total_chunks - SLOTS_OUT, total_chunks):
        own_copy(c).wait()


def backward_call(seq, x, gains, x2, tables, hidden_t, eb, lefts, qh, kh, vh, lse, weights, hidden, slope, swish):
    tokens, model = x.shape
    rows = model // 8
    sub = rows // seq
    kvd, ff = weights[1].shape[1], hidden.shape[1]
    wide = 2 * ff + 2 * model + 2 * kvd
    chunks = hidden_t.shape[0] // 8 * 3 // rows + wide // COLS
    anyspec = pl.BlockSpec(memory_space=pl.ANY)
    vmem = pl.BlockSpec(memory_space=pltpu.VMEM)
    dma, regular = pltpu.SemaphoreType.DMA, pltpu.SemaphoreType.REGULAR
    hops = 2 * (seq - 1)
    heads = pltpu.VMEM((HEADS, tokens, HEAD_DIM), BF)
    keys = pltpu.VMEM((2, seq * tokens, HEAD_DIM), BF)
    panel = pltpu.VMEM((2, tokens, COLS), F32)
    pieces = KV_HEADS // 2
    return pl.pallas_call(
        functools.partial(backward_body, seq),
        out_shape=[
            jax.ShapeDtypeStruct((tokens, model), F32),
            jax.ShapeDtypeStruct((8, 256), F32),
            jax.ShapeDtypeStruct((tokens, model), F32),
            jax.ShapeDtypeStruct((chunks * rows, COLS), BF),
        ],
        in_specs=[vmem] * 13 + [anyspec] * 10,
        out_specs=[vmem, vmem, vmem, anyspec],
        scratch_shapes=[
            pltpu.VMEM((tokens, wide), BF),
            heads, heads, keys, keys,
            pltpu.VMEM((seq * tokens, HEAD_DIM), F32),
            pltpu.VMEM((seq * tokens, HEAD_DIM), F32),
            pltpu.VMEM((seq, pieces, tokens, 4 * HEAD_DIM), BF),
            pltpu.VMEM((seq - 1, pieces, tokens, 4 * HEAD_DIM), BF),
            pltpu.VMEM((tokens, model), F32),
            pltpu.VMEM((2, TILE, max(ff, 2 * model)), BF),
            pltpu.VMEM((2, tokens, COLS), BF),
            panel, panel,
            pltpu.VMEM((8, model), F32),
            pltpu.VMEM((SLOTS_CORE, 4 * rows, COLS), BF),
            pltpu.VMEM((SLOTS_CORE, 4 * rows, COLS), BF),
            pltpu.VMEM((SLOTS_SUM, 4 * rows, COLS), BF),
            pltpu.VMEM((SLOTS, 2 * rows, COLS), BF),
            pltpu.VMEM((SLOTS, rows, COLS), BF),
            pltpu.VMEM((hops, SLOTS, sub, COLS), BF),
            pltpu.VMEM((hops, SLOTS, sub, COLS), BF),
            pltpu.VMEM((SLOTS_OUT, sub, COLS), BF),
            pltpu.VMEM((8, 8, 256), F32),
            pltpu.VMEM((8, 8, 256), F32),
            pltpu.VMEM((8, 256), F32),
            pltpu.VMEM((seq, 8, 256), F32),
            dma((2, 5)), dma((2, 3)),
            dma((SLOTS_CORE,)), dma((SLOTS_CORE,)),
            dma((SLOTS,)), dma((SLOTS,)),
            dma((SLOTS,)), dma((SLOTS,)),
            dma((hops, SLOTS)), dma((hops, SLOTS)),
            dma((hops, SLOTS_OUT)), dma((hops, SLOTS_OUT)),
            dma((SLOTS_OUT,)),
            dma((seq, pieces)), dma((seq, pieces)),
            dma((8,)), dma((8,)),
            dma((seq,)), dma((seq,)),
            regular, regular((2,)), regular((2,)), regular((hops,)),
        ],
        compiler_params=pltpu.CompilerParams(
            collective_id=1, has_side_effects=True, vmem_limit_bytes=62 * 1024 * 1024
        ),
        name="backward",
    )(x, gains, x2, *tables, hidden_t, eb, lefts, qh, kh, vh, lse, *weights, hidden, slope, swish)


def finish_call(res, dx, result, d_rows, ff, kvd):
    tokens, model = dx.shape
    block = res.shape[1]
    steps = 4
    per_d, per_f, per_m = d_rows * 3 // block // steps, ff // COLS // steps, model // COLS
    at_f = per_d * steps // per_f
    at_m = per_d * steps + 2 * per_f * steps
    panel = block // 3
    assert per_d and per_f and per_d * steps % per_f == 0 and per_m < steps

    def body(d_in, g_in, u_in, o_in, q_in, kv_in, dx_in, y_in, down, gate, up, out, query, key, value, dx_out, y_out):
        s = pl.program_id(0)
        dx_out[...] = dx_in[...]
        y_out[...] = y_in[...]
        for i in range(per_d):
            for j in range(3):
                down[i * panel : (i + 1) * panel, j * COLS : (j + 1) * COLS] = d_in[i, j * panel : (j + 1) * panel, :].astype(F32)
        for i in range(per_f):
            gate[:, i * COLS : (i + 1) * COLS] = g_in[i].astype(F32)
            up[:, i * COLS : (i + 1) * COLS] = u_in[i].astype(F32)
        for i in range(per_m):

            @pl.when(s == i)
            def _():
                out[:, i * COLS : (i + 1) * COLS] = o_in[0].astype(F32)
                query[:, i * COLS : (i + 1) * COLS] = q_in[0].astype(F32)
                mid = min(max(kvd - i * COLS, 0), COLS)
                if mid:
                    key[:, i * COLS : i * COLS + mid] = kv_in[0, :, :mid].astype(F32)
                if mid < COLS:
                    lo = i * COLS + mid - kvd
                    value[:, lo : lo + COLS - mid] = kv_in[0, :, mid:].astype(F32)

    def chunk(count, at):
        return pl.BlockSpec((count, block, COLS), at)

    wide = lambda base: chunk(per_f, lambda s: (base + s, 0, 0))
    thin = lambda base: chunk(1, lambda s: (base + jnp.minimum(s, per_m - 1), 0, 0))
    line = pl.BlockSpec((tokens // steps, model), lambda s: (s, 0))
    whole = lambda width: pl.BlockSpec((block, width), lambda s: (0, 0))
    return pl.pallas_call(
        body,
        grid=(steps,),
        in_specs=[
            chunk(per_d, lambda s: (s, 0, 0)),
            wide(at_f),
            wide(at_f + steps),
            thin(at_m),
            thin(at_m + per_m),
            thin(at_m + 2 * per_m),
            line,
            line,
        ],
        out_specs=[
            pl.BlockSpec((d_rows // steps, model), lambda s: (s, 0)),
            pl.BlockSpec((block, ff // steps), lambda s: (0, s)),
            pl.BlockSpec((block, ff // steps), lambda s: (0, s)),
            whole(model),
            whole(model),
            whole(kvd),
            whole(kvd),
            line,
            line,
        ],
        out_shape=[
            jax.ShapeDtypeStruct((d_rows, model), F32),
            jax.ShapeDtypeStruct((block, ff), F32),
            jax.ShapeDtypeStruct((block, ff), F32),
            jax.ShapeDtypeStruct((block, model), F32),
            jax.ShapeDtypeStruct((block, model), F32),
            jax.ShapeDtypeStruct((block, kvd), F32),
            jax.ShapeDtypeStruct((block, kvd), F32),
            jax.ShapeDtypeStruct((tokens, model), F32),
            jax.ShapeDtypeStruct((tokens, model), F32),
        ],
        compiler_params=pltpu.CompilerParams(vmem_limit_bytes=60 * 1024 * 1024),
        name="finish",
    )(*[res] * 6, dx, result)


def attend_back(place, qh, kh, vh, doh, lse):
    chunks = kh.shape[1] // qh.shape[1]

    def body(place_ref, q_ref, k_ref, v_ref, do_ref, lse_ref, dq_ref, dk_ref, dv_ref, acc_k, acc_v):
        @pl.loop(0, KV_HEADS)
        def _(g):
            back_group(place_ref[0], chunks, g, g, q_ref, do_ref, lse_ref[...], k_ref.at[g], v_ref.at[g], dq_ref, dk_ref, dv_ref, acc_k, acc_v)

    vmem = pl.BlockSpec(memory_space=pltpu.VMEM)
    acc = pltpu.VMEM(kh.shape[1:], F32)
    return pl.pallas_call(
        body,
        in_specs=[pl.BlockSpec(memory_space=pltpu.SMEM)] + [vmem] * 5,
        out_specs=[vmem] * 3,
        out_shape=[jax.ShapeDtypeStruct(a.shape, BF) for a in (qh, kh, vh)],
        scratch_shapes=[acc, acc],
        name="attend_back",
    )(place, qh, kh, vh, doh, lse)


def flip(value, axis, bit):
    size = lax.axis_size(axis)
    return lax.ppermute(value, axis, [(i, i ^ bit) for i in range(size)])


def xor_order(bits):
    order = [0]
    for bit in list(reversed(bits)) + [1]:
        order = order + [off ^ bit for off in order]
    return order


def scatter_term(left, right, bits):
    half = left.shape[1] // 2
    away = tn(left[:, half:], right).astype(BF)
    came = flip(away, "dp", 1)
    quarter = half // 2
    away = (tn(left[:, quarter:half], right) + came[quarter:]).astype(BF)
    kept = (tn(left[:, :quarter], right) + came[:quarter]).astype(BF)
    came = flip(away, "dp", bits[0])
    for bit in bits[1:]:
        size = kept.shape[0] // 2
        away = (kept[size:].astype(F32) + came[size:]).astype(BF)
        kept = (kept[:size].astype(F32) + came[:size]).astype(BF)
        came = flip(away, "dp", bit)
    return (kept.astype(F32) + came).astype(BF)


def line_sum(value, place):
    size = lax.axis_size("seq")
    rows = value.shape[0] // size

    def chunk(index):
        index = jnp.clip(index, 0, size - 1)
        return lax.dynamic_slice_in_dim(value, index * rows, rows, 0)

    total = chunk(place).astype(F32)
    for way in (1, -1):
        held = None
        for far in range(size - 1, 0, -1):
            mine = chunk(place + way * far)
            if held is not None:
                mine = (mine.astype(F32) + held).astype(BF)
            pairs = [(i, i + way) for i in range(size) if 0 <= i + way * far < size]
            held = lax.ppermute(mine, "seq", pairs)
        total = total + held
    total = total.astype(BF)
    out = jnp.zeros(value.shape, F32)
    out = lax.dynamic_update_slice(out, total.astype(F32), (place * rows, 0))
    for way in (1, -1):
        held = total
        for far in range(1, size):
            pairs = [
                (i, i + way) for i in range(size) if 0 <= i + way < size and 0 <= i - way * (far - 1) < size
            ]
            held = lax.ppermute(held, "seq", pairs)
            source = place - way * far
            index = jnp.clip(source, 0, size - 1) * rows
            old = lax.dynamic_slice(out, (index, 0), held.shape)
            good = (source >= 0) & (source < size)
            out = lax.dynamic_update_slice(
                out, jnp.where(good, held.astype(F32), old), (index, 0)
            )
    return out


def rope_tables(place, tokens, width):
    half = HEAD_DIM // 2
    positions = (place * tokens + jnp.arange(tokens, dtype=jnp.int32)).astype(F32)
    frequency = ROPE_BASE ** (-jnp.arange(half).astype(F32) / half)
    angles = positions[:, None] * frequency[None, :]
    cos, sin = jnp.cos(angles), jnp.sin(angles)
    zero = jnp.zeros_like(sin)
    heads = width // HEAD_DIM
    tile = lambda a, b: jnp.tile(jnp.concatenate([a, b], axis=1), (1, heads))
    return tile(cos, cos), tile(sin, zero), tile(zero, sin)


def rotate(field, tables, sign):
    cos, first, second = tables
    half = HEAD_DIM // 2
    width = field.shape[1]
    cos, first, second = cos[:, :width], first[:, :width], second[:, :width]
    ahead = jnp.concatenate([field[:, half:], field[:, :half]], axis=1)
    behind = jnp.concatenate([field[:, -half:], field[:, :-half]], axis=1)
    return field * cos + sign * (behind * second - ahead * first)


def norm_scale(values):
    return lax.rsqrt(jnp.mean(values * values, axis=-1, keepdims=True) + EPS)


def norm_back(values, scale, gain, grad):
    unit = values * scale
    grad_gain = jnp.sum(grad * unit, axis=0)
    scaled = grad * gain
    inner = jnp.mean(scaled * unit, axis=-1, keepdims=True)
    return scale * (scaled - unit * inner), grad_gain


def local(tokens, cotangent, w_query, w_key, w_value, w_out, w_gate, w_up, w_down, gain_attn, gain_mlp):
    dp, seq = lax.axis_size("dp"), lax.axis_size("seq")
    me, place = lax.axis_index("dp"), lax.axis_index("seq")
    bits = [1 << i for i in range(1, dp.bit_length() - 1)]
    turned = bits[1:] + bits[:1]
    model = tokens.shape[-1]
    rows = tokens.shape[1]
    kvd = w_key.shape[-1]
    place_arr = place.reshape(1).astype(jnp.int32)

    half_model = model // 2

    def xor_columns(value, way):
        width = value.shape[1] // dp
        cut = lambda off: lax.dynamic_slice_in_dim(value, (me ^ off) * width, width, 1)
        return jnp.concatenate([cut(off) for off in xor_order(way)], axis=1)

    tables = rope_tables(place, rows, model)
    x = tokens[0].astype(F32)
    packed = jnp.zeros((8, 256), F32)
    packed = packed.at[0, : gain_attn.shape[1]].set(gain_attn[0].astype(F32))
    packed = packed.at[1, : gain_mlp.shape[1]].set(gain_mlp[0].astype(F32))
    shards = [w[0] for w in (w_query, w_key, w_value, w_out, w_gate, w_up, w_down)]
    outs = forward_call(dp, seq, tokens[0], packed, [t[:, :TILE] for t in tables], shards)
    w_q, w_k, w_v, w_o, w_g, w_u, w_d = outs[:7]
    qh, kh, vh, lefts, x2, hidden, hidden_t, slope, swish, lse, gains = outs[7:]
    gain_one, gain_two = gains[0:1], gains[1:2]
    eb = cotangent[0]
    if len(bits) == 2 and (model // dp) % (16 * seq) == 0:
        dx, grads, result, res = backward_call(
            seq, tokens[0], gains, x2, [t[:, :TILE] for t in tables], hidden_t, eb, lefts,
            qh, kh, vh, lse, outs[:7], hidden, slope, swish,
        )
        block = model // dp
        g_down, g_gate, g_up, g_out, g_query, g_key, g_value, dx, result = finish_call(
            res.reshape(-1, block, COLS), dx, result, w_down.shape[1], w_gate.shape[2], kvd
        )
        return (
            result[None],
            dx[None],
            g_query[None],
            g_key[None],
            g_value[None],
            g_out[None],
            g_gate[None],
            g_up[None],
            g_down[None],
            grads[0:1, :block],
            grads[1:2, :block],
        )

    scale_one = norm_scale(x)
    scale_two = norm_scale(x2)
    result = x2 + nn(hidden, w_d)
    e = eb.astype(F32)
    dh = nt(eb, w_d)
    dgate = (dh * slope).astype(BF)
    dup = (dh * swish).astype(BF)
    dn2 = nt(dgate, w_g) + nt(dup, w_u)
    dx2, term_gain_two = norm_back(x2, scale_two, gain_two, dn2)
    e2 = e + dx2
    e2b = e2.astype(BF)
    do = nt(e2b, w_o).astype(BF)
    n2, mixed, n1 = (lefts[i * model : (i + 1) * model].T for i in range(3))
    hidden_a = xor_columns(hidden, bits)
    hidden_b = xor_columns(hidden, turned)
    sum_down = jnp.concatenate(
        [
            scatter_term(hidden_a, eb[:, :half_model], bits),
            scatter_term(hidden_b, eb[:, half_model:], turned),
        ],
        axis=1,
    )
    n2_a, n2_b = xor_columns(n2, bits), xor_columns(n2, turned)
    sum_gate = scatter_term(n2_a, dgate, bits)
    sum_up = scatter_term(n2_b, dup, turned)
    mixed_a, mixed_b = xor_columns(mixed, bits), xor_columns(mixed, turned)
    sum_out = jnp.concatenate(
        [
            scatter_term(mixed_a, e2b[:, :half_model], bits),
            scatter_term(mixed_b, e2b[:, half_model:], turned),
        ],
        axis=1,
    )
    doh = do.reshape(rows, HEADS, HEAD_DIM).transpose(1, 0, 2)
    dqh, dkh, dvh = attend_back(place_arr, qh, kh, vh, doh, lse)
    dq = dqh.transpose(1, 0, 2).reshape(rows, model)
    dks, dvs = (a.reshape(KV_HEADS, seq, rows, HEAD_DIM).transpose(1, 2, 0, 3).reshape(seq, rows, kvd) for a in (dkh, dvh))
    held = None
    for far in range(seq - 1, -1, -1):
        mine = jnp.concatenate([dks[far], dvs[far]], axis=1)
        if held is not None:
            mine = (mine.astype(F32) + held).astype(BF)
        if far:
            held = lax.ppermute(mine, "seq", [(i, i - 1) for i in range(far, seq)])
    dk, dv = mine[:, :kvd], mine[:, kvd:]
    dqp = rotate(dq.astype(F32), tables, -1.0).astype(BF)
    dkp = rotate(dk.astype(F32), tables, -1.0).astype(BF)
    n1_a, n1_b = xor_columns(n1, bits), xor_columns(n1, turned)
    sum_query = scatter_term(n1_a, dqp, bits)
    sum_kv = scatter_term(n1_b, jnp.concatenate([dkp, dv], axis=1), turned)
    dn1 = nt(dqp, w_q) + nt(dkp, w_k) + nt(dv, w_v)
    dx1, term_gain_one = norm_back(x, scale_one, gain_one, dn1)
    input_grad = e2 + dx1

    both = jnp.stack([term_gain_one, term_gain_two])
    for bit in [1] + bits:
        both = both + flip(both, "dp", bit)
    for bit in [1 << i for i in range(seq.bit_length() - 1)]:
        both = both + flip(both, "seq", bit)
    width = model // dp
    both = lax.dynamic_slice_in_dim(both, me * width, width, 1)

    g_down = line_sum(sum_down, place)
    g_gate = line_sum(sum_gate, place)
    g_up = line_sum(sum_up, place)
    g_out = line_sum(sum_out, place)
    g_query = line_sum(sum_query, place)
    g_kv = line_sum(sum_kv, place)
    return (
        result[None],
        input_grad[None],
        g_query[None],
        g_kv[None, :, :kvd],
        g_kv[None, :, kvd:],
        g_out[None],
        g_gate[None],
        g_up[None],
        g_down[None],
        both[0:1],
        both[1:2],
    )


def solution(mesh):
    by_token = P("dp", "seq", None)
    by_row = P(None, "dp", None)
    by_gain = P(None, "dp")
    in_specs = (by_token,) * 2 + (by_row,) * 7 + (by_gain,) * 2
    return jax.shard_map(local, mesh=mesh, in_specs=in_specs, out_specs=in_specs, check_vma=False)
```

```python
import functools

import jax
import jax.numpy as jnp
from jax import lax
from jax.experimental import pallas as pl
from jax.experimental.pallas import tpu as pltpu
from jax.sharding import PartitionSpec as P

HEADS = 16
KV_HEADS = 8
HEAD_DIM = 96
GROUP = HEADS // KV_HEADS
EPS = 1e-05
ROPE_BASE = 100000.0
BF = jnp.bfloat16
F32 = jnp.float32
NEG = -1e30
SCALE = HEAD_DIM ** (-0.5)


def dot(a, b, dims):
    return lax.dot_general(a, b, (dims, ((), ())), preferred_element_type=F32)


def nn(a, b):
    return dot(a, b, ((1,), (0,)))


def nt(a, b):
    return dot(a, b, ((1,), (1,)))


def tn(a, b):
    return dot(a, b, ((0,), (0,)))


def lanes(ref, head, width=HEAD_DIM):
    return ref[:, head * HEAD_DIM : head * HEAD_DIM + width]


MESH = pl.DeviceIdType.MESH
TILE = 4 * HEAD_DIM
COLS = 512


class Gather:
    def __init__(self, me, place, bits, src, out, send, recv):
        self.me, self.bits, self.src, self.out = me, bits, src, out
        self.send, self.recv = send, recv
        self.rows = src.shape[0]
        self.quarter = -(-self.rows // 96) * 16
        self.most = self.rows - self.quarter
        units, parts = self.most // 16, len(bits)
        self.size = [16 * (units // parts + (i < units % parts)) for i in range(parts)]
        self.start = [sum(self.size[:i]) for i in range(parts)]
        self.odd = place % 2
        self.pair = place + 1 - 2 * self.odd
        self.count = 0
        self.waits = []
        own = {}
        for bit in bits:
            own[bit] = self.copy(self.src, 0, 1, self.most, bit, self.odd * self.quarter)
        self.own = own
        self.own_core = self.copy(self.src, 0, 0, self.rows, 1, 0)
        self.forwards = []
        self.arrival = {}
        for bit in bits:
            for i in range(len(bits)):
                self.arrival[(bit, i)] = own[bit]
        for step in range(1, len(bits)):
            for i in range(len(bits)):
                order = bits[i:] + bits[:i]
                bit = order[step]
                held = [0]
                for b in order[:step]:
                    held = held + [m | b for m in held]
                for m in held[1:]:
                    start = self.odd * self.quarter + self.start[i]
                    made = self.copy(out, m, 1, self.size[i], bit, start)
                    self.forwards.append((m, i, made))
                    self.arrival[(m | bit, i)] = made
        masks = list(range(2, 2 * max(bits), 2))
        self.masks = masks
        self.across = [
            self.copy(out, m, 2, self.quarter, 0, self.odd * self.most) for m in masks
        ]
        self.core = [self.copy(out, m, 1, self.rows, 1, 0) for m in masks]
        self.seen = set()

    def copy(self, ref, m, kind, rows, bit, start):
        at = (self.me ^ m) * self.rows + start
        source = ref.at[pl.ds(pl.multiple_of(start, 16), rows)] if ref is self.src else ref.at[pl.ds(pl.multiple_of(at, 16), rows)]
        target = {"seq": self.pair} if kind == 2 else {"dp": self.me ^ bit}
        index = self.count
        self.count += 1
        return pltpu.make_async_remote_copy(
            src_ref=source,
            dst_ref=self.out.at[pl.ds(pl.multiple_of(at, 16), rows)],
            send_sem=self.send.at[index],
            recv_sem=self.recv.at[index],
            device_id=target,
            device_id_type=MESH,
        )

    def begin(self):
        for bit in self.bits:
            self.own[bit].start()
        self.own_core.start()

    def arrived(self, copy):
        if id(copy) not in self.seen:
            self.seen.add(id(copy))
            copy.wait_recv()

    def forward(self):
        for m, i, made in self.forwards:
            self.arrived(self.arrival[(m, i)])
            made.start()

    def chosen(self, near):
        return [i for i, m in enumerate(self.masks) if near is None or (m in self.bits) == near]

    def cross(self, near=None):
        for at in self.chosen(near):
            for i in range(len(self.bits)):
                self.arrived(self.arrival[(self.masks[at], i)])
            self.across[at].start()

    def share(self, near=None):
        for at in self.chosen(near):
            self.across[at].wait_recv()
            self.core[at].start()

    def finish(self):
        self.own_core.wait_recv()
        for made in self.core:
            made.wait_recv()

    def drain(self):
        for made in list(self.own.values()) + [self.own_core] + [f[2] for f in self.forwards] + self.across + self.core:
            made.wait_send()


def gather_copies(chip_bits):
    forwards = sum(chip_bits * (2**step - 1) for step in range(1, chip_bits))
    return chip_bits + 1 + forwards + 2 * (2**chip_bits - 1)


def forward_body(dp, seq, x_ref, gain_ref, cos_ref, first_ref, second_ref, *refs):
    w_in, refs = refs[:7], refs[7:]
    w_out, refs = refs[:7], refs[7:]
    kept, lse_ref, gains_ref, refs = refs[:9], refs[9], refs[10], refs[11:]
    made, stage, refs = refs[:9], refs[9:16], refs[16:]
    qh, kh, vh, lefts, x2_ref, hidden, hidden_t, slope, swish = made
    (wq, wk, wv, kvbuf, gbuf, oh, n1_ref, n2_ref, o_ref, wt, send, recv, kv_send, kv_recv, g_send, g_recv, own_sem,
     load_sem, tile_sem, keep_sem) = refs
    me, place = lax.axis_index("dp"), lax.axis_index("seq")
    bits = [1 << i for i in range(1, dp.bit_length() - 1)]
    tokens, model = x_ref.shape
    block = model // dp

    for i in range(7):
        pltpu.make_async_copy(w_in[i], stage[i], own_sem.at[i]).start()
    for r in range(1, seq):
        kvbuf[r] = jnp.zeros_like(kvbuf[r])

    barrier = pltpu.get_barrier_semaphore()
    for off in range(1, dp):
        pl.semaphore_signal(barrier, inc=1, device_id={"dp": me ^ off}, device_id_type=MESH)
    up, down = place + 1, place - 1
    odd = place % 2
    pair = place + 1 - 2 * odd
    other = place - 1 + 2 * odd
    has_other = (other >= 0) & (other < seq)
    pl.semaphore_signal(barrier, inc=1, device_id={"seq": pair}, device_id_type=MESH)

    @pl.when(has_other)
    def _():
        pl.semaphore_signal(barrier, inc=1, device_id={"seq": other}, device_id_type=MESH)

        pl.semaphore_wait(barrier, dp + 1)

    @pl.when(jnp.logical_not(has_other))
    def _():
        pl.semaphore_wait(barrier, dp)

    gains = [
        pltpu.make_async_remote_copy(
            src_ref=gain_ref,
            dst_ref=gbuf.at[me],
            send_sem=g_send.at[off],
            recv_sem=g_recv.at[off],
            device_id={"dp": me ^ off},
            device_id_type=MESH,
        )
        for off in range(1, dp)
    ]
    for g in gains:
        g.start()
    turned = bits[1:] + bits[:1]
    jobs = [
        Gather(me, place, turned if i in (1, 2, 5) else bits, w_in[i], w_out[i], send.at[i], recv.at[i])
        for i in range(7)
    ]
    first = jobs[:3]
    job_o, job_g, job_u, job_d = jobs[3:]
    for job in first:
        job.begin()

    def own_out(i):
        rows = w_in[i].shape[0]
        return pltpu.make_async_copy(stage[i], w_out[i].at[pl.ds(pl.multiple_of(me * rows, 8), rows)], own_sem.at[i])

    for i in range(7):
        pltpu.make_async_copy(w_in[i], stage[i], own_sem.at[i]).wait()
        own_out(i).start()

    gbuf[me] = gain_ref[...]
    x = x_ref[...].astype(F32)
    scale = lax.rsqrt(jnp.mean(x * x, axis=1, keepdims=True) + EPS)
    for g in gains:
        g.wait_recv()
    for k in range(dp):
        gains_ref[:, k * block : (k + 1) * block] = gbuf[k, :, :block]
    n1_ref[...] = (x * scale * gains_ref[0:1, :]).astype(BF)

    def keep(i):
        return pltpu.make_async_copy(made[i], kept[i], keep_sem.at[i])

    def put_left(which, source):
        @pl.loop(0, model // TILE)
        def _(t):
            at = pl.multiple_of(t * TILE, 128)
            lefts[pl.ds(pl.multiple_of(which * model + at, 16), TILE), :] = source[:, pl.ds(at, TILE)].T

    for job in first:
        job.forward()
    job_o.begin()
    job_g.begin()
    for job in first:
        job.cross()
    for job in first:
        job.share()
    for i in range(7):
        own_out(i).wait()
    for job in first:
        job.finish()
    loads = [
        pltpu.make_async_copy(w_out[i], ref, load_sem.at[i]) for i, ref in enumerate((wq, wk, wv))
    ]
    for load in loads:
        load.start()

    def turn(value):
        ahead = pltpu.roll(value, TILE - HEAD_DIM // 2, 1)
        behind = pltpu.roll(value, HEAD_DIM // 2, 1)
        return value * cos_ref[...] + behind * second_ref[...] - ahead * first_ref[...]

    kvd = wk.shape[1]
    loads[1].wait()

    @pl.loop(0, kvd // TILE)
    def _(t):
        at = pl.multiple_of(t * TILE, 128)
        kvbuf[0, :, pl.ds(at, TILE)] = turn(nn(n1_ref[...], wk[:, pl.ds(at, TILE)])).astype(BF)

    loads[2].wait()

    @pl.loop(0, kvd // TILE)
    def _(t):
        at = pl.multiple_of(t * TILE, 128)
        kvbuf[0, :, pl.ds(kvd + at, TILE)] = nn(n1_ref[...], wv[:, pl.ds(at, TILE)]).astype(BF)

    def kv_copy(r):
        return pltpu.make_async_remote_copy(
            src_ref=kvbuf.at[r],
            dst_ref=kvbuf.at[r + 1],
            send_sem=kv_send.at[r],
            recv_sem=kv_recv.at[r],
            device_id={"seq": up},
            device_id_type=MESH,
        )

    def kv_send_on(r):
        @pl.when((place >= r) & (place < seq - 1))
        def _():
            kv_copy(r).start()

    def kv_wait(r):
        @pl.when(place >= r)
        def _():
            pltpu.make_async_remote_copy(
                src_ref=kvbuf.at[r - 1],
                dst_ref=kvbuf.at[r],
                send_sem=kv_send.at[r - 1],
                recv_sem=kv_recv.at[r - 1],
                device_id={"seq": down},
                device_id_type=MESH,
            ).wait_recv()

    kv_send_on(0)
    loads[0].wait()

    @pl.loop(0, model // TILE)
    def _(t):
        at = pl.multiple_of(t * TILE, 128)
        q = turn(nn(n1_ref[...], wq[:, pl.ds(at, TILE)])).astype(BF)
        for i in range(TILE // HEAD_DIM):
            qh[t * (TILE // HEAD_DIM) + i] = q[:, i * HEAD_DIM : (i + 1) * HEAD_DIM]

    def split_heads(r):
        for g in range(KV_HEADS):
            kh[g, r * tokens : (r + 1) * tokens, :] = kvbuf[r, :, g * HEAD_DIM : (g + 1) * HEAD_DIM]
            vh[g, r * tokens : (r + 1) * tokens, :] = kvbuf[r, :, kvd + g * HEAD_DIM : kvd + (g + 1) * HEAD_DIM]

    job_o.forward()
    job_u.begin()
    split_heads(0)
    for r in range(1, seq):
        kv_wait(r)
        if r < seq - 1:
            kv_send_on(r)
        if r == min(2, seq - 1):
            job_o.cross()
            job_g.forward()
            job_d.begin()
        split_heads(r)
    job_o.share()
    job_g.cross(True)

    row = lax.broadcasted_iota(jnp.int32, (tokens, tokens), 0)
    col = lax.broadcasted_iota(jnp.int32, (tokens, tokens), 1)
    lse_ref[...] = jnp.zeros_like(lse_ref)
    lane = lax.broadcasted_iota(jnp.int32, (tokens, 128), 1)

    half = HEADS // 2

    def attend_heads(start, stop):
        @pl.loop(start, stop)
        def _(h):
            g = h // GROUP
            q = qh[h]
            scores = []
            for r in range(seq):
                s = nt(q, kh[g, r * tokens : (r + 1) * tokens, :]) * SCALE
                scores.append(jnp.where(col <= row if r == 0 else place >= r, s, NEG))
            top = functools.reduce(jnp.maximum, [jnp.max(s, axis=1, keepdims=True) for s in scores])
            weights = [jnp.exp(s - top) for s in scores]
            total = sum(jnp.sum(w, axis=1, keepdims=True) for w in weights)
            inverse = 1.0 / total
            oh[h] = sum(
                nn((w * inverse).astype(BF), vh[g, r * tokens : (r + 1) * tokens, :])
                for r, w in enumerate(weights)
            ).astype(BF)
            lse_ref[...] += jnp.where(lane == h, top + jnp.log(total), 0.0)

    attend_heads(0, half)
    job_u.forward()
    job_g.share(True)
    attend_heads(half, HEADS)
    job_g.cross(False)
    job_u.cross(True)
    for i in range(3):
        keep(i).start()
    for h in range(HEADS):
        o_ref[:, h * HEAD_DIM : (h + 1) * HEAD_DIM] = oh[h]

    job_o.finish()
    load_o = pltpu.make_async_copy(w_out[3], wq, load_sem.at[0])
    load_o.start()
    put_left(2, n1_ref)
    put_left(1, o_ref)
    load_o.wait()

    @pl.loop(0, model // TILE)
    def _(t):
        at = pl.multiple_of(t * TILE, 128)
        x2_ref[:, pl.ds(at, TILE)] = x_ref[:, pl.ds(at, TILE)].astype(F32) + nn(o_ref[...], wq[:, pl.ds(at, TILE)])

    x2 = x2_ref[...]
    n2_ref[...] = (x2 * lax.rsqrt(jnp.mean(x2 * x2, axis=1, keepdims=True) + EPS) * gains_ref[1:2, :]).astype(BF)
    put_left(0, n2_ref)
    for i in (3, 4):
        keep(i).start()

    def project(weight, take, first=0, last=None):
        panels = weight.shape[1] // COLS if last is None else last

        def panel(t):
            at = pl.multiple_of(t * COLS, 128)
            return pltpu.make_async_copy(weight.at[:, pl.ds(at, COLS)], wt.at[t % 2], tile_sem.at[t % 2])

        panel(first).start()

        @pl.loop(first, panels)
        def _(t):
            panel(t).wait()

            @pl.when(t + 1 < panels)
            def _():
                panel(t + 1).start()

            take(pl.multiple_of(t * COLS, 128), nn(n2_ref[...], wt[t % 2]))

    def take_gate(at, gate):
        swish[:, pl.ds(at, COLS)] = gate

    def take_up(at, up):
        gate = swish[:, pl.ds(at, COLS)]
        sig = jax.nn.sigmoid(gate)
        act = gate * sig
        value = (act * up).astype(BF)
        hidden[:, pl.ds(at, COLS)] = value
        hidden_t[pl.ds(at, COLS), :] = value.T
        slope[:, pl.ds(at, COLS)] = up * sig * (1.0 + gate * (1.0 - sig))
        swish[:, pl.ds(at, COLS)] = act

    job_g.share(False)
    job_d.forward()
    job_g.finish()
    project(w_out[4], take_gate)
    job_u.cross(False)
    job_u.share(True)
    job_d.cross(True)
    job_u.share(False)
    job_u.finish()
    middle = w_out[5].shape[1] // COLS // 2
    project(w_out[5], take_up, 0, middle)
    job_d.cross(False)
    job_d.share(True)
    project(w_out[5], take_up, middle)
    for i in range(5, 9):
        keep(i).start()
    job_d.share(False)
    job_d.finish()
    for i in range(9):
        keep(i).wait()
    for r in range(seq - 1):

        @pl.when((place >= r) & (place < seq - 1))
        def _():
            kv_copy(r).wait_send()

    for g in gains:
        g.wait_send()
    for job in jobs:
        job.drain()


def forward_call(dp, seq, x, gains, tables, weights):
    tokens, model = x.shape
    chip_bits = dp.bit_length() - 2
    copies = gather_copies(chip_bits)
    anyspec = pl.BlockSpec(memory_space=pl.ANY)
    vmem = pl.BlockSpec(memory_space=pltpu.VMEM)
    out_shape = [jax.ShapeDtypeStruct((dp * w.shape[0], w.shape[1]), BF) for w in weights]
    heads = jax.ShapeDtypeStruct((HEADS, tokens, HEAD_DIM), BF)
    keys = jax.ShapeDtypeStruct((KV_HEADS, seq * tokens, HEAD_DIM), BF)
    kvd, ff = weights[1].shape[1], weights[4].shape[1]
    made = [
        heads,
        keys,
        keys,
        jax.ShapeDtypeStruct((3 * model, tokens), BF),
        jax.ShapeDtypeStruct((tokens, model), F32),
        jax.ShapeDtypeStruct((tokens, ff), BF),
        jax.ShapeDtypeStruct((ff, tokens), BF),
        jax.ShapeDtypeStruct((tokens, ff), F32),
        jax.ShapeDtypeStruct((tokens, ff), F32),
    ]
    out_shape += made + [jax.ShapeDtypeStruct((tokens, 128), F32), jax.ShapeDtypeStruct((8, model), F32)]
    line = pltpu.VMEM((tokens, model), BF)
    dma = pltpu.SemaphoreType.DMA
    return pl.pallas_call(
        functools.partial(forward_body, dp, seq),
        out_shape=out_shape,
        in_specs=[vmem] * 5 + [anyspec] * 7,
        out_specs=[anyspec] * 16 + [vmem] * 2,
        scratch_shapes=[pltpu.VMEM(a.shape, a.dtype) for a in made]
        + [pltpu.VMEM(w.shape, BF) for w in weights]
        + [
            pltpu.VMEM((model, model), BF),
            pltpu.VMEM((model, kvd), BF),
            pltpu.VMEM((model, kvd), BF),
            pltpu.VMEM((seq, tokens, model), BF),
            pltpu.VMEM((dp, 8, 256), F32),
            pltpu.VMEM((HEADS, tokens, HEAD_DIM), BF),
            line,
            line,
            line,
            pltpu.VMEM((2, model, COLS), BF),
            dma((7, copies)),
            dma((7, copies)),
            dma((seq,)),
            dma((seq,)),
            dma((dp,)),
            dma((dp,)),
            dma((7,)),
            dma((3,)),
            dma((2,)),
            dma((9,)),
        ],
        compiler_params=pltpu.CompilerParams(
            collective_id=0, has_side_effects=True, vmem_limit_bytes=60 * 1024 * 1024
        ),
        name="forward",
    )(x, gains, *tables, *weights)


def head_column(lse, h):
    lane = lax.broadcasted_iota(jnp.int32, lse.shape, 1)
    return jnp.sum(jnp.where(lane == h, lse, 0.0), axis=1, keepdims=True)


def back_group(place, chunks, g, slot, q_ref, do_ref, lse, k, v, dq_ref, dk_ref, dv_ref, acc_k, acc_v):
    tokens = q_ref.shape[1]
    row = lax.broadcasted_iota(jnp.int32, (tokens, tokens), 0)
    col = lax.broadcasted_iota(jnp.int32, (tokens, tokens), 1)
    for i in range(GROUP):
        h = GROUP * g + i
        q, do = q_ref[h], do_ref[h]
        total = head_column(lse, h)
        probs, dprobs = [], []
        for r in range(chunks):
            span = slice(r * tokens, (r + 1) * tokens)
            s = nt(q, k[span, :]) * SCALE
            s = jnp.where(col <= row if r == 0 else place >= r, s, NEG)
            probs.append(jnp.exp(s - total))
            dprobs.append(nt(do, v[span, :]))
        inner = sum(jnp.sum(p * d, axis=1, keepdims=True) for p, d in zip(probs, dprobs))
        dq = jnp.zeros((tokens, HEAD_DIM), F32)
        for r in range(chunks):
            span = slice(r * tokens, (r + 1) * tokens)
            ds = (probs[r] * (dprobs[r] - inner)).astype(BF)
            dq += nn(ds, k[span, :])
            dk = tn(ds, q)
            dv = tn(probs[r].astype(BF), do)
            if i == 0:
                acc_k[span, :] = dk
                acc_v[span, :] = dv
            else:
                dk_ref[slot, span, :] = ((acc_k[span, :] + dk) * SCALE).astype(BF)
                dv_ref[slot, span, :] = (acc_v[span, :] + dv).astype(BF)
        dq_ref[h] = (dq * SCALE).astype(BF)


LAG_B, LAG_C, LAG_D = 1, 4, 6
SLOTS_CORE, SLOTS, SLOTS_SUM, SLOTS_OUT = 2, 4, 11, 8


def backward_body(seq, x_ref, gains_ref, x2_ref, cos_ref, first_ref, second_ref, hidden_ref, eb_ref, lefts_ref,
                  qh, kh, vh, lse_ref, wq_in, wk_in, wv_in, wo_in, wg_in, wu_in, wd_in, hid_in, slope_in, swish_in, *refs):
    dx_ref, gain_out, out_ref, res = refs[:4]
    (rights, doh, dqh, dkh, dvh, acc_k, acc_v, dkv, dkv_in, dn1, wt, hid, slope, swish, term2,
     cs, cr, sums, r0, r1, zs, zr, zt, gsend, grecv, gsum, gzrecv,
     mid_sem, w_sem, core_s, core_r, s0_s, s0_r, s1_s, s1_r, z_s, z_r, a_s, a_r, t_sem, kv_s, kv_r,
     g_s, g_r, gz_s, gz_r, core_free, s0_free, s1_free, z_free) = refs[4:]
    me, place = lax.axis_index("dp"), lax.axis_index("seq")
    core, chip_x, chip_y = me % 2, (me // 2) % 2, me // 4
    tokens, model = x_ref.shape
    rows = model // 8
    sub = rows // seq
    kvd = wk_in.shape[1]
    d_rows = hidden_ref.shape[0] // 8
    d_chunks = d_rows * 3 // rows
    n_chunks = rights.shape[1] // COLS
    o_panels = model // COLS
    gu_panels = n_chunks - 3 * o_panels
    total_chunks = d_chunks + n_chunks

    def owner(x, y, c):
        return ((chip_y + y) % 2) * 4 + ((chip_x + x) % 2) * 2 + (core + c) % 2

    partner = owner(0, 0, 1)
    near = [[owner(1, 0, 0), owner(0, 1, 0)], [owner(0, 1, 0), owner(1, 0, 0)]]

    ff = wg_in.shape[1]
    part_d = COLS // 2

    def mid_loads(k):
        s = k % 2
        at = pl.multiple_of(k * COLS, 128)
        pairs = [
            (wd_in.at[pl.ds(at, part_d)], wt.at[s, pl.ds(0, part_d), pl.ds(0, model)]),
            (wd_in.at[pl.ds(at + part_d, part_d)], wt.at[s, pl.ds(0, part_d), pl.ds(model, model)]),
            (hid_in.at[:, pl.ds(at, COLS)], hid.at[s]),
            (slope_in.at[:, pl.ds(at, COLS)], slope.at[s]),
            (swish_in.at[:, pl.ds(at, COLS)], swish.at[s]),
        ]
        return [pltpu.make_async_copy(a, b, mid_sem.at[s, i]) for i, (a, b) in enumerate(pairs)]

    def ff_load(j, i):
        return pltpu.make_async_copy(
            (wg_in, wu_in)[i].at[pl.ds(pl.multiple_of(j * TILE, 16), TILE)], wt.at[i, :, pl.ds(0, ff)], w_sem.at[i, 0]
        )

    def o_load(t):
        return pltpu.make_async_copy(
            wo_in.at[pl.ds(t * TILE, TILE)], wt.at[t % 2, :, pl.ds(t // 2 * model, model)], w_sem.at[t % 2, t // 2]
        )

    for k in range(2):
        for made in mid_loads(k):
            made.start()
    out_ref[...] = x2_ref[...]

    barrier = pltpu.get_barrier_semaphore()
    for off in range(1, 8):
        pl.semaphore_signal(barrier, inc=1, device_id={"dp": me ^ off}, device_id_type=MESH)
    for far in range(1, seq):
        to = (place + far) % seq
        pl.semaphore_signal(barrier, inc=1, device_id={"seq": to}, device_id_type=MESH)
    pl.semaphore_wait(barrier, 7 + seq - 1)

    def remote(src, dst, send, recv, **target):
        return pltpu.make_async_remote_copy(
            src_ref=src, dst_ref=dst, send_sem=send, recv_sem=recv, device_id=target, device_id_type=MESH
        )

    def signal(sem, **target):
        pl.semaphore_signal(sem, inc=1, device_id=target, device_id_type=MESH)

    def core_copy(c):
        s = c % SLOTS_CORE
        return remote(cs.at[s], cr.at[s], core_s.at[s], core_r.at[s], dp=partner)

    def first_copy(c, parity):
        s = c % SLOTS
        return remote(sums.at[c % SLOTS_SUM, pl.ds(2 * rows, 2 * rows)], r0.at[s], s0_s.at[s], s0_r.at[s], dp=near[parity][0])

    def second_copy(c, parity):
        s = c % SLOTS
        return remote(sums.at[c % SLOTS_SUM, pl.ds(rows, rows)], r1.at[s], s1_s.at[s], s1_r.at[s], dp=near[parity][1])

    def offsets(index, parity):
        low, high = index % 2, index // 2
        return (high, low) if parity == 0 else (low, high)

    def stage_a(c, parity):
        s, t = c % SLOTS_CORE, c % SLOTS_SUM

        @pl.when(c >= SLOTS_CORE)
        def _():
            core_copy(c).wait_send()

        def put(away, term):
            @pl.loop(0, 4)
            def _(index):
                dx, dy = offsets(index, parity)
                at = pl.multiple_of(index * rows, 16)
                if away:
                    cs[s, pl.ds(at, rows), :] = term(owner(dx, dy, 1)).astype(BF)
                else:
                    sums[t, pl.ds(at, rows), :] = term(owner(dx, dy, 0)).astype(BF)

        def term_d(who):
            size = rows // 3
            at = pl.multiple_of(who * d_rows + c * size, 16)
            left = hidden_ref[pl.ds(at, size), :]
            return jnp.concatenate(
                [nn(left, eb_ref[:, i * COLS : (i + 1) * COLS]) for i in range(3)], axis=0
            )

        k = c - d_chunks
        which = (k >= gu_panels).astype(jnp.int32) + (k >= gu_panels + o_panels).astype(jnp.int32)

        def term_n(who):
            left = lefts_ref[pl.ds(pl.multiple_of(which * model + who * rows, 16), rows), :]
            return nn(left, rights[:, pl.ds(pl.multiple_of(k * COLS, 128), COLS)])

        def both(term):
            put(True, term)

            @pl.when(c >= SLOTS_CORE)
            def _():
                pl.semaphore_wait(core_free, 1)

            core_copy(c).start()
            put(False, term)

        @pl.when(c < d_chunks)
        def _():
            both(term_d)

        @pl.when(c >= d_chunks)
        def _():
            both(term_n)

    def add_rows(count, target, extra):
        @pl.loop(0, count // 64)
        def _(i):
            at = pl.multiple_of(i * 64, 16)
            target[pl.ds(at, 64), :] = (target[pl.ds(at, 64), :].astype(F32) + extra[pl.ds(at, 64), :].astype(F32)).astype(BF)

    def stage_b(c, parity):
        core_copy(c).wait_recv()
        add_rows(4 * rows, sums.at[c % SLOTS_SUM], cr.at[c % SLOTS_CORE])

        @pl.when(c < total_chunks - SLOTS_CORE)
        def _():
            signal(core_free, dp=partner)

        @pl.when(c >= SLOTS)
        def _():
            pl.semaphore_wait(s0_free.at[parity], 1)

        first_copy(c, parity).start()

    def stage_c(c, parity):
        first_copy(c, parity).wait_recv()
        add_rows(2 * rows, sums.at[c % SLOTS_SUM], r0.at[c % SLOTS])

        @pl.when(c < total_chunks - SLOTS)
        def _():
            signal(s0_free.at[parity], dp=near[parity][0])

        @pl.when(c >= SLOTS)
        def _():
            pl.semaphore_wait(s1_free.at[parity], 1)

        second_copy(c, parity).start()
        first_copy(c, parity).wait_send()

    def stage_d(c, parity):
        second_copy(c, parity).wait_recv()
        add_rows(rows, sums.at[c % SLOTS_SUM], r1.at[c % SLOTS])

        @pl.when(c < total_chunks - SLOTS)
        def _():
            signal(s1_free.at[parity], dp=near[parity][1])

        second_copy(c, parity).wait_send()

    def step_of(way):
        return 1 - 2 * way

    def inside(at):
        return (at >= 0) & (at < seq)

    def z_copy(c, way, hop):
        s = c % SLOTS
        slot = way * (seq - 1) + hop - 1
        return remote(zs.at[slot, s], zr.at[slot, s], z_s.at[slot, s], z_r.at[slot, s], seq=place + step_of(way))

    def z_sends(way, hop):
        return inside(place + step_of(way) * (seq - hop))

    def z_gets(way, hop):
        return inside(place - step_of(way)) & inside(place - step_of(way) + step_of(way) * (seq - hop))

    def part(c, index):
        index = jnp.minimum(jnp.maximum(index, 0), seq - 1)
        return sums[c % SLOTS_SUM, pl.ds(pl.multiple_of(index * sub, 16), sub), :].astype(F32)

    def z_take(c, way, hop):
        slot = way * (seq - 1) + hop - 1
        gets = z_gets(way, hop)

        @pl.when(gets)
        def _():
            z_copy(c, way, hop).wait_recv()

        return jnp.where(gets, zr[slot, c % SLOTS].astype(F32), 0.0)

    def z_release(c, way, hop):
        slot = way * (seq - 1) + hop - 1

        @pl.when(z_gets(way, hop) & (c < total_chunks - SLOTS))
        def _():
            signal(z_free.at[slot], seq=place - step_of(way))

    def stage_z(c, hop):
        for way in range(2):
            slot = way * (seq - 1) + hop - 1
            value = part(c, place + step_of(way) * (seq - hop))
            if hop > 1:
                value = value + z_take(c, way, hop - 1)
            sends = z_sends(way, hop)

            @pl.when(sends & (c >= SLOTS))
            def _():
                z_copy(c, way, hop).wait_send()

            zs[slot, c % SLOTS] = value.astype(BF)
            if hop > 1:
                z_release(c, way, hop - 1)

            @pl.when(sends & (c >= SLOTS))
            def _():
                pl.semaphore_wait(z_free.at[slot], 1)

            @pl.when(sends)
            def _():
                z_copy(c, way, hop).start()

    def res_at(c, source):
        index = jnp.minimum(jnp.maximum(source, 0), seq - 1)
        return res.at[pl.ds(pl.multiple_of(c * rows + index * sub, 16), sub)]

    def own_copy(c):
        s = c % SLOTS_OUT
        return pltpu.make_async_copy(zt.at[s], res_at(c, place), t_sem.at[s])

    def a_copy(c, way, hop):
        s = c % SLOTS_OUT
        slot = way * (seq - 1) + hop - 1
        source = place - step_of(way) * (hop - 1)
        src = zt.at[s] if hop == 1 else res_at(c, source)
        return remote(src, res_at(c, source), a_s.at[slot, s], a_r.at[slot, s], seq=place + step_of(way))

    def a_sends(way, hop):
        return inside(place + step_of(way)) & inside(place - step_of(way) * (hop - 1))

    def a_gets(way, hop):
        return inside(place - step_of(way) * hop)

    def stage_total(c):
        value = part(c, place)
        for way in range(2):
            value = value + z_take(c, way, seq - 1)

        @pl.when(c >= SLOTS_OUT)
        def _():
            own_copy(c).wait()

        for way in range(2):
            @pl.when((c >= SLOTS_OUT) & a_sends(way, 1))
            def _():
                a_copy(c, way, 1).wait_send()

        zt[c % SLOTS_OUT] = value.astype(BF)
        for way in range(2):
            z_release(c, way, seq - 1)
        own_copy(c).start()
        stage_out(c, 1)

    def stage_out(c, hop):
        for way in range(2):
            if hop > 1:
                @pl.when(a_gets(way, hop - 1))
                def _():
                    a_copy(c, way, hop - 1).wait_recv()

            if hop < seq:
                if hop > 1:
                    @pl.when((c >= SLOTS_OUT) & a_sends(way, hop))
                    def _():
                        a_copy(c, way, hop).wait_send()

                @pl.when(a_sends(way, hop))
                def _():
                    a_copy(c, way, hop).start()

    lag_total = LAG_D + seq - 1
    stages = [(LAG_B, stage_b), (LAG_C, stage_c), (LAG_D, stage_d), (LAG_D, lambda c, parity: stage_z(c, 1))]
    stages += [(LAG_D + hop - 1, lambda c, parity, hop=hop: stage_z(c, hop)) for hop in range(2, seq)]
    stages += [(lag_total, lambda c, parity: stage_total(c))]
    stages += [(lag_total + hop - 1, lambda c, parity, hop=hop: stage_out(c, hop)) for hop in range(2, seq + 1)]
    last_lag = lag_total + seq - 1

    def tick(c, parity):
        for lag, stage in sorted(stages, key=lambda pair: -pair[0]):
            then = c - lag

            @pl.when((then >= 0) & (then < total_chunks))
            def _():
                stage(then, (parity + lag) % 2)

        @pl.when(c < total_chunks)
        def _():
            stage_a(c, parity)

    pair_width = 2 * HEAD_DIM

    def kv_copy(r, i):
        return remote(dkv.at[r, i], dkv_in.at[r - 1, i], kv_s.at[r, i], kv_r.at[r, i], seq=place - 1)

    def kv_send(r, i):
        @pl.when(place >= r)
        def _():
            kv_copy(r, i).start()

    def kv_take(r, i):
        gets = (place + 1 >= r) & (place + 1 < seq)

        @pl.when(gets)
        def _():
            kv_copy(r, i).wait_recv()
            add_rows(tokens, dkv.at[r - 1, i], dkv_in.at[r - 1, i])

    def mid_down(k):
        s = k % 2
        at = pl.multiple_of(k * COLS, 128)
        for made in mid_loads(k):
            made.wait()
        for half in range(2):
            lo = half * part_d
            dh = nt(eb_ref[...], wt[s, :part_d, half * model : (half + 1) * model])
            rights[:, pl.ds(at + lo, part_d)] = (dh * slope[s, :, lo : lo + part_d]).astype(BF)
            rights[:, pl.ds(ff + at + lo, part_d)] = (dh * swish[s, :, lo : lo + part_d]).astype(BF)
        for j in range(model // COLS):
            span = slice(j * COLS, (j + 1) * COLS)
            out_ref[:, span] += sum(
                nn(
                    hid[s, :, half * part_d : (half + 1) * part_d],
                    wt[s, :part_d, half * model + j * COLS : half * model + (j + 1) * COLS],
                )
                for half in range(2)
            )

        @pl.when(k + 2 < ff // COLS)
        def _():
            for made in mid_loads(k + 2):
                made.start()

    def mid_ff(j):
        at = pl.multiple_of(j * TILE, 128)
        for i in range(2):
            ff_load(j, i).wait()
        dn1[:, pl.ds(at, TILE)] = nt(rights[:, :ff], wt[0, :, :ff]) + nt(rights[:, ff : 2 * ff], wt[1, :, :ff])

        @pl.when(j + 1 < model // TILE)
        def _():
            for i in range(2):
                ff_load(j + 1, i).start()

    def mid_out():
        x2 = x2_ref[...]
        scale = lax.rsqrt(jnp.mean(x2 * x2, axis=1, keepdims=True) + EPS)
        unit = x2 * scale
        grad = dn1[...]
        term2[0:1, :] = jnp.sum(grad * unit, axis=0, keepdims=True)
        scaled = grad * gains_ref[1:2, :]
        inner = jnp.mean(scaled * unit, axis=1, keepdims=True)
        e2 = eb_ref[...].astype(F32) + scale * (scaled - unit * inner)
        dx_ref[...] = e2
        rights[:, 2 * ff : 2 * ff + model] = e2.astype(BF)
        for t in range(model // TILE):
            o_load(t).wait()
            do = nt(rights[:, 2 * ff : 2 * ff + model], wt[t % 2, :, t // 2 * model : (t // 2 + 1) * model]).astype(BF)
            for i in range(TILE // HEAD_DIM):
                doh[t * (TILE // HEAD_DIM) + i] = do[:, i * HEAD_DIM : (i + 1) * HEAD_DIM]

    def turn_back(value):
        ahead = pltpu.roll(value, TILE - HEAD_DIM // 2, 1)
        behind = pltpu.roll(value, HEAD_DIM // 2, 1)
        return (value * cos_ref[...] - behind * second_ref[...] + ahead * first_ref[...]).astype(BF)

    q_at = (gu_panels + o_panels) * COLS

    def w_load(t, i):
        at = pl.multiple_of(t * TILE, 16)
        s = t % 2
        src, lo, width = ((wq_in, 0, model), (wk_in, model, kvd), (wv_in, model + kvd, kvd))[i]
        return pltpu.make_async_copy(src.at[pl.ds(at, TILE)], wt.at[s, :, pl.ds(lo, width)], w_sem.at[s, i])

    def last_norm():
        for h in range(HEADS):
            rights[:, q_at + h * HEAD_DIM : q_at + (h + 1) * HEAD_DIM] = dqh[h]
        for t in range(model // TILE):
            at = q_at + t * TILE
            rights[:, at : at + TILE] = turn_back(rights[:, at : at + TILE].astype(F32))
        for t in range(kvd // TILE):
            at = q_at + model + t * TILE
            pieces = [dkv[0, 2 * t + i, :, :pair_width] for i in range(2)]
            rights[:, at : at + TILE] = turn_back(jnp.concatenate(pieces, axis=1).astype(F32))
        for i in range(KV_HEADS // 2):
            at = q_at + model + kvd + i * pair_width
            rights[:, at : at + pair_width] = dkv[0, i, :, pair_width:]
        for i in range(3):
            w_load(0, i).start()

        @pl.loop(0, model // TILE)
        def _(t):
            for i in range(3):
                w_load(t, i).wait()

            @pl.when(t + 1 < model // TILE)
            def _():
                for i in range(3):
                    w_load(t + 1, i).start()

            dn1[:, pl.ds(pl.multiple_of(t * TILE, 128), TILE)] = nt(rights[:, q_at:], wt[t % 2, :, : model + 2 * kvd])

        x = x_ref[...].astype(F32)
        scale = lax.rsqrt(jnp.mean(x * x, axis=1, keepdims=True) + EPS)
        unit = x * scale
        grad = dn1[...]
        term = jnp.sum(grad * unit, axis=0, keepdims=True)
        scaled = grad * gains_ref[0:1, :]
        inner = jnp.mean(scaled * unit, axis=1, keepdims=True)
        dx_ref[...] += scale * (scaled - unit * inner)
        for k in range(8):
            gsend[k, 0:1, :rows] = term[:, k * rows : (k + 1) * rows]
            gsend[k, 1:2, :rows] = term2[0:1, k * rows : (k + 1) * rows]

    def gain_copies():
        return [
            remote(gsend.at[me ^ off], grecv.at[me], g_s.at[off], g_r.at[off], dp=me ^ off) for off in range(1, 8)
        ]

    def gain_line():
        return [
            remote(gsum, gzrecv.at[place], gz_s.at[far], gz_r.at[far], seq=(place + far) % seq) for far in range(1, seq)
        ]

    ticks = total_chunks + last_lag
    pairs = KV_HEADS // 2
    d_steps, f_steps = ff // COLS, model // TILE
    d_ticks = d_steps // 2
    out_at = (d_ticks + f_steps) // 2
    first_at = out_at + 1
    norm_at = first_at + pairs + seq - 2
    assert d_ticks <= d_chunks and 2 * norm_at + 1 < total_chunks - 2 * o_panels

    @pl.loop(0, -(-ticks // 2))
    def _(p):
        for parity in range(2):
            c = 2 * p + parity
            tick(c, parity)

            @pl.when(c < d_ticks)
            def _():
                @pl.loop(0, 2)
                def _(i):
                    mid_down(2 * c + i)

            @pl.when(c == d_ticks - 1)
            def _():
                for i in range(2):
                    ff_load(0, i).start()

            @pl.when((c >= d_ticks) & (c < d_ticks + f_steps))
            def _():
                mid_ff(c - d_ticks)

        @pl.when(p == out_at - 1)
        def _():
            for t in range(f_steps):
                o_load(t).start()

        @pl.when(p == out_at)
        def _():
            mid_out()

        for r in range(seq - 1, 0, -1):
            piece = p - first_at - (seq - r)

            @pl.when((piece >= 0) & (piece < pairs))
            def _():
                kv_take(r, piece)
                if r > 1:
                    kv_send(r - 1, piece)

        @pl.when((p >= first_at) & (p < first_at + pairs))
        def _():
            piece = p - first_at
            for i in range(2):
                g = 2 * piece + i
                back_group(place, seq, g, i, qh, doh, lse_ref[...], kh.at[g], vh.at[g], dqh, dkh, dvh, acc_k, acc_v)
            for r in range(seq):
                for i in range(2):
                    span = slice(r * tokens, (r + 1) * tokens)
                    dkv[r, piece, :, i * HEAD_DIM : (i + 1) * HEAD_DIM] = dkh[i, span, :]
                    lo = pair_width + i * HEAD_DIM
                    dkv[r, piece, :, lo : lo + HEAD_DIM] = dvh[i, span, :]
            kv_send(seq - 1, piece)

        @pl.when(p == norm_at)
        def _():
            last_norm()
            for made in gain_copies():
                made.start()
            grecv[me] = gsend[me]

        @pl.when(p == norm_at + 1)
        def _():
            for made in gain_copies():
                made.wait_recv()
            gsum[...] = sum(grecv[k] for k in range(1, 8)) + grecv[0]
            gzrecv[place] = gsum[...]
            for made in gain_line():
                made.start()

        @pl.when(p == norm_at + 2)
        def _():
            for made in gain_line():
                made.wait_recv()
            gain_out[...] = sum(gzrecv[k] for k in range(seq))

    for made in gain_copies() + gain_line():
        made.wait_send()
    for r in range(1, seq):
        @pl.when(place >= r)
        def _():
            for i in range(pairs):
                kv_copy(r, i).wait_send()
    for c in range(total_chunks - SLOTS_CORE, total_chunks):
        core_copy(c).wait_send()
    for way in range(2):
        for hop in range(1, seq):
            for c in range(total_chunks - SLOTS, total_chunks):
                @pl.when(z_sends(way, hop))
                def _():
                    z_copy(c, way, hop).wait_send()
            for c in range(total_chunks - SLOTS_OUT, total_chunks):
                @pl.when(a_sends(way, hop))
                def _():
                    a_copy(c, way, hop).wait_send()
    for c in range(total_chunks - SLOTS_OUT, total_chunks):
        own_copy(c).wait()


def backward_call(seq, x, gains, x2, tables, hidden_t, eb, lefts, qh, kh, vh, lse, weights, hidden, slope, swish):
    tokens, model = x.shape
    rows = model // 8
    sub = rows // seq
    kvd, ff = weights[1].shape[1], hidden.shape[1]
    wide = 2 * ff + 2 * model + 2 * kvd
    chunks = hidden_t.shape[0] // 8 * 3 // rows + wide // COLS
    anyspec = pl.BlockSpec(memory_space=pl.ANY)
    vmem = pl.BlockSpec(memory_space=pltpu.VMEM)
    dma, regular = pltpu.SemaphoreType.DMA, pltpu.SemaphoreType.REGULAR
    hops = 2 * (seq - 1)
    heads = pltpu.VMEM((HEADS, tokens, HEAD_DIM), BF)
    keys = pltpu.VMEM((2, seq * tokens, HEAD_DIM), BF)
    panel = pltpu.VMEM((2, tokens, COLS), F32)
    pieces = KV_HEADS // 2
    return pl.pallas_call(
        functools.partial(backward_body, seq),
        out_shape=[
            jax.ShapeDtypeStruct((tokens, model), F32),
            jax.ShapeDtypeStruct((8, 256), F32),
            jax.ShapeDtypeStruct((tokens, model), F32),
            jax.ShapeDtypeStruct((chunks * rows, COLS), BF),
        ],
        in_specs=[vmem] * 13 + [anyspec] * 10,
        out_specs=[vmem, vmem, vmem, anyspec],
        scratch_shapes=[
            pltpu.VMEM((tokens, wide), BF),
            heads, heads, keys, keys,
            pltpu.VMEM((seq * tokens, HEAD_DIM), F32),
            pltpu.VMEM((seq * tokens, HEAD_DIM), F32),
            pltpu.VMEM((seq, pieces, tokens, 4 * HEAD_DIM), BF),
            pltpu.VMEM((seq - 1, pieces, tokens, 4 * HEAD_DIM), BF),
            pltpu.VMEM((tokens, model), F32),
            pltpu.VMEM((2, TILE, max(ff, 2 * model)), BF),
            pltpu.VMEM((2, tokens, COLS), BF),
            panel, panel,
            pltpu.VMEM((8, model), F32),
            pltpu.VMEM((SLOTS_CORE, 4 * rows, COLS), BF),
            pltpu.VMEM((SLOTS_CORE, 4 * rows, COLS), BF),
            pltpu.VMEM((SLOTS_SUM, 4 * rows, COLS), BF),
            pltpu.VMEM((SLOTS, 2 * rows, COLS), BF),
            pltpu.VMEM((SLOTS, rows, COLS), BF),
            pltpu.VMEM((hops, SLOTS, sub, COLS), BF),
            pltpu.VMEM((hops, SLOTS, sub, COLS), BF),
            pltpu.VMEM((SLOTS_OUT, sub, COLS), BF),
            pltpu.VMEM((8, 8, 256), F32),
            pltpu.VMEM((8, 8, 256), F32),
            pltpu.VMEM((8, 256), F32),
            pltpu.VMEM((seq, 8, 256), F32),
            dma((2, 5)), dma((2, 3)),
            dma((SLOTS_CORE,)), dma((SLOTS_CORE,)),
            dma((SLOTS,)), dma((SLOTS,)),
            dma((SLOTS,)), dma((SLOTS,)),
            dma((hops, SLOTS)), dma((hops, SLOTS)),
            dma((hops, SLOTS_OUT)), dma((hops, SLOTS_OUT)),
            dma((SLOTS_OUT,)),
            dma((seq, pieces)), dma((seq, pieces)),
            dma((8,)), dma((8,)),
            dma((seq,)), dma((seq,)),
            regular, regular((2,)), regular((2,)), regular((hops,)),
        ],
        compiler_params=pltpu.CompilerParams(
            collective_id=1, has_side_effects=True, vmem_limit_bytes=62 * 1024 * 1024
        ),
        name="backward",
    )(x, gains, x2, *tables, hidden_t, eb, lefts, qh, kh, vh, lse, *weights, hidden, slope, swish)


def finish_call(res, dx, result, d_rows, ff, kvd):
    tokens, model = dx.shape
    block = res.shape[1]
    steps = 4
    per_d, per_f, per_m = d_rows * 3 // block // steps, ff // COLS // steps, model // COLS
    at_f = per_d * steps // per_f
    at_m = per_d * steps + 2 * per_f * steps
    panel = block // 3
    assert per_d and per_f and per_d * steps % per_f == 0 and per_m < steps

    def body(d_in, g_in, u_in, o_in, q_in, kv_in, dx_in, y_in, down, gate, up, out, query, key, value, dx_out, y_out):
        s = pl.program_id(0)
        dx_out[...] = dx_in[...]
        y_out[...] = y_in[...]
        for i in range(per_d):
            for j in range(3):
                down[i * panel : (i + 1) * panel, j * COLS : (j + 1) * COLS] = d_in[i, j * panel : (j + 1) * panel, :].astype(F32)
        for i in range(per_f):
            gate[:, i * COLS : (i + 1) * COLS] = g_in[i].astype(F32)
            up[:, i * COLS : (i + 1) * COLS] = u_in[i].astype(F32)
        for i in range(per_m):

            @pl.when(s == i)
            def _():
                out[:, i * COLS : (i + 1) * COLS] = o_in[0].astype(F32)
                query[:, i * COLS : (i + 1) * COLS] = q_in[0].astype(F32)
                mid = min(max(kvd - i * COLS, 0), COLS)
                if mid:
                    key[:, i * COLS : i * COLS + mid] = kv_in[0, :, :mid].astype(F32)
                if mid < COLS:
                    lo = i * COLS + mid - kvd
                    value[:, lo : lo + COLS - mid] = kv_in[0, :, mid:].astype(F32)

    def chunk(count, at):
        return pl.BlockSpec((count, block, COLS), at)

    wide = lambda base: chunk(per_f, lambda s: (base + s, 0, 0))
    thin = lambda base: chunk(1, lambda s: (base + jnp.minimum(s, per_m - 1), 0, 0))
    line = pl.BlockSpec((tokens // steps, model), lambda s: (s, 0))
    whole = lambda width: pl.BlockSpec((block, width), lambda s: (0, 0))
    return pl.pallas_call(
        body,
        grid=(steps,),
        in_specs=[
            chunk(per_d, lambda s: (s, 0, 0)),
            wide(at_f),
            wide(at_f + steps),
            thin(at_m),
            thin(at_m + per_m),
            thin(at_m + 2 * per_m),
            line,
            line,
        ],
        out_specs=[
            pl.BlockSpec((d_rows // steps, model), lambda s: (s, 0)),
            pl.BlockSpec((block, ff // steps), lambda s: (0, s)),
            pl.BlockSpec((block, ff // steps), lambda s: (0, s)),
            whole(model),
            whole(model),
            whole(kvd),
            whole(kvd),
            line,
            line,
        ],
        out_shape=[
            jax.ShapeDtypeStruct((d_rows, model), F32),
            jax.ShapeDtypeStruct((block, ff), F32),
            jax.ShapeDtypeStruct((block, ff), F32),
            jax.ShapeDtypeStruct((block, model), F32),
            jax.ShapeDtypeStruct((block, model), F32),
            jax.ShapeDtypeStruct((block, kvd), F32),
            jax.ShapeDtypeStruct((block, kvd), F32),
            jax.ShapeDtypeStruct((tokens, model), F32),
            jax.ShapeDtypeStruct((tokens, model), F32),
        ],
        compiler_params=pltpu.CompilerParams(vmem_limit_bytes=60 * 1024 * 1024),
        name="finish",
    )(*[res] * 6, dx, result)


def attend_back(place, qh, kh, vh, doh, lse):
    chunks = kh.shape[1] // qh.shape[1]

    def body(place_ref, q_ref, k_ref, v_ref, do_ref, lse_ref, dq_ref, dk_ref, dv_ref, acc_k, acc_v):
        @pl.loop(0, KV_HEADS)
        def _(g):
            back_group(place_ref[0], chunks, g, g, q_ref, do_ref, lse_ref[...], k_ref.at[g], v_ref.at[g], dq_ref, dk_ref, dv_ref, acc_k, acc_v)

    vmem = pl.BlockSpec(memory_space=pltpu.VMEM)
    acc = pltpu.VMEM(kh.shape[1:], F32)
    return pl.pallas_call(
        body,
        in_specs=[pl.BlockSpec(memory_space=pltpu.SMEM)] + [vmem] * 5,
        out_specs=[vmem] * 3,
        out_shape=[jax.ShapeDtypeStruct(a.shape, BF) for a in (qh, kh, vh)],
        scratch_shapes=[acc, acc],
        name="attend_back",
    )(place, qh, kh, vh, doh, lse)


def flip(value, axis, bit):
    size = lax.axis_size(axis)
    return lax.ppermute(value, axis, [(i, i ^ bit) for i in range(size)])


def xor_order(bits):
    order = [0]
    for bit in list(reversed(bits)) + [1]:
        order = order + [off ^ bit for off in order]
    return order


def scatter_term(left, right, bits):
    half = left.shape[1] // 2
    away = tn(left[:, half:], right).astype(BF)
    came = flip(away, "dp", 1)
    quarter = half // 2
    away = (tn(left[:, quarter:half], right) + came[quarter:]).astype(BF)
    kept = (tn(left[:, :quarter], right) + came[:quarter]).astype(BF)
    came = flip(away, "dp", bits[0])
    for bit in bits[1:]:
        size = kept.shape[0] // 2
        away = (kept[size:].astype(F32) + came[size:]).astype(BF)
        kept = (kept[:size].astype(F32) + came[:size]).astype(BF)
        came = flip(away, "dp", bit)
    return (kept.astype(F32) + came).astype(BF)


def line_sum(value, place):
    size = lax.axis_size("seq")
    rows = value.shape[0] // size

    def chunk(index):
        index = jnp.clip(index, 0, size - 1)
        return lax.dynamic_slice_in_dim(value, index * rows, rows, 0)

    total = chunk(place).astype(F32)
    for way in (1, -1):
        held = None
        for far in range(size - 1, 0, -1):
            mine = chunk(place + way * far)
            if held is not None:
                mine = (mine.astype(F32) + held).astype(BF)
            pairs = [(i, i + way) for i in range(size) if 0 <= i + way * far < size]
            held = lax.ppermute(mine, "seq", pairs)
        total = total + held
    total = total.astype(BF)
    out = jnp.zeros(value.shape, F32)
    out = lax.dynamic_update_slice(out, total.astype(F32), (place * rows, 0))
    for way in (1, -1):
        held = total
        for far in range(1, size):
            pairs = [
                (i, i + way) for i in range(size) if 0 <= i + way < size and 0 <= i - way * (far - 1) < size
            ]
            held = lax.ppermute(held, "seq", pairs)
            source = place - way * far
            index = jnp.clip(source, 0, size - 1) * rows
            old = lax.dynamic_slice(out, (index, 0), held.shape)
            good = (source >= 0) & (source < size)
            out = lax.dynamic_update_slice(
                out, jnp.where(good, held.astype(F32), old), (index, 0)
            )
    return out


def rope_tables(place, tokens, width):
    half = HEAD_DIM // 2
    positions = (place * tokens + jnp.arange(tokens, dtype=jnp.int32)).astype(F32)
    frequency = ROPE_BASE ** (-jnp.arange(half).astype(F32) / half)
    angles = positions[:, None] * frequency[None, :]
    cos, sin = jnp.cos(angles), jnp.sin(angles)
    zero = jnp.zeros_like(sin)
    heads = width // HEAD_DIM
    tile = lambda a, b: jnp.tile(jnp.concatenate([a, b], axis=1), (1, heads))
    return tile(cos, cos), tile(sin, zero), tile(zero, sin)


def rotate(field, tables, sign):
    cos, first, second = tables
    half = HEAD_DIM // 2
    width = field.shape[1]
    cos, first, second = cos[:, :width], first[:, :width], second[:, :width]
    ahead = jnp.concatenate([field[:, half:], field[:, :half]], axis=1)
    behind = jnp.concatenate([field[:, -half:], field[:, :-half]], axis=1)
    return field * cos + sign * (behind * second - ahead * first)


def norm_scale(values):
    return lax.rsqrt(jnp.mean(values * values, axis=-1, keepdims=True) + EPS)


def norm_back(values, scale, gain, grad):
    unit = values * scale
    grad_gain = jnp.sum(grad * unit, axis=0)
    scaled = grad * gain
    inner = jnp.mean(scaled * unit, axis=-1, keepdims=True)
    return scale * (scaled - unit * inner), grad_gain


def local(tokens, cotangent, w_query, w_key, w_value, w_out, w_gate, w_up, w_down, gain_attn, gain_mlp):
    dp, seq = lax.axis_size("dp"), lax.axis_size("seq")
    me, place = lax.axis_index("dp"), lax.axis_index("seq")
    bits = [1 << i for i in range(1, dp.bit_length() - 1)]
    turned = bits[1:] + bits[:1]
    model = tokens.shape[-1]
    rows = tokens.shape[1]
    kvd = w_key.shape[-1]
    place_arr = place.reshape(1).astype(jnp.int32)

    half_model = model // 2

    def xor_columns(value, way):
        width = value.shape[1] // dp
        cut = lambda off: lax.dynamic_slice_in_dim(value, (me ^ off) * width, width, 1)
        return jnp.concatenate([cut(off) for off in xor_order(way)], axis=1)

    tables = rope_tables(place, rows, model)
    x = tokens[0].astype(F32)
    packed = jnp.zeros((8, 256), F32)
    packed = packed.at[0, : gain_attn.shape[1]].set(gain_attn[0].astype(F32))
    packed = packed.at[1, : gain_mlp.shape[1]].set(gain_mlp[0].astype(F32))
    shards = [w[0] for w in (w_query, w_key, w_value, w_out, w_gate, w_up, w_down)]
    outs = forward_call(dp, seq, tokens[0], packed, [t[:, :TILE] for t in tables], shards)
    w_q, w_k, w_v, w_o, w_g, w_u, w_d = outs[:7]
    qh, kh, vh, lefts, x2, hidden, hidden_t, slope, swish, lse, gains = outs[7:]
    gain_one, gain_two = gains[0:1], gains[1:2]
    eb = cotangent[0]
    if len(bits) == 2 and (model // dp) % (16 * seq) == 0:
        dx, grads, result, res = backward_call(
            seq, tokens[0], gains, x2, [t[:, :TILE] for t in tables], hidden_t, eb, lefts,
            qh, kh, vh, lse, outs[:7], hidden, slope, swish,
        )
        block = model // dp
        g_down, g_gate, g_up, g_out, g_query, g_key, g_value, dx, result = finish_call(
            res.reshape(-1, block, COLS), dx, result, w_down.shape[1], w_gate.shape[2], kvd
        )
        return (
            result[None],
            dx[None],
            g_query[None],
            g_key[None],
            g_value[None],
            g_out[None],
            g_gate[None],
            g_up[None],
            g_down[None],
            grads[0:1, :block],
            grads[1:2, :block],
        )

    scale_one = norm_scale(x)
    scale_two = norm_scale(x2)
    result = x2 + nn(hidden, w_d)
    e = eb.astype(F32)
    dh = nt(eb, w_d)
    dgate = (dh * slope).astype(BF)
    dup = (dh * swish).astype(BF)
    dn2 = nt(dgate, w_g) + nt(dup, w_u)
    dx2, term_gain_two = norm_back(x2, scale_two, gain_two, dn2)
    e2 = e + dx2
    e2b = e2.astype(BF)
    do = nt(e2b, w_o).astype(BF)
    n2, mixed, n1 = (lefts[i * model : (i + 1) * model].T for i in range(3))
    hidden_a = xor_columns(hidden, bits)
    hidden_b = xor_columns(hidden, turned)
    sum_down = jnp.concatenate(
        [
            scatter_term(hidden_a, eb[:, :half_model], bits),
            scatter_term(hidden_b, eb[:, half_model:], turned),
        ],
        axis=1,
    )
    n2_a, n2_b = xor_columns(n2, bits), xor_columns(n2, turned)
    sum_gate = scatter_term(n2_a, dgate, bits)
    sum_up = scatter_term(n2_b, dup, turned)
    mixed_a, mixed_b = xor_columns(mixed, bits), xor_columns(mixed, turned)
    sum_out = jnp.concatenate(
        [
            scatter_term(mixed_a, e2b[:, :half_model], bits),
            scatter_term(mixed_b, e2b[:, half_model:], turned),
        ],
        axis=1,
    )
    doh = do.reshape(rows, HEADS, HEAD_DIM).transpose(1, 0, 2)
    dqh, dkh, dvh = attend_back(place_arr, qh, kh, vh, doh, lse)
    dq = dqh.transpose(1, 0, 2).reshape(rows, model)
    dks, dvs = (a.reshape(KV_HEADS, seq, rows, HEAD_DIM).transpose(1, 2, 0, 3).reshape(seq, rows, kvd) for a in (dkh, dvh))
    held = None
    for far in range(seq - 1, -1, -1):
        mine = jnp.concatenate([dks[far], dvs[far]], axis=1)
        if held is not None:
            mine = (mine.astype(F32) + held).astype(BF)
        if far:
            held = lax.ppermute(mine, "seq", [(i, i - 1) for i in range(far, seq)])
    dk, dv = mine[:, :kvd], mine[:, kvd:]
    dqp = rotate(dq.astype(F32), tables, -1.0).astype(BF)
    dkp = rotate(dk.astype(F32), tables, -1.0).astype(BF)
    n1_a, n1_b = xor_columns(n1, bits), xor_columns(n1, turned)
    sum_query = scatter_term(n1_a, dqp, bits)
    sum_kv = scatter_term(n1_b, jnp.concatenate([dkp, dv], axis=1), turned)
    dn1 = nt(dqp, w_q) + nt(dkp, w_k) + nt(dv, w_v)
    dx1, term_gain_one = norm_back(x, scale_one, gain_one, dn1)
    input_grad = e2 + dx1

    both = jnp.stack([term_gain_one, term_gain_two])
    for bit in [1] + bits:
        both = both + flip(both, "dp", bit)
    for bit in [1 << i for i in range(seq.bit_length() - 1)]:
        both = both + flip(both, "seq", bit)
    width = model // dp
    both = lax.dynamic_slice_in_dim(both, me * width, width, 1)

    g_down = line_sum(sum_down, place)
    g_gate = line_sum(sum_gate, place)
    g_up = line_sum(sum_up, place)
    g_out = line_sum(sum_out, place)
    g_query = line_sum(sum_query, place)
    g_kv = line_sum(sum_kv, place)
    return (
        result[None],
        input_grad[None],
        g_query[None],
        g_kv[None, :, :kvd],
        g_kv[None, :, kvd:],
        g_out[None],
        g_gate[None],
        g_up[None],
        g_down[None],
        both[0:1],
        both[1:2],
    )


def solution(mesh):
    by_token = P("dp", "seq", None)
    by_row = P(None, "dp", None)
    by_gain = P(None, "dp")
    in_specs = (by_token,) * 2 + (by_row,) * 7 + (by_gain,) * 2
    return jax.shard_map(local, mesh=mesh, in_specs=in_specs, out_specs=in_specs, check_vma=False)
```

```python
import functools

import jax
import jax.numpy as jnp
from jax import lax
from jax.experimental import pallas as pl
from jax.experimental.pallas import tpu as pltpu
from jax.sharding import PartitionSpec as P

HEADS = 16
KV_HEADS = 8
HEAD_DIM = 96
GROUP = HEADS // KV_HEADS
EPS = 1e-05
ROPE_BASE = 100000.0
BF = jnp.bfloat16
F32 = jnp.float32
NEG = -1e30
SCALE = HEAD_DIM ** (-0.5)


def dot(a, b, dims):
    return lax.dot_general(a, b, (dims, ((), ())), preferred_element_type=F32)


def nn(a, b):
    return dot(a, b, ((1,), (0,)))


def nt(a, b):
    return dot(a, b, ((1,), (1,)))


def tn(a, b):
    return dot(a, b, ((0,), (0,)))


def lanes(ref, head, width=HEAD_DIM):
    return ref[:, head * HEAD_DIM : head * HEAD_DIM + width]


MESH = pl.DeviceIdType.MESH
TILE = 4 * HEAD_DIM
COLS = 512


class Gather:
    def __init__(self, me, place, bits, src, out, send, recv):
        self.me, self.bits, self.src, self.out = me, bits, src, out
        self.send, self.recv = send, recv
        self.rows = src.shape[0]
        self.quarter = -(-self.rows // 96) * 16
        self.most = self.rows - self.quarter
        units, parts = self.most // 16, len(bits)
        self.size = [16 * (units // parts + (i < units % parts)) for i in range(parts)]
        self.start = [sum(self.size[:i]) for i in range(parts)]
        self.odd = place % 2
        self.pair = place + 1 - 2 * self.odd
        self.count = 0
        self.waits = []
        own = {}
        for bit in bits:
            own[bit] = self.copy(self.src, 0, 1, self.most, bit, self.odd * self.quarter)
        self.own = own
        self.own_core = self.copy(self.src, 0, 0, self.rows, 1, 0)
        self.forwards = []
        self.arrival = {}
        for bit in bits:
            for i in range(len(bits)):
                self.arrival[(bit, i)] = own[bit]
        for step in range(1, len(bits)):
            for i in range(len(bits)):
                order = bits[i:] + bits[:i]
                bit = order[step]
                held = [0]
                for b in order[:step]:
                    held = held + [m | b for m in held]
                for m in held[1:]:
                    start = self.odd * self.quarter + self.start[i]
                    made = self.copy(out, m, 1, self.size[i], bit, start)
                    self.forwards.append((m, i, made))
                    self.arrival[(m | bit, i)] = made
        masks = list(range(2, 2 * max(bits), 2))
        self.masks = masks
        self.across = [
            self.copy(out, m, 2, self.quarter, 0, self.odd * self.most) for m in masks
        ]
        self.core = [self.copy(out, m, 1, self.rows, 1, 0) for m in masks]
        self.seen = set()

    def copy(self, ref, m, kind, rows, bit, start):
        at = (self.me ^ m) * self.rows + start
        source = ref.at[pl.ds(pl.multiple_of(start, 16), rows)] if ref is self.src else ref.at[pl.ds(pl.multiple_of(at, 16), rows)]
        target = {"seq": self.pair} if kind == 2 else {"dp": self.me ^ bit}
        index = self.count
        self.count += 1
        return pltpu.make_async_remote_copy(
            src_ref=source,
            dst_ref=self.out.at[pl.ds(pl.multiple_of(at, 16), rows)],
            send_sem=self.send.at[index],
            recv_sem=self.recv.at[index],
            device_id=target,
            device_id_type=MESH,
        )

    def begin(self):
        for bit in self.bits:
            self.own[bit].start()
        self.own_core.start()

    def arrived(self, copy):
        if id(copy) not in self.seen:
            self.seen.add(id(copy))
            copy.wait_recv()

    def forward(self):
        for m, i, made in self.forwards:
            self.arrived(self.arrival[(m, i)])
            made.start()

    def chosen(self, near):
        return [i for i, m in enumerate(self.masks) if near is None or (m in self.bits) == near]

    def cross(self, near=None):
        for at in self.chosen(near):
            for i in range(len(self.bits)):
                self.arrived(self.arrival[(self.masks[at], i)])
            self.across[at].start()

    def share(self, near=None):
        for at in self.chosen(near):
            self.across[at].wait_recv()
            self.core[at].start()

    def finish(self):
        self.own_core.wait_recv()
        for made in self.core:
            made.wait_recv()

    def drain(self):
        for made in list(self.own.values()) + [self.own_core] + [f[2] for f in self.forwards] + self.across + self.core:
            made.wait_send()


def gather_copies(chip_bits):
    forwards = sum(chip_bits * (2**step - 1) for step in range(1, chip_bits))
    return chip_bits + 1 + forwards + 2 * (2**chip_bits - 1)


def forward_body(dp, seq, x_ref, gain_ref, cos_ref, first_ref, second_ref, *refs):
    w_in, refs = refs[:7], refs[7:]
    w_out, refs = refs[:7], refs[7:]
    kept, lse_ref, gains_ref, refs = refs[:9], refs[9], refs[10], refs[11:]
    made, stage, refs = refs[:9], refs[9:16], refs[16:]
    qh, kh, vh, lefts, x2_ref, hidden, hidden_t, slope, swish = made
    (wq, wk, wv, kvbuf, gbuf, oh, n1_ref, n2_ref, o_ref, wt, send, recv, kv_send, kv_recv, g_send, g_recv, own_sem,
     load_sem, tile_sem, keep_sem) = refs
    me, place = lax.axis_index("dp"), lax.axis_index("seq")
    bits = [1 << i for i in range(1, dp.bit_length() - 1)]
    tokens, model = x_ref.shape
    block = model // dp

    for i in range(7):
        pltpu.make_async_copy(w_in[i], stage[i], own_sem.at[i]).start()
    for r in range(1, seq):
        kvbuf[r] = jnp.zeros_like(kvbuf[r])

    barrier = pltpu.get_barrier_semaphore()
    for off in range(1, dp):
        pl.semaphore_signal(barrier, inc=1, device_id={"dp": me ^ off}, device_id_type=MESH)
    up, down = place + 1, place - 1
    odd = place % 2
    pair = place + 1 - 2 * odd
    other = place - 1 + 2 * odd
    has_other = (other >= 0) & (other < seq)
    pl.semaphore_signal(barrier, inc=1, device_id={"seq": pair}, device_id_type=MESH)

    @pl.when(has_other)
    def _():
        pl.semaphore_signal(barrier, inc=1, device_id={"seq": other}, device_id_type=MESH)

        pl.semaphore_wait(barrier, dp + 1)

    @pl.when(jnp.logical_not(has_other))
    def _():
        pl.semaphore_wait(barrier, dp)

    gains = [
        pltpu.make_async_remote_copy(
            src_ref=gain_ref,
            dst_ref=gbuf.at[me],
            send_sem=g_send.at[off],
            recv_sem=g_recv.at[off],
            device_id={"dp": me ^ off},
            device_id_type=MESH,
        )
        for off in range(1, dp)
    ]
    for g in gains:
        g.start()
    turned = bits[1:] + bits[:1]
    jobs = [
        Gather(me, place, turned if i in (1, 2, 5) else bits, w_in[i], w_out[i], send.at[i], recv.at[i])
        for i in range(7)
    ]
    first = jobs[:3]
    job_o, job_g, job_u, job_d = jobs[3:]
    for job in first:
        job.begin()

    def own_out(i):
        rows = w_in[i].shape[0]
        return pltpu.make_async_copy(stage[i], w_out[i].at[pl.ds(pl.multiple_of(me * rows, 8), rows)], own_sem.at[i])

    for i in range(7):
        pltpu.make_async_copy(w_in[i], stage[i], own_sem.at[i]).wait()
        own_out(i).start()

    gbuf[me] = gain_ref[...]
    x = x_ref[...].astype(F32)
    scale = lax.rsqrt(jnp.mean(x * x, axis=1, keepdims=True) + EPS)
    for g in gains:
        g.wait_recv()
    for k in range(dp):
        gains_ref[:, k * block : (k + 1) * block] = gbuf[k, :, :block]
    n1_ref[...] = (x * scale * gains_ref[0:1, :]).astype(BF)

    def keep(i):
        return pltpu.make_async_copy(made[i], kept[i], keep_sem.at[i])

    def put_left(which, source):
        @pl.loop(0, model // TILE)
        def _(t):
            at = pl.multiple_of(t * TILE, 128)
            lefts[pl.ds(pl.multiple_of(which * model + at, 16), TILE), :] = source[:, pl.ds(at, TILE)].T

    for job in first:
        job.forward()
    job_o.begin()
    job_g.begin()
    for job in first:
        job.cross()
    for job in first:
        job.share()
    for i in range(7):
        own_out(i).wait()
    for job in first:
        job.finish()
    loads = [
        pltpu.make_async_copy(w_out[i], ref, load_sem.at[i]) for i, ref in enumerate((wq, wk, wv))
    ]
    for load in loads:
        load.start()

    def turn(value):
        ahead = pltpu.roll(value, TILE - HEAD_DIM // 2, 1)
        behind = pltpu.roll(value, HEAD_DIM // 2, 1)
        return value * cos_ref[...] + behind * second_ref[...] - ahead * first_ref[...]

    kvd = wk.shape[1]
    loads[1].wait()

    @pl.loop(0, kvd // TILE)
    def _(t):
        at = pl.multiple_of(t * TILE, 128)
        kvbuf[0, :, pl.ds(at, TILE)] = turn(nn(n1_ref[...], wk[:, pl.ds(at, TILE)])).astype(BF)

    loads[2].wait()

    @pl.loop(0, kvd // TILE)
    def _(t):
        at = pl.multiple_of(t * TILE, 128)
        kvbuf[0, :, pl.ds(kvd + at, TILE)] = nn(n1_ref[...], wv[:, pl.ds(at, TILE)]).astype(BF)

    def kv_copy(r):
        return pltpu.make_async_remote_copy(
            src_ref=kvbuf.at[r],
            dst_ref=kvbuf.at[r + 1],
            send_sem=kv_send.at[r],
            recv_sem=kv_recv.at[r],
            device_id={"seq": up},
            device_id_type=MESH,
        )

    def kv_send_on(r):
        @pl.when((place >= r) & (place < seq - 1))
        def _():
            kv_copy(r).start()

    def kv_wait(r):
        @pl.when(place >= r)
        def _():
            pltpu.make_async_remote_copy(
                src_ref=kvbuf.at[r - 1],
                dst_ref=kvbuf.at[r],
                send_sem=kv_send.at[r - 1],
                recv_sem=kv_recv.at[r - 1],
                device_id={"seq": down},
                device_id_type=MESH,
            ).wait_recv()

    kv_send_on(0)
    loads[0].wait()

    @pl.loop(0, model // TILE)
    def _(t):
        at = pl.multiple_of(t * TILE, 128)
        q = turn(nn(n1_ref[...], wq[:, pl.ds(at, TILE)])).astype(BF)
        for i in range(TILE // HEAD_DIM):
            qh[t * (TILE // HEAD_DIM) + i] = q[:, i * HEAD_DIM : (i + 1) * HEAD_DIM]

    def split_heads(r):
        for g in range(KV_HEADS):
            kh[g, r * tokens : (r + 1) * tokens, :] = kvbuf[r, :, g * HEAD_DIM : (g + 1) * HEAD_DIM]
            vh[g, r * tokens : (r + 1) * tokens, :] = kvbuf[r, :, kvd + g * HEAD_DIM : kvd + (g + 1) * HEAD_DIM]

    job_o.forward()
    job_u.begin()
    split_heads(0)
    for r in range(1, seq):
        kv_wait(r)
        if r < seq - 1:
            kv_send_on(r)
        if r == min(2, seq - 1):
            job_o.cross()
            job_g.forward()
            job_d.begin()
        split_heads(r)
    job_o.share()
    job_g.cross(True)

    row = lax.broadcasted_iota(jnp.int32, (tokens, tokens), 0)
    col = lax.broadcasted_iota(jnp.int32, (tokens, tokens), 1)
    lse_ref[...] = jnp.zeros_like(lse_ref)
    lane = lax.broadcasted_iota(jnp.int32, (tokens, 128), 1)

    half = HEADS // 2

    def attend_heads(start, stop):
        @pl.loop(start, stop)
        def _(h):
            g = h // GROUP
            q = qh[h]
            scores = []
            for r in range(seq):
                s = nt(q, kh[g, r * tokens : (r + 1) * tokens, :]) * SCALE
                scores.append(jnp.where(col <= row if r == 0 else place >= r, s, NEG))
            top = functools.reduce(jnp.maximum, [jnp.max(s, axis=1, keepdims=True) for s in scores])
            weights = [jnp.exp(s - top) for s in scores]
            total = sum(jnp.sum(w, axis=1, keepdims=True) for w in weights)
            inverse = 1.0 / total
            oh[h] = sum(
                nn((w * inverse).astype(BF), vh[g, r * tokens : (r + 1) * tokens, :])
                for r, w in enumerate(weights)
            ).astype(BF)
            lse_ref[...] += jnp.where(lane == h, top + jnp.log(total), 0.0)

    attend_heads(0, half)
    job_u.forward()
    job_g.share(True)
    attend_heads(half, HEADS)
    job_g.cross(False)
    job_u.cross(True)
    for i in range(3):
        keep(i).start()
    for h in range(HEADS):
        o_ref[:, h * HEAD_DIM : (h + 1) * HEAD_DIM] = oh[h]

    job_o.finish()
    load_o = pltpu.make_async_copy(w_out[3], wq, load_sem.at[0])
    load_o.start()
    put_left(2, n1_ref)
    put_left(1, o_ref)
    load_o.wait()

    @pl.loop(0, model // TILE)
    def _(t):
        at = pl.multiple_of(t * TILE, 128)
        x2_ref[:, pl.ds(at, TILE)] = x_ref[:, pl.ds(at, TILE)].astype(F32) + nn(o_ref[...], wq[:, pl.ds(at, TILE)])

    x2 = x2_ref[...]
    n2_ref[...] = (x2 * lax.rsqrt(jnp.mean(x2 * x2, axis=1, keepdims=True) + EPS) * gains_ref[1:2, :]).astype(BF)
    put_left(0, n2_ref)
    for i in (3, 4):
        keep(i).start()

    def project(weight, take, first=0, last=None):
        panels = weight.shape[1] // COLS if last is None else last

        def panel(t):
            at = pl.multiple_of(t * COLS, 128)
            return pltpu.make_async_copy(weight.at[:, pl.ds(at, COLS)], wt.at[t % 2], tile_sem.at[t % 2])

        panel(first).start()

        @pl.loop(first, panels)
        def _(t):
            panel(t).wait()

            @pl.when(t + 1 < panels)
            def _():
                panel(t + 1).start()

            take(pl.multiple_of(t * COLS, 128), nn(n2_ref[...], wt[t % 2]))

    def take_gate(at, gate):
        swish[:, pl.ds(at, COLS)] = gate

    def take_up(at, up):
        gate = swish[:, pl.ds(at, COLS)]
        sig = jax.nn.sigmoid(gate)
        act = gate * sig
        value = (act * up).astype(BF)
        hidden[:, pl.ds(at, COLS)] = value
        hidden_t[pl.ds(at, COLS), :] = value.T
        slope[:, pl.ds(at, COLS)] = up * sig * (1.0 + gate * (1.0 - sig))
        swish[:, pl.ds(at, COLS)] = act

    job_g.share(False)
    job_d.forward()
    job_g.finish()
    project(w_out[4], take_gate)
    job_u.cross(False)
    job_u.share(True)
    job_d.cross(True)
    job_u.share(False)
    job_u.finish()
    middle = w_out[5].shape[1] // COLS // 2
    project(w_out[5], take_up, 0, middle)
    job_d.cross(False)
    job_d.share(True)
    project(w_out[5], take_up, middle)
    for i in range(5, 9):
        keep(i).start()
    job_d.share(False)
    job_d.finish()
    for i in range(9):
        keep(i).wait()
    for r in range(seq - 1):

        @pl.when((place >= r) & (place < seq - 1))
        def _():
            kv_copy(r).wait_send()

    for g in gains:
        g.wait_send()
    for job in jobs:
        job.drain()


def forward_call(dp, seq, x, gains, tables, weights):
    tokens, model = x.shape
    chip_bits = dp.bit_length() - 2
    copies = gather_copies(chip_bits)
    anyspec = pl.BlockSpec(memory_space=pl.ANY)
    vmem = pl.BlockSpec(memory_space=pltpu.VMEM)
    out_shape = [jax.ShapeDtypeStruct((dp * w.shape[0], w.shape[1]), BF) for w in weights]
    heads = jax.ShapeDtypeStruct((HEADS, tokens, HEAD_DIM), BF)
    keys = jax.ShapeDtypeStruct((KV_HEADS, seq * tokens, HEAD_DIM), BF)
    kvd, ff = weights[1].shape[1], weights[4].shape[1]
    made = [
        heads,
        keys,
        keys,
        jax.ShapeDtypeStruct((3 * model, tokens), BF),
        jax.ShapeDtypeStruct((tokens, model), F32),
        jax.ShapeDtypeStruct((tokens, ff), BF),
        jax.ShapeDtypeStruct((ff, tokens), BF),
        jax.ShapeDtypeStruct((tokens, ff), F32),
        jax.ShapeDtypeStruct((tokens, ff), F32),
    ]
    out_shape += made + [jax.ShapeDtypeStruct((tokens, 128), F32), jax.ShapeDtypeStruct((8, model), F32)]
    line = pltpu.VMEM((tokens, model), BF)
    dma = pltpu.SemaphoreType.DMA
    return pl.pallas_call(
        functools.partial(forward_body, dp, seq),
        out_shape=out_shape,
        in_specs=[vmem] * 5 + [anyspec] * 7,
        out_specs=[anyspec] * 16 + [vmem] * 2,
        scratch_shapes=[pltpu.VMEM(a.shape, a.dtype) for a in made]
        + [pltpu.VMEM(w.shape, BF) for w in weights]
        + [
            pltpu.VMEM((model, model), BF),
            pltpu.VMEM((model, kvd), BF),
            pltpu.VMEM((model, kvd), BF),
            pltpu.VMEM((seq, tokens, model), BF),
            pltpu.VMEM((dp, 8, 256), F32),
            pltpu.VMEM((HEADS, tokens, HEAD_DIM), BF),
            line,
            line,
            line,
            pltpu.VMEM((2, model, COLS), BF),
            dma((7, copies)),
            dma((7, copies)),
            dma((seq,)),
            dma((seq,)),
            dma((dp,)),
            dma((dp,)),
            dma((7,)),
            dma((3,)),
            dma((2,)),
            dma((9,)),
        ],
        compiler_params=pltpu.CompilerParams(
            collective_id=0, has_side_effects=True, vmem_limit_bytes=60 * 1024 * 1024
        ),
        name="forward",
    )(x, gains, *tables, *weights)


def head_column(lse, h):
    lane = lax.broadcasted_iota(jnp.int32, lse.shape, 1)
    return jnp.sum(jnp.where(lane == h, lse, 0.0), axis=1, keepdims=True)


def back_group(place, chunks, g, slot, q_ref, do_ref, lse, k, v, dq_ref, dk_ref, dv_ref, acc_k, acc_v):
    tokens = q_ref.shape[1]
    row = lax.broadcasted_iota(jnp.int32, (tokens, tokens), 0)
    col = lax.broadcasted_iota(jnp.int32, (tokens, tokens), 1)
    for i in range(GROUP):
        h = GROUP * g + i
        q, do = q_ref[h], do_ref[h]
        total = head_column(lse, h)
        probs, dprobs = [], []
        for r in range(chunks):
            span = slice(r * tokens, (r + 1) * tokens)
            s = nt(q, k[span, :]) * SCALE
            s = jnp.where(col <= row if r == 0 else place >= r, s, NEG)
            probs.append(jnp.exp(s - total))
            dprobs.append(nt(do, v[span, :]))
        inner = sum(jnp.sum(p * d, axis=1, keepdims=True) for p, d in zip(probs, dprobs))
        dq = jnp.zeros((tokens, HEAD_DIM), F32)
        for r in range(chunks):
            span = slice(r * tokens, (r + 1) * tokens)
            ds = (probs[r] * (dprobs[r] - inner)).astype(BF)
            dq += nn(ds, k[span, :])
            dk = tn(ds, q)
            dv = tn(probs[r].astype(BF), do)
            if i == 0:
                acc_k[span, :] = dk
                acc_v[span, :] = dv
            else:
                dk_ref[slot, span, :] = ((acc_k[span, :] + dk) * SCALE).astype(BF)
                dv_ref[slot, span, :] = (acc_v[span, :] + dv).astype(BF)
        dq_ref[h] = (dq * SCALE).astype(BF)


LAG_B, LAG_C, LAG_D = 1, 4, 6
SLOTS_CORE, SLOTS, SLOTS_SUM, SLOTS_OUT = 2, 4, 11, 8


def backward_body(seq, x_ref, gains_ref, x2_ref, cos_ref, first_ref, second_ref, hidden_ref, eb_ref, lefts_ref,
                  qh, kh, vh, lse_ref, wq_in, wk_in, wv_in, wo_in, wg_in, wu_in, wd_in, hid_in, slope_in, swish_in, *refs):
    dx_ref, gain_out, out_ref, res = refs[:4]
    (rights, doh, dqh, dkh, dvh, acc_k, acc_v, dkv, dkv_in, dn1, wt, hid, slope, swish, term2,
     cs, cr, sums, r0, r1, zs, zr, zt, gsend, grecv, gsum, gzrecv,
     mid_sem, w_sem, core_s, core_r, s0_s, s0_r, s1_s, s1_r, z_s, z_r, a_s, a_r, t_sem, kv_s, kv_r,
     g_s, g_r, gz_s, gz_r, core_free, s0_free, s1_free, z_free) = refs[4:]
    me, place = lax.axis_index("dp"), lax.axis_index("seq")
    core, chip_x, chip_y = me % 2, (me // 2) % 2, me // 4
    tokens, model = x_ref.shape
    rows = model // 8
    sub = rows // seq
    kvd = wk_in.shape[1]
    d_rows = hidden_ref.shape[0] // 8
    d_chunks = d_rows * 3 // rows
    n_chunks = rights.shape[1] // COLS
    o_panels = model // COLS
    gu_panels = n_chunks - 3 * o_panels
    total_chunks = d_chunks + n_chunks

    def owner(x, y, c):
        return ((chip_y + y) % 2) * 4 + ((chip_x + x) % 2) * 2 + (core + c) % 2

    partner = owner(0, 0, 1)
    near = [[owner(1, 0, 0), owner(0, 1, 0)], [owner(0, 1, 0), owner(1, 0, 0)]]

    ff = wg_in.shape[1]
    part_d = COLS // 2

    def mid_loads(k):
        s = k % 2
        at = pl.multiple_of(k * COLS, 128)
        pairs = [
            (wd_in.at[pl.ds(at, part_d)], wt.at[s, pl.ds(0, part_d), pl.ds(0, model)]),
            (wd_in.at[pl.ds(at + part_d, part_d)], wt.at[s, pl.ds(0, part_d), pl.ds(model, model)]),
            (hid_in.at[:, pl.ds(at, COLS)], hid.at[s]),
            (slope_in.at[:, pl.ds(at, COLS)], slope.at[s]),
            (swish_in.at[:, pl.ds(at, COLS)], swish.at[s]),
        ]
        return [pltpu.make_async_copy(a, b, mid_sem.at[s, i]) for i, (a, b) in enumerate(pairs)]

    def ff_load(j, i):
        return pltpu.make_async_copy(
            (wg_in, wu_in)[i].at[pl.ds(pl.multiple_of(j * TILE, 16), TILE)], wt.at[i, :, pl.ds(0, ff)], w_sem.at[i, 0]
        )

    def o_load(t):
        return pltpu.make_async_copy(
            wo_in.at[pl.ds(t * TILE, TILE)], wt.at[t % 2, :, pl.ds(t // 2 * model, model)], w_sem.at[t % 2, t // 2]
        )

    for k in range(2):
        for made in mid_loads(k):
            made.start()
    out_ref[...] = x2_ref[...]

    barrier = pltpu.get_barrier_semaphore()
    for off in range(1, 8):
        pl.semaphore_signal(barrier, inc=1, device_id={"dp": me ^ off}, device_id_type=MESH)
    for far in range(1, seq):
        to = (place + far) % seq
        pl.semaphore_signal(barrier, inc=1, device_id={"seq": to}, device_id_type=MESH)
    pl.semaphore_wait(barrier, 7 + seq - 1)

    def remote(src, dst, send, recv, **target):
        return pltpu.make_async_remote_copy(
            src_ref=src, dst_ref=dst, send_sem=send, recv_sem=recv, device_id=target, device_id_type=MESH
        )

    def signal(sem, **target):
        pl.semaphore_signal(sem, inc=1, device_id=target, device_id_type=MESH)

    def core_copy(c):
        s = c % SLOTS_CORE
        return remote(cs.at[s], cr.at[s], core_s.at[s], core_r.at[s], dp=partner)

    def first_copy(c, parity):
        s = c % SLOTS
        return remote(sums.at[c % SLOTS_SUM, pl.ds(2 * rows, 2 * rows)], r0.at[s], s0_s.at[s], s0_r.at[s], dp=near[parity][0])

    def second_copy(c, parity):
        s = c % SLOTS
        return remote(sums.at[c % SLOTS_SUM, pl.ds(rows, rows)], r1.at[s], s1_s.at[s], s1_r.at[s], dp=near[parity][1])

    def offsets(index, parity):
        low, high = index % 2, index // 2
        return (high, low) if parity == 0 else (low, high)

    def stage_a(c, parity):
        s, t = c % SLOTS_CORE, c % SLOTS_SUM

        @pl.when(c >= SLOTS_CORE)
        def _():
            core_copy(c).wait_send()

        def put(away, term):
            @pl.loop(0, 4)
            def _(index):
                dx, dy = offsets(index, parity)
                at = pl.multiple_of(index * rows, 16)
                if away:
                    cs[s, pl.ds(at, rows), :] = term(owner(dx, dy, 1)).astype(BF)
                else:
                    sums[t, pl.ds(at, rows), :] = term(owner(dx, dy, 0)).astype(BF)

        def term_d(who):
            size = rows // 3
            at = pl.multiple_of(who * d_rows + c * size, 16)
            left = hidden_ref[pl.ds(at, size), :]
            return jnp.concatenate(
                [nn(left, eb_ref[:, i * COLS : (i + 1) * COLS]) for i in range(3)], axis=0
            )

        k = c - d_chunks
        which = (k >= gu_panels).astype(jnp.int32) + (k >= gu_panels + o_panels).astype(jnp.int32)

        def term_n(who):
            left = lefts_ref[pl.ds(pl.multiple_of(which * model + who * rows, 16), rows), :]
            return nn(left, rights[:, pl.ds(pl.multiple_of(k * COLS, 128), COLS)])

        def both(term):
            put(True, term)

            @pl.when(c >= SLOTS_CORE)
            def _():
                pl.semaphore_wait(core_free, 1)

            core_copy(c).start()
            put(False, term)

        @pl.when(c < d_chunks)
        def _():
            both(term_d)

        @pl.when(c >= d_chunks)
        def _():
            both(term_n)

    def add_rows(count, target, extra):
        @pl.loop(0, count // 64)
        def _(i):
            at = pl.multiple_of(i * 64, 16)
            target[pl.ds(at, 64), :] = (target[pl.ds(at, 64), :].astype(F32) + extra[pl.ds(at, 64), :].astype(F32)).astype(BF)

    def stage_b(c, parity):
        core_copy(c).wait_recv()
        add_rows(4 * rows, sums.at[c % SLOTS_SUM], cr.at[c % SLOTS_CORE])

        @pl.when(c < total_chunks - SLOTS_CORE)
        def _():
            signal(core_free, dp=partner)

        @pl.when(c >= SLOTS)
        def _():
            pl.semaphore_wait(s0_free.at[parity], 1)

        first_copy(c, parity).start()

    def stage_c(c, parity):
        first_copy(c, parity).wait_recv()
        add_rows(2 * rows, sums.at[c % SLOTS_SUM], r0.at[c % SLOTS])

        @pl.when(c < total_chunks - SLOTS)
        def _():
            signal(s0_free.at[parity], dp=near[parity][0])

        @pl.when(c >= SLOTS)
        def _():
            pl.semaphore_wait(s1_free.at[parity], 1)

        second_copy(c, parity).start()
        first_copy(c, parity).wait_send()

    def stage_d(c, parity):
        second_copy(c, parity).wait_recv()
        add_rows(rows, sums.at[c % SLOTS_SUM], r1.at[c % SLOTS])

        @pl.when(c < total_chunks - SLOTS)
        def _():
            signal(s1_free.at[parity], dp=near[parity][1])

        second_copy(c, parity).wait_send()

    def step_of(way):
        return 1 - 2 * way

    def inside(at):
        return (at >= 0) & (at < seq)

    def z_copy(c, way, hop):
        s = c % SLOTS
        slot = way * (seq - 1) + hop - 1
        return remote(zs.at[slot, s], zr.at[slot, s], z_s.at[slot, s], z_r.at[slot, s], seq=place + step_of(way))

    def z_sends(way, hop):
        return inside(place + step_of(way) * (seq - hop))

    def z_gets(way, hop):
        return inside(place - step_of(way)) & inside(place - step_of(way) + step_of(way) * (seq - hop))

    def part(c, index):
        index = jnp.minimum(jnp.maximum(index, 0), seq - 1)
        return sums[c % SLOTS_SUM, pl.ds(pl.multiple_of(index * sub, 16), sub), :].astype(F32)

    def z_take(c, way, hop):
        slot = way * (seq - 1) + hop - 1
        gets = z_gets(way, hop)

        @pl.when(gets)
        def _():
            z_copy(c, way, hop).wait_recv()

        return jnp.where(gets, zr[slot, c % SLOTS].astype(F32), 0.0)

    def z_release(c, way, hop):
        slot = way * (seq - 1) + hop - 1

        @pl.when(z_gets(way, hop) & (c < total_chunks - SLOTS))
        def _():
            signal(z_free.at[slot], seq=place - step_of(way))

    def stage_z(c, hop):
        for way in range(2):
            slot = way * (seq - 1) + hop - 1
            value = part(c, place + step_of(way) * (seq - hop))
            if hop > 1:
                value = value + z_take(c, way, hop - 1)
            sends = z_sends(way, hop)

            @pl.when(sends & (c >= SLOTS))
            def _():
                z_copy(c, way, hop).wait_send()

            zs[slot, c % SLOTS] = value.astype(BF)
            if hop > 1:
                z_release(c, way, hop - 1)

            @pl.when(sends & (c >= SLOTS))
            def _():
                pl.semaphore_wait(z_free.at[slot], 1)

            @pl.when(sends)
            def _():
                z_copy(c, way, hop).start()

    def res_at(c, source):
        index = jnp.minimum(jnp.maximum(source, 0), seq - 1)
        return res.at[pl.ds(pl.multiple_of(c * rows + index * sub, 16), sub)]

    def own_copy(c):
        s = c % SLOTS_OUT
        return pltpu.make_async_copy(zt.at[s], res_at(c, place), t_sem.at[s])

    def a_copy(c, way, hop):
        s = c % SLOTS_OUT
        slot = way * (seq - 1) + hop - 1
        source = place - step_of(way) * (hop - 1)
        src = zt.at[s] if hop == 1 else res_at(c, source)
        return remote(src, res_at(c, source), a_s.at[slot, s], a_r.at[slot, s], seq=place + step_of(way))

    def a_sends(way, hop):
        return inside(place + step_of(way)) & inside(place - step_of(way) * (hop - 1))

    def a_gets(way, hop):
        return inside(place - step_of(way) * hop)

    def stage_total(c):
        value = part(c, place)
        for way in range(2):
            value = value + z_take(c, way, seq - 1)

        @pl.when(c >= SLOTS_OUT)
        def _():
            own_copy(c).wait()

        for way in range(2):
            @pl.when((c >= SLOTS_OUT) & a_sends(way, 1))
            def _():
                a_copy(c, way, 1).wait_send()

        zt[c % SLOTS_OUT] = value.astype(BF)
        for way in range(2):
            z_release(c, way, seq - 1)
        own_copy(c).start()
        stage_out(c, 1)

    def stage_out(c, hop):
        for way in range(2):
            if hop > 1:
                @pl.when(a_gets(way, hop - 1))
                def _():
                    a_copy(c, way, hop - 1).wait_recv()

            if hop < seq:
                if hop > 1:
                    @pl.when((c >= SLOTS_OUT) & a_sends(way, hop))
                    def _():
                        a_copy(c, way, hop).wait_send()

                @pl.when(a_sends(way, hop))
                def _():
                    a_copy(c, way, hop).start()

    lag_total = LAG_D + seq - 1
    stages = [(LAG_B, stage_b), (LAG_C, stage_c), (LAG_D, stage_d), (LAG_D, lambda c, parity: stage_z(c, 1))]
    stages += [(LAG_D + hop - 1, lambda c, parity, hop=hop: stage_z(c, hop)) for hop in range(2, seq)]
    stages += [(lag_total, lambda c, parity: stage_total(c))]
    stages += [(lag_total + hop - 1, lambda c, parity, hop=hop: stage_out(c, hop)) for hop in range(2, seq + 1)]
    last_lag = lag_total + seq - 1

    def tick(c, parity):
        for lag, stage in sorted(stages, key=lambda pair: -pair[0]):
            then = c - lag

            @pl.when((then >= 0) & (then < total_chunks))
            def _():
                stage(then, (parity + lag) % 2)

        @pl.when(c < total_chunks)
        def _():
            stage_a(c, parity)

    pair_width = 2 * HEAD_DIM

    def kv_copy(r, i):
        return remote(dkv.at[r, i], dkv_in.at[r - 1, i], kv_s.at[r, i], kv_r.at[r, i], seq=place - 1)

    def kv_send(r, i):
        @pl.when(place >= r)
        def _():
            kv_copy(r, i).start()

    def kv_take(r, i):
        gets = (place + 1 >= r) & (place + 1 < seq)

        @pl.when(gets)
        def _():
            kv_copy(r, i).wait_recv()
            add_rows(tokens, dkv.at[r - 1, i], dkv_in.at[r - 1, i])

    def mid_down(k):
        s = k % 2
        at = pl.multiple_of(k * COLS, 128)
        for made in mid_loads(k):
            made.wait()
        for half in range(2):
            lo = half * part_d
            dh = nt(eb_ref[...], wt[s, :part_d, half * model : (half + 1) * model])
            rights[:, pl.ds(at + lo, part_d)] = (dh * slope[s, :, lo : lo + part_d]).astype(BF)
            rights[:, pl.ds(ff + at + lo, part_d)] = (dh * swish[s, :, lo : lo + part_d]).astype(BF)
        for j in range(model // COLS):
            span = slice(j * COLS, (j + 1) * COLS)
            out_ref[:, span] += sum(
                nn(
                    hid[s, :, half * part_d : (half + 1) * part_d],
                    wt[s, :part_d, half * model + j * COLS : half * model + (j + 1) * COLS],
                )
                for half in range(2)
            )

        @pl.when(k + 2 < ff // COLS)
        def _():
            for made in mid_loads(k + 2):
                made.start()

    def mid_ff(j):
        at = pl.multiple_of(j * TILE, 128)
        for i in range(2):
            ff_load(j, i).wait()
        dn1[:, pl.ds(at, TILE)] = nt(rights[:, :ff], wt[0, :, :ff]) + nt(rights[:, ff : 2 * ff], wt[1, :, :ff])

        @pl.when(j + 1 < model // TILE)
        def _():
            for i in range(2):
                ff_load(j + 1, i).start()

    def mid_out():
        x2 = x2_ref[...]
        scale = lax.rsqrt(jnp.mean(x2 * x2, axis=1, keepdims=True) + EPS)
        unit = x2 * scale
        grad = dn1[...]
        term2[0:1, :] = jnp.sum(grad * unit, axis=0, keepdims=True)
        scaled = grad * gains_ref[1:2, :]
        inner = jnp.mean(scaled * unit, axis=1, keepdims=True)
        e2 = eb_ref[...].astype(F32) + scale * (scaled - unit * inner)
        dx_ref[...] = e2
        rights[:, 2 * ff : 2 * ff + model] = e2.astype(BF)
        for t in range(model // TILE):
            o_load(t).wait()
            do = nt(rights[:, 2 * ff : 2 * ff + model], wt[t % 2, :, t // 2 * model : (t // 2 + 1) * model]).astype(BF)
            for i in range(TILE // HEAD_DIM):
                doh[t * (TILE // HEAD_DIM) + i] = do[:, i * HEAD_DIM : (i + 1) * HEAD_DIM]

    def turn_back(value):
        ahead = pltpu.roll(value, TILE - HEAD_DIM // 2, 1)
        behind = pltpu.roll(value, HEAD_DIM // 2, 1)
        return (value * cos_ref[...] - behind * second_ref[...] + ahead * first_ref[...]).astype(BF)

    q_at = (gu_panels + o_panels) * COLS

    def w_load(t, i):
        at = pl.multiple_of(t * TILE, 16)
        s = t % 2
        src, lo, width = ((wq_in, 0, model), (wk_in, model, kvd), (wv_in, model + kvd, kvd))[i]
        return pltpu.make_async_copy(src.at[pl.ds(at, TILE)], wt.at[s, :, pl.ds(lo, width)], w_sem.at[s, i])

    def last_norm():
        for h in range(HEADS):
            rights[:, q_at + h * HEAD_DIM : q_at + (h + 1) * HEAD_DIM] = dqh[h]
        for t in range(model // TILE):
            at = q_at + t * TILE
            rights[:, at : at + TILE] = turn_back(rights[:, at : at + TILE].astype(F32))
        for t in range(kvd // TILE):
            at = q_at + model + t * TILE
            pieces = [dkv[0, 2 * t + i, :, :pair_width] for i in range(2)]
            rights[:, at : at + TILE] = turn_back(jnp.concatenate(pieces, axis=1).astype(F32))
        for i in range(KV_HEADS // 2):
            at = q_at + model + kvd + i * pair_width
            rights[:, at : at + pair_width] = dkv[0, i, :, pair_width:]
        for i in range(3):
            w_load(0, i).start()

        @pl.loop(0, model // TILE)
        def _(t):
            for i in range(3):
                w_load(t, i).wait()

            @pl.when(t + 1 < model // TILE)
            def _():
                for i in range(3):
                    w_load(t + 1, i).start()

            dn1[:, pl.ds(pl.multiple_of(t * TILE, 128), TILE)] = nt(rights[:, q_at:], wt[t % 2, :, : model + 2 * kvd])

        x = x_ref[...].astype(F32)
        scale = lax.rsqrt(jnp.mean(x * x, axis=1, keepdims=True) + EPS)
        unit = x * scale
        grad = dn1[...]
        term = jnp.sum(grad * unit, axis=0, keepdims=True)
        scaled = grad * gains_ref[0:1, :]
        inner = jnp.mean(scaled * unit, axis=1, keepdims=True)
        dx_ref[...] += scale * (scaled - unit * inner)
        for k in range(8):
            gsend[k, 0:1, :rows] = term[:, k * rows : (k + 1) * rows]
            gsend[k, 1:2, :rows] = term2[0:1, k * rows : (k + 1) * rows]

    def gain_copies():
        return [
            remote(gsend.at[me ^ off], grecv.at[me], g_s.at[off], g_r.at[off], dp=me ^ off) for off in range(1, 8)
        ]

    def gain_line():
        return [
            remote(gsum, gzrecv.at[place], gz_s.at[far], gz_r.at[far], seq=(place + far) % seq) for far in range(1, seq)
        ]

    ticks = total_chunks + last_lag
    pairs = KV_HEADS // 2
    d_steps, f_steps = ff // COLS, model // TILE
    d_ticks = d_steps // 2
    out_at = (d_ticks + f_steps) // 2
    first_at = out_at + 1
    norm_at = first_at + pairs + seq - 1
    assert d_ticks <= d_chunks and 2 * norm_at + 1 < total_chunks - 2 * o_panels

    @pl.loop(0, -(-ticks // 2))
    def _(p):
        for parity in range(2):
            c = 2 * p + parity
            tick(c, parity)

            @pl.when(c < d_ticks)
            def _():
                @pl.loop(0, 2)
                def _(i):
                    mid_down(2 * c + i)

            @pl.when(c == d_ticks - 1)
            def _():
                for i in range(2):
                    ff_load(0, i).start()

            @pl.when((c >= d_ticks) & (c < d_ticks + f_steps))
            def _():
                mid_ff(c - d_ticks)

        @pl.when(p == out_at - 1)
        def _():
            for t in range(f_steps):
                o_load(t).start()

        @pl.when(p == out_at)
        def _():
            mid_out()

        for r in range(seq - 1, 0, -1):
            piece = p - first_at - (seq - r) - (r < seq - 1)

            @pl.when((piece >= 0) & (piece < pairs))
            def _():
                kv_take(r, piece)
                if r > 1:
                    kv_send(r - 1, piece)

        @pl.when((p >= first_at) & (p < first_at + pairs))
        def _():
            piece = p - first_at
            for i in range(2):
                g = 2 * piece + i
                back_group(place, seq, g, i, qh, doh, lse_ref[...], kh.at[g], vh.at[g], dqh, dkh, dvh, acc_k, acc_v)
            for r in range(seq):
                for i in range(2):
                    span = slice(r * tokens, (r + 1) * tokens)
                    dkv[r, piece, :, i * HEAD_DIM : (i + 1) * HEAD_DIM] = dkh[i, span, :]
                    lo = pair_width + i * HEAD_DIM
                    dkv[r, piece, :, lo : lo + HEAD_DIM] = dvh[i, span, :]
            kv_send(seq - 1, piece)

        @pl.when(p == norm_at)
        def _():
            last_norm()
            for made in gain_copies():
                made.start()
            grecv[me] = gsend[me]

        @pl.when(p == norm_at + 1)
        def _():
            for made in gain_copies():
                made.wait_recv()
            gsum[...] = sum(grecv[k] for k in range(1, 8)) + grecv[0]
            gzrecv[place] = gsum[...]
            for made in gain_line():
                made.start()

        @pl.when(p == norm_at + 2)
        def _():
            for made in gain_line():
                made.wait_recv()
            gain_out[...] = sum(gzrecv[k] for k in range(seq))

    for made in gain_copies() + gain_line():
        made.wait_send()
    for r in range(1, seq):
        @pl.when(place >= r)
        def _():
            for i in range(pairs):
                kv_copy(r, i).wait_send()
    for c in range(total_chunks - SLOTS_CORE, total_chunks):
        core_copy(c).wait_send()
    for way in range(2):
        for hop in range(1, seq):
            for c in range(total_chunks - SLOTS, total_chunks):
                @pl.when(z_sends(way, hop))
                def _():
                    z_copy(c, way, hop).wait_send()
            for c in range(total_chunks - SLOTS_OUT, total_chunks):
                @pl.when(a_sends(way, hop))
                def _():
                    a_copy(c, way, hop).wait_send()
    for c in range(total_chunks - SLOTS_OUT, total_chunks):
        own_copy(c).wait()


def backward_call(seq, x, gains, x2, tables, hidden_t, eb, lefts, qh, kh, vh, lse, weights, hidden, slope, swish):
    tokens, model = x.shape
    rows = model // 8
    sub = rows // seq
    kvd, ff = weights[1].shape[1], hidden.shape[1]
    wide = 2 * ff + 2 * model + 2 * kvd
    chunks = hidden_t.shape[0] // 8 * 3 // rows + wide // COLS
    anyspec = pl.BlockSpec(memory_space=pl.ANY)
    vmem = pl.BlockSpec(memory_space=pltpu.VMEM)
    dma, regular = pltpu.SemaphoreType.DMA, pltpu.SemaphoreType.REGULAR
    hops = 2 * (seq - 1)
    heads = pltpu.VMEM((HEADS, tokens, HEAD_DIM), BF)
    keys = pltpu.VMEM((2, seq * tokens, HEAD_DIM), BF)
    panel = pltpu.VMEM((2, tokens, COLS), F32)
    pieces = KV_HEADS // 2
    return pl.pallas_call(
        functools.partial(backward_body, seq),
        out_shape=[
            jax.ShapeDtypeStruct((tokens, model), F32),
            jax.ShapeDtypeStruct((8, 256), F32),
            jax.ShapeDtypeStruct((tokens, model), F32),
            jax.ShapeDtypeStruct((chunks * rows, COLS), BF),
        ],
        in_specs=[vmem] * 13 + [anyspec] * 10,
        out_specs=[vmem, vmem, vmem, anyspec],
        scratch_shapes=[
            pltpu.VMEM((tokens, wide), BF),
            heads, heads, keys, keys,
            pltpu.VMEM((seq * tokens, HEAD_DIM), F32),
            pltpu.VMEM((seq * tokens, HEAD_DIM), F32),
            pltpu.VMEM((seq, pieces, tokens, 4 * HEAD_DIM), BF),
            pltpu.VMEM((seq - 1, pieces, tokens, 4 * HEAD_DIM), BF),
            pltpu.VMEM((tokens, model), F32),
            pltpu.VMEM((2, TILE, max(ff, 2 * model)), BF),
            pltpu.VMEM((2, tokens, COLS), BF),
            panel, panel,
            pltpu.VMEM((8, model), F32),
            pltpu.VMEM((SLOTS_CORE, 4 * rows, COLS), BF),
            pltpu.VMEM((SLOTS_CORE, 4 * rows, COLS), BF),
            pltpu.VMEM((SLOTS_SUM, 4 * rows, COLS), BF),
            pltpu.VMEM((SLOTS, 2 * rows, COLS), BF),
            pltpu.VMEM((SLOTS, rows, COLS), BF),
            pltpu.VMEM((hops, SLOTS, sub, COLS), BF),
            pltpu.VMEM((hops, SLOTS, sub, COLS), BF),
            pltpu.VMEM((SLOTS_OUT, sub, COLS), BF),
            pltpu.VMEM((8, 8, 256), F32),
            pltpu.VMEM((8, 8, 256), F32),
            pltpu.VMEM((8, 256), F32),
            pltpu.VMEM((seq, 8, 256), F32),
            dma((2, 5)), dma((2, 3)),
            dma((SLOTS_CORE,)), dma((SLOTS_CORE,)),
            dma((SLOTS,)), dma((SLOTS,)),
            dma((SLOTS,)), dma((SLOTS,)),
            dma((hops, SLOTS)), dma((hops, SLOTS)),
            dma((hops, SLOTS_OUT)), dma((hops, SLOTS_OUT)),
            dma((SLOTS_OUT,)),
            dma((seq, pieces)), dma((seq, pieces)),
            dma((8,)), dma((8,)),
            dma((seq,)), dma((seq,)),
            regular, regular((2,)), regular((2,)), regular((hops,)),
        ],
        compiler_params=pltpu.CompilerParams(
            collective_id=1, has_side_effects=True, vmem_limit_bytes=62 * 1024 * 1024
        ),
        name="backward",
    )(x, gains, x2, *tables, hidden_t, eb, lefts, qh, kh, vh, lse, *weights, hidden, slope, swish)


def finish_call(res, dx, result, d_rows, ff, kvd):
    tokens, model = dx.shape
    block = res.shape[1]
    steps = 4
    per_d, per_f, per_m = d_rows * 3 // block // steps, ff // COLS // steps, model // COLS
    at_f = per_d * steps // per_f
    at_m = per_d * steps + 2 * per_f * steps
    panel = block // 3
    assert per_d and per_f and per_d * steps % per_f == 0 and per_m < steps

    def body(d_in, g_in, u_in, o_in, q_in, kv_in, dx_in, y_in, down, gate, up, out, query, key, value, dx_out, y_out):
        s = pl.program_id(0)
        dx_out[...] = dx_in[...]
        y_out[...] = y_in[...]
        for i in range(per_d):
            for j in range(3):
                down[i * panel : (i + 1) * panel, j * COLS : (j + 1) * COLS] = d_in[i, j * panel : (j + 1) * panel, :].astype(F32)
        for i in range(per_f):
            gate[:, i * COLS : (i + 1) * COLS] = g_in[i].astype(F32)
            up[:, i * COLS : (i + 1) * COLS] = u_in[i].astype(F32)
        for i in range(per_m):

            @pl.when(s == i)
            def _():
                out[:, i * COLS : (i + 1) * COLS] = o_in[0].astype(F32)
                query[:, i * COLS : (i + 1) * COLS] = q_in[0].astype(F32)
                mid = min(max(kvd - i * COLS, 0), COLS)
                if mid:
                    key[:, i * COLS : i * COLS + mid] = kv_in[0, :, :mid].astype(F32)
                if mid < COLS:
                    lo = i * COLS + mid - kvd
                    value[:, lo : lo + COLS - mid] = kv_in[0, :, mid:].astype(F32)

    def chunk(count, at):
        return pl.BlockSpec((count, block, COLS), at)

    wide = lambda base: chunk(per_f, lambda s: (base + s, 0, 0))
    thin = lambda base: chunk(1, lambda s: (base + jnp.minimum(s, per_m - 1), 0, 0))
    line = pl.BlockSpec((tokens // steps, model), lambda s: (s, 0))
    whole = lambda width: pl.BlockSpec((block, width), lambda s: (0, 0))
    return pl.pallas_call(
        body,
        grid=(steps,),
        in_specs=[
            chunk(per_d, lambda s: (s, 0, 0)),
            wide(at_f),
            wide(at_f + steps),
            thin(at_m),
            thin(at_m + per_m),
            thin(at_m + 2 * per_m),
            line,
            line,
        ],
        out_specs=[
            pl.BlockSpec((d_rows // steps, model), lambda s: (s, 0)),
            pl.BlockSpec((block, ff // steps), lambda s: (0, s)),
            pl.BlockSpec((block, ff // steps), lambda s: (0, s)),
            whole(model),
            whole(model),
            whole(kvd),
            whole(kvd),
            line,
            line,
        ],
        out_shape=[
            jax.ShapeDtypeStruct((d_rows, model), F32),
            jax.ShapeDtypeStruct((block, ff), F32),
            jax.ShapeDtypeStruct((block, ff), F32),
            jax.ShapeDtypeStruct((block, model), F32),
            jax.ShapeDtypeStruct((block, model), F32),
            jax.ShapeDtypeStruct((block, kvd), F32),
            jax.ShapeDtypeStruct((block, kvd), F32),
            jax.ShapeDtypeStruct((tokens, model), F32),
            jax.ShapeDtypeStruct((tokens, model), F32),
        ],
        compiler_params=pltpu.CompilerParams(vmem_limit_bytes=60 * 1024 * 1024),
        name="finish",
    )(*[res] * 6, dx, result)


def attend_back(place, qh, kh, vh, doh, lse):
    chunks = kh.shape[1] // qh.shape[1]

    def body(place_ref, q_ref, k_ref, v_ref, do_ref, lse_ref, dq_ref, dk_ref, dv_ref, acc_k, acc_v):
        @pl.loop(0, KV_HEADS)
        def _(g):
            back_group(place_ref[0], chunks, g, g, q_ref, do_ref, lse_ref[...], k_ref.at[g], v_ref.at[g], dq_ref, dk_ref, dv_ref, acc_k, acc_v)

    vmem = pl.BlockSpec(memory_space=pltpu.VMEM)
    acc = pltpu.VMEM(kh.shape[1:], F32)
    return pl.pallas_call(
        body,
        in_specs=[pl.BlockSpec(memory_space=pltpu.SMEM)] + [vmem] * 5,
        out_specs=[vmem] * 3,
        out_shape=[jax.ShapeDtypeStruct(a.shape, BF) for a in (qh, kh, vh)],
        scratch_shapes=[acc, acc],
        name="attend_back",
    )(place, qh, kh, vh, doh, lse)


def flip(value, axis, bit):
    size = lax.axis_size(axis)
    return lax.ppermute(value, axis, [(i, i ^ bit) for i in range(size)])


def xor_order(bits):
    order = [0]
    for bit in list(reversed(bits)) + [1]:
        order = order + [off ^ bit for off in order]
    return order


def scatter_term(left, right, bits):
    half = left.shape[1] // 2
    away = tn(left[:, half:], right).astype(BF)
    came = flip(away, "dp", 1)
    quarter = half // 2
    away = (tn(left[:, quarter:half], right) + came[quarter:]).astype(BF)
    kept = (tn(left[:, :quarter], right) + came[:quarter]).astype(BF)
    came = flip(away, "dp", bits[0])
    for bit in bits[1:]:
        size = kept.shape[0] // 2
        away = (kept[size:].astype(F32) + came[size:]).astype(BF)
        kept = (kept[:size].astype(F32) + came[:size]).astype(BF)
        came = flip(away, "dp", bit)
    return (kept.astype(F32) + came).astype(BF)


def line_sum(value, place):
    size = lax.axis_size("seq")
    rows = value.shape[0] // size

    def chunk(index):
        index = jnp.clip(index, 0, size - 1)
        return lax.dynamic_slice_in_dim(value, index * rows, rows, 0)

    total = chunk(place).astype(F32)
    for way in (1, -1):
        held = None
        for far in range(size - 1, 0, -1):
            mine = chunk(place + way * far)
            if held is not None:
                mine = (mine.astype(F32) + held).astype(BF)
            pairs = [(i, i + way) for i in range(size) if 0 <= i + way * far < size]
            held = lax.ppermute(mine, "seq", pairs)
        total = total + held
    total = total.astype(BF)
    out = jnp.zeros(value.shape, F32)
    out = lax.dynamic_update_slice(out, total.astype(F32), (place * rows, 0))
    for way in (1, -1):
        held = total
        for far in range(1, size):
            pairs = [
                (i, i + way) for i in range(size) if 0 <= i + way < size and 0 <= i - way * (far - 1) < size
            ]
            held = lax.ppermute(held, "seq", pairs)
            source = place - way * far
            index = jnp.clip(source, 0, size - 1) * rows
            old = lax.dynamic_slice(out, (index, 0), held.shape)
            good = (source >= 0) & (source < size)
            out = lax.dynamic_update_slice(
                out, jnp.where(good, held.astype(F32), old), (index, 0)
            )
    return out


def rope_tables(place, tokens, width):
    half = HEAD_DIM // 2
    lane = lax.broadcasted_iota(jnp.int32, (tokens, width), 1)
    positions = (place * tokens + lax.broadcasted_iota(jnp.int32, (tokens, width), 0)).astype(F32)
    frequency = ROPE_BASE ** (-jnp.arange(half).astype(F32) / half)
    angles = positions * jnp.tile(frequency, width // half)[None, :]
    cos, sin = jnp.cos(angles), jnp.sin(angles)
    low = lane % HEAD_DIM < half
    return cos, jnp.where(low, sin, 0.0), jnp.where(low, 0.0, sin)


def rotate(field, tables, sign):
    cos, first, second = tables
    half = HEAD_DIM // 2
    width = field.shape[1]
    cos, first, second = cos[:, :width], first[:, :width], second[:, :width]
    ahead = jnp.concatenate([field[:, half:], field[:, :half]], axis=1)
    behind = jnp.concatenate([field[:, -half:], field[:, :-half]], axis=1)
    return field * cos + sign * (behind * second - ahead * first)


def norm_scale(values):
    return lax.rsqrt(jnp.mean(values * values, axis=-1, keepdims=True) + EPS)


def norm_back(values, scale, gain, grad):
    unit = values * scale
    grad_gain = jnp.sum(grad * unit, axis=0)
    scaled = grad * gain
    inner = jnp.mean(scaled * unit, axis=-1, keepdims=True)
    return scale * (scaled - unit * inner), grad_gain


def local(tokens, cotangent, w_query, w_key, w_value, w_out, w_gate, w_up, w_down, gain_attn, gain_mlp):
    dp, seq = lax.axis_size("dp"), lax.axis_size("seq")
    me, place = lax.axis_index("dp"), lax.axis_index("seq")
    bits = [1 << i for i in range(1, dp.bit_length() - 1)]
    turned = bits[1:] + bits[:1]
    model = tokens.shape[-1]
    rows = tokens.shape[1]
    kvd = w_key.shape[-1]
    place_arr = place.reshape(1).astype(jnp.int32)

    half_model = model // 2

    def xor_columns(value, way):
        width = value.shape[1] // dp
        cut = lambda off: lax.dynamic_slice_in_dim(value, (me ^ off) * width, width, 1)
        return jnp.concatenate([cut(off) for off in xor_order(way)], axis=1)

    tables = rope_tables(place, rows, TILE)
    x = tokens[0].astype(F32)
    packed = jnp.zeros((8, 256), F32)
    packed = packed.at[0, : gain_attn.shape[1]].set(gain_attn[0].astype(F32))
    packed = packed.at[1, : gain_mlp.shape[1]].set(gain_mlp[0].astype(F32))
    shards = [w[0] for w in (w_query, w_key, w_value, w_out, w_gate, w_up, w_down)]
    outs = forward_call(dp, seq, tokens[0], packed, tables, shards)
    w_q, w_k, w_v, w_o, w_g, w_u, w_d = outs[:7]
    qh, kh, vh, lefts, x2, hidden, hidden_t, slope, swish, lse, gains = outs[7:]
    gain_one, gain_two = gains[0:1], gains[1:2]
    eb = cotangent[0]
    if len(bits) == 2 and (model // dp) % (16 * seq) == 0:
        dx, grads, result, res = backward_call(
            seq, tokens[0], gains, x2, tables, hidden_t, eb, lefts,
            qh, kh, vh, lse, outs[:7], hidden, slope, swish,
        )
        block = model // dp
        g_down, g_gate, g_up, g_out, g_query, g_key, g_value, dx, result = finish_call(
            res.reshape(-1, block, COLS), dx, result, w_down.shape[1], w_gate.shape[2], kvd
        )
        return (
            result[None],
            dx[None],
            g_query[None],
            g_key[None],
            g_value[None],
            g_out[None],
            g_gate[None],
            g_up[None],
            g_down[None],
            grads[0:1, :block],
            grads[1:2, :block],
        )

    tables = [jnp.tile(t, (1, model // TILE)) for t in tables]
    scale_one = norm_scale(x)
    scale_two = norm_scale(x2)
    result = x2 + nn(hidden, w_d)
    e = eb.astype(F32)
    dh = nt(eb, w_d)
    dgate = (dh * slope).astype(BF)
    dup = (dh * swish).astype(BF)
    dn2 = nt(dgate, w_g) + nt(dup, w_u)
    dx2, term_gain_two = norm_back(x2, scale_two, gain_two, dn2)
    e2 = e + dx2
    e2b = e2.astype(BF)
    do = nt(e2b, w_o).astype(BF)
    n2, mixed, n1 = (lefts[i * model : (i + 1) * model].T for i in range(3))
    hidden_a = xor_columns(hidden, bits)
    hidden_b = xor_columns(hidden, turned)
    sum_down = jnp.concatenate(
        [
            scatter_term(hidden_a, eb[:, :half_model], bits),
            scatter_term(hidden_b, eb[:, half_model:], turned),
        ],
        axis=1,
    )
    n2_a, n2_b = xor_columns(n2, bits), xor_columns(n2, turned)
    sum_gate = scatter_term(n2_a, dgate, bits)
    sum_up = scatter_term(n2_b, dup, turned)
    mixed_a, mixed_b = xor_columns(mixed, bits), xor_columns(mixed, turned)
    sum_out = jnp.concatenate(
        [
            scatter_term(mixed_a, e2b[:, :half_model], bits),
            scatter_term(mixed_b, e2b[:, half_model:], turned),
        ],
        axis=1,
    )
    doh = do.reshape(rows, HEADS, HEAD_DIM).transpose(1, 0, 2)
    dqh, dkh, dvh = attend_back(place_arr, qh, kh, vh, doh, lse)
    dq = dqh.transpose(1, 0, 2).reshape(rows, model)
    dks, dvs = (a.reshape(KV_HEADS, seq, rows, HEAD_DIM).transpose(1, 2, 0, 3).reshape(seq, rows, kvd) for a in (dkh, dvh))
    held = None
    for far in range(seq - 1, -1, -1):
        mine = jnp.concatenate([dks[far], dvs[far]], axis=1)
        if held is not None:
            mine = (mine.astype(F32) + held).astype(BF)
        if far:
            held = lax.ppermute(mine, "seq", [(i, i - 1) for i in range(far, seq)])
    dk, dv = mine[:, :kvd], mine[:, kvd:]
    dqp = rotate(dq.astype(F32), tables, -1.0).astype(BF)
    dkp = rotate(dk.astype(F32), tables, -1.0).astype(BF)
    n1_a, n1_b = xor_columns(n1, bits), xor_columns(n1, turned)
    sum_query = scatter_term(n1_a, dqp, bits)
    sum_kv = scatter_term(n1_b, jnp.concatenate([dkp, dv], axis=1), turned)
    dn1 = nt(dqp, w_q) + nt(dkp, w_k) + nt(dv, w_v)
    dx1, term_gain_one = norm_back(x, scale_one, gain_one, dn1)
    input_grad = e2 + dx1

    both = jnp.stack([term_gain_one, term_gain_two])
    for bit in [1] + bits:
        both = both + flip(both, "dp", bit)
    for bit in [1 << i for i in range(seq.bit_length() - 1)]:
        both = both + flip(both, "seq", bit)
    width = model // dp
    both = lax.dynamic_slice_in_dim(both, me * width, width, 1)

    g_down = line_sum(sum_down, place)
    g_gate = line_sum(sum_gate, place)
    g_up = line_sum(sum_up, place)
    g_out = line_sum(sum_out, place)
    g_query = line_sum(sum_query, place)
    g_kv = line_sum(sum_kv, place)
    return (
        result[None],
        input_grad[None],
        g_query[None],
        g_kv[None, :, :kvd],
        g_kv[None, :, kvd:],
        g_out[None],
        g_gate[None],
        g_up[None],
        g_down[None],
        both[0:1],
        both[1:2],
    )


def solution(mesh):
    by_token = P("dp", "seq", None)
    by_row = P(None, "dp", None)
    by_gain = P(None, "dp")
    in_specs = (by_token,) * 2 + (by_row,) * 7 + (by_gain,) * 2
    return jax.shard_map(local, mesh=mesh, in_specs=in_specs, out_specs=in_specs, check_vma=False)
```
